32 devices in a mesh: seq: 8 (over z, x), rep: 4 (over y, core).
Axes of the slice: x: 2, y: 2, z: 4, core: 2. Of those that a mesh axis runs over, the one named last changes fastest.
Arguments:
- tokens: bfloat16 [4, 1024, 960], P('rep', 'seq'), may hold values from -6 to 6
- depths: int32 [4, 1024], P('rep', 'seq'), may hold values from 1 to 3
- seq_spans: int32 [4, 3], P('rep'), may hold values from 1 to 4, 8 in all within a row
- cotangent: bfloat16 [4, 1024, 960], P('rep', 'seq'), may hold values from -6 to 6
- w_query: float32 [921600], P(('seq', 'rep')), may hold values from -0.1875 to 0.1875
- key_weight: float32 [307200], P(('seq', 'rep')), may hold values from -0.1875 to 0.1875
- value_weight: float32 [307200], P(('seq', 'rep')), may hold values from -0.1875 to 0.1875
- w_out: float32 [921600], P(('seq', 'rep')), may hold values from -0.75 to 0.75
- w_gate: float32 [2457600], P(('seq', 'rep')), may hold values from -0.1875 to 0.1875
- w_up: float32 [2457600], P(('seq', 'rep')), may hold values from -0.1875 to 0.1875
- w_down: float32 [2457600], P(('seq', 'rep')), may hold values from -0.125 to 0.125
- attn_gain: float32 [960], replicated, may hold values from 0.1 to 1.9
- ffn_gain: float32 [960], replicated, may hold values from 0.1 to 1.9
- router: float32 [3, 960], replicated, may hold values from -0.1875 to 0.1875
Outputs:
- output: bfloat16 [4, 1024, 960], P('rep', 'seq')
- input_grad: float32 [4, 1024, 960], P('rep', 'seq')
- grad_query: float32 [921600], P(('seq', 'rep'))
- grad_key: float32 [307200], P(('seq', 'rep'))
- grad_value: float32 [307200], P(('seq', 'rep'))
- grad_out: float32 [921600], P(('seq', 'rep'))
- grad_gate: float32 [2457600], P(('seq', 'rep'))
- grad_up: float32 [2457600], P(('seq', 'rep'))
- grad_down: float32 [2457600], P(('seq', 'rep'))
- grad_attn_gain: float32 [960], replicated
- grad_ffn_gain: float32 [960], replicated
- grad_router: float32 [3, 960], replicated
The draws below stay inside these ranges and needn't reach their ends.
Inputs may be any that keep to these rules, and one draw needn't show every extreme that they name: `seq_spans`: each row gives the span counts of the 3 sequences of a group; they add up to 8, and some sequence has exactly 4 spans.
All inputs are finite; a program needn't handle non-finite values.
Results may differ from the reference program's by a relative error of at most 0.025.
Values may be sent and summed in bfloat16 or wider, within the bound.
A program may use at most 448 MiB of HBM per device.

```python
import math
import jax
import jax.numpy as jnp
import numpy as np
from jax import lax

MODEL_WIDTH = 960
QUERY_HEADS = 15
KEY_VALUE_HEADS = 5
HEAD_SIZE = 64
FEEDFORWARD_UNITS = 2560
SPAN_TOKENS = 128
RECUR = 3
MOSTC = 4
GROUPS = 4
STREAM = 1024
NSEQS = 3
N_SEQ = 8


def plant(drawn, own_key, least, high):
    longest = drawn.shape.index(max(drawn.shape))
    spots = []
    for shift in (0, 1):
        where = [jax.random.randint(jax.random.fold_in(own_key, axis), (), 0, length) for axis, length in enumerate(drawn.shape)]
        where[longest] = (where[longest] + shift) % drawn.shape[longest]
        spots.append(tuple(where))
    return drawn.at[spots[0]].set(least).at[spots[1]].set(high)


def levels(own_key, extent, split, least, high):
    def one(axis_at, blocks):
        heights = jax.random.uniform(jax.random.fold_in(jax.random.fold_in(own_key, 6), axis_at), (blocks,), jnp.float32, least / len(split), high / len(split))
        return jnp.repeat(jnp.exp(heights), extent[axis_at] // blocks).reshape((-1,) + (1,) * (len(extent) - axis_at - 1))

    loudness = one(*split[0])
    for cut in split[1:]:
        loudness = loudness * one(*cut)
    return loudness


def split_up(number_of, total, limit, skew):
    loads = [(1 << 20) // math.isqrt(rank ** skew) + 1 for rank in range(2, number_of + 1)]
    spare, holding = total - limit - (number_of - 1), [1] * (number_of - 1)
    while spare > 0:
        movable = [i for i in range(number_of - 1) if holding[i] < limit]
        whole, left = sum([loads[i] for i in movable]), spare
        for i in movable:
            extra = min(limit - holding[i], max(1, left * loads[i] // whole), spare)
            holding[i] = holding[i] + extra
            spare = spare - extra
    return np.array([limit] + holding)


def ragged_sizes(key, number_of, total, most, lean):
    if number_of == 2:
        one = jax.random.randint(key, (), max(1, total - most), min(most, total - 1) + 1)
        return jnp.stack([one, total - one])
    sizes = jnp.asarray(split_up(number_of, total, most, lean), jnp.int32)
    twos = (number_of - 1) // 2
    source_of, receiver = sizes[1:1 + 2 * twos:2], sizes[2:2 + 2 * twos:2]
    slack = jnp.minimum(source_of - 1, most - receiver)
    passed = jax.random.randint(jax.random.fold_in(key, 1), (twos,), 0, 1 << 20) % (slack + 1)
    sizes = sizes.at[1:1 + 2 * twos:2].set(source_of - passed).at[2:2 + 2 * twos:2].set(receiver + passed)
    return sizes[jax.random.permutation(jax.random.fold_in(key, 2), number_of)]


def centred(key, extent, spread, most, shards=(), kind=jnp.bfloat16):
    loudness = levels(key, extent, shards, -0.22, 0.18) if shards else 1.0
    values = jax.random.normal(key, extent, jnp.float32) * spread * loudness
    return jnp.minimum(jnp.maximum(values, -most), most).astype(kind)


def setup_inputs(seed: int = 0) -> dict:
    arg_keys = jax.random.split(jax.random.key(seed), 15)
    return {
        "tokens": centred(arg_keys[0], (GROUPS, STREAM, MODEL_WIDTH), 1.0, 6.0, ((0, 4), (1, 8))),
        "depths": plant(jax.random.randint(arg_keys[1], (GROUPS, STREAM), 1, RECUR + 1), jax.random.fold_in(arg_keys[1], 1), 1, RECUR).astype(jnp.int32),
        "seq_spans": jax.vmap(lambda own: ragged_sizes(own, NSEQS, N_SEQ, MOSTC, 0))(jax.random.split(arg_keys[2], GROUPS)).reshape((GROUPS, NSEQS)).astype(jnp.int32),
        "cotangent": centred(arg_keys[3], (GROUPS, STREAM, MODEL_WIDTH), 1.0, 6.0, ((0, 4), (1, 8))),
        "w_query": centred(arg_keys[4], (MODEL_WIDTH * QUERY_HEADS * HEAD_SIZE,), MODEL_WIDTH ** -0.5, 0.1875, ((0, 32),), jnp.float32),
        "key_weight": centred(arg_keys[5], (MODEL_WIDTH * KEY_VALUE_HEADS * HEAD_SIZE,), MODEL_WIDTH ** -0.5, 0.1875, ((0, 32),), jnp.float32),
        "value_weight": centred(arg_keys[6], (MODEL_WIDTH * KEY_VALUE_HEADS * HEAD_SIZE,), MODEL_WIDTH ** -0.5, 0.1875, ((0, 32),), jnp.float32),
        "w_out": centred(arg_keys[7], (QUERY_HEADS * HEAD_SIZE * MODEL_WIDTH,), (QUERY_HEADS * HEAD_SIZE // 16) ** -0.5, 0.75, ((0, 32),), jnp.float32),
        "w_gate": centred(arg_keys[8], (MODEL_WIDTH * FEEDFORWARD_UNITS,), MODEL_WIDTH ** -0.5, 0.1875, ((0, 32),), jnp.float32),
        "w_up": centred(arg_keys[9], (MODEL_WIDTH * FEEDFORWARD_UNITS,), MODEL_WIDTH ** -0.5, 0.1875, ((0, 32),), jnp.float32),
        "w_down": centred(arg_keys[10], (FEEDFORWARD_UNITS * MODEL_WIDTH,), FEEDFORWARD_UNITS ** -0.5, 0.125, ((0, 32),), jnp.float32),
        "attn_gain": jnp.clip(1.0 + 0.18 * jax.random.normal(arg_keys[11], (MODEL_WIDTH,), jnp.float32), 0.1, 1.9),
        "ffn_gain": jnp.clip(1.0 + 0.18 * jax.random.normal(arg_keys[12], (MODEL_WIDTH,), jnp.float32), 0.1, 1.9),
        "router": centred(arg_keys[13], (RECUR, MODEL_WIDTH), MODEL_WIDTH ** -0.5, 0.1875, (), jnp.float32),
    }


@jax.custom_vjp
def lower_bound(v):
    return lax.optimization_barrier(v.astype(jnp.bfloat16)).astype(jnp.float32)

@jax.custom_vjp
def lower_bound_backward(v):
    return v

def low_keep(v):
    return (lower_bound(v), None)

def low_pass(kept, grad):
    return (grad,)

def back_keep(v):
    return (v, None)

def back_low(kept, grad):
    return (lower_bound(grad),)
lower_bound.defvjp(low_keep, low_pass)
lower_bound_backward.defvjp(back_keep, back_low)
highest = lax.Precision.HIGHEST
epsilon = 1e-06
masked_score = -1e+30

def matrix_product(left, right):
    return jnp.dot(left, right, precision=highest)

def rms_norm(vectors, gain):
    inv_rms = lax.rsqrt(lax.optimization_barrier(jnp.mean(vectors * vectors, axis=-1, keepdims=True)) + epsilon)
    return vectors * inv_rms * gain

def angle_tables(positions, width):
    half_width = width // 2
    frequency = 10000.0 ** (-jnp.arange(half_width, dtype=jnp.float32) / half_width)
    angle_grid = positions[:, None] * frequency[None, :]
    return (jnp.cos(angle_grid)[:, None, :], jnp.sin(angle_grid)[:, None, :])

def apply_rotation(vectors, cosine_table, sine_table):
    half_width = vectors.shape[-1] // 2
    front_half = vectors[..., :half_width]
    back_half = vectors[..., half_width:]
    return jnp.concatenate([front_half * cosine_table - back_half * sine_table, back_half * cosine_table + front_half * sine_table], axis=-1)

def span_table(lengths, span_count):
    seq_ends = jnp.cumsum(lengths).astype(jnp.int32)
    span_ids = jnp.arange(span_count, dtype=jnp.int32)
    owners = lax.optimization_barrier(jnp.sum((seq_ends[None, :] <= span_ids[:, None]).astype(jnp.int32), axis=1)).astype(jnp.int32)
    seq_starts = (seq_ends - lengths).astype(jnp.int32)
    numbers = jnp.arange(lengths.shape[0], dtype=jnp.int32)
    first_span = lax.optimization_barrier(jnp.sum(jnp.where(numbers[None, :] == owners[:, None], seq_starts[None, :], 0), axis=1)).astype(jnp.int32)
    return (span_ids - first_span).astype(jnp.int32)

def apply_attention(query_rows, every_key, every_value, current_active, index_of_span):
    query_groupings = QUERY_HEADS // KEY_VALUE_HEADS
    window = MOSTC * SPAN_TOKENS
    padding_rows = (MOSTC - 1) * SPAN_TOKENS
    padded_keys = jnp.concatenate([jnp.zeros((padding_rows, KEY_VALUE_HEADS, HEAD_SIZE), jnp.float32), every_key], axis=0)
    padded_values = jnp.concatenate([jnp.zeros((padding_rows, KEY_VALUE_HEADS, HEAD_SIZE), jnp.float32), every_value], axis=0)
    active_pad = jnp.concatenate([jnp.zeros((padding_rows,), jnp.float32), current_active], axis=0)
    query_block_list = query_rows.reshape(N_SEQ, SPAN_TOKENS, KEY_VALUE_HEADS, query_groupings, HEAD_SIZE)
    row_ids = jnp.arange(SPAN_TOKENS, dtype=jnp.int32)
    col_ids = jnp.arange(window, dtype=jnp.int32)
    offsets = MOSTC - 1 - col_ids // SPAN_TOKENS
    local_col = col_ids - padding_rows
    causal = jnp.where(offsets[None, :] == 0, local_col[None, :] <= row_ids[:, None], True)
    diagonal = (offsets[None, :] == 0) & (local_col[None, :] == row_ids[:, None])

    def one_block(element):
        block_query, span_number, block_index = element
        start_row = (span_number * SPAN_TOKENS).astype(jnp.int32)
        block_keys = lax.dynamic_slice_in_dim(padded_keys, start_row, window, 0)
        block_values = lax.dynamic_slice_in_dim(padded_values, start_row, window, 0)
        key_active = lax.dynamic_slice_in_dim(active_pad, start_row, window, 0)
        allowed = (block_index >= offsets)[None, :] & causal & ((key_active > 0)[None, :] | diagonal)
        scores = jnp.einsum('qgjd,kgd->gjqk', block_query, block_keys, precision=highest) * 0.125
        scores = lower_bound_backward(scores)
        scores = jnp.where(allowed[None, None], scores, masked_score)
        row_max = lax.optimization_barrier(jnp.max(scores, axis=-1, keepdims=True))
        expon = jnp.exp(scores - row_max)
        probability = lower_bound(expon / lax.optimization_barrier(jnp.sum(expon, axis=-1, keepdims=True)))
        result = jnp.einsum('gjqk,kgd->qgjd', probability, block_values, precision=highest)
        return result.reshape(SPAN_TOKENS, QUERY_HEADS * HEAD_SIZE)
    span_numbers = jnp.arange(N_SEQ, dtype=jnp.int32)
    results = lax.map(jax.checkpoint(one_block), (query_block_list, span_numbers, index_of_span))
    return results.reshape(N_SEQ * SPAN_TOKENS, QUERY_HEADS * HEAD_SIZE)

def forward(inputs, w_query, key_weight, value_weight, w_out, w_gate, w_up, w_down, attn_gain, ffn_gain, router, active_all, index_of_span):
    count_of_rows = inputs.shape[0]
    query_groupings = QUERY_HEADS // KEY_VALUE_HEADS
    positions = (index_of_span[:, None] * SPAN_TOKENS + jnp.arange(SPAN_TOKENS, dtype=jnp.int32)[None, :]).reshape(-1).astype(jnp.float32)
    cosine_table, sine_table = angle_tables(positions, HEAD_SIZE)
    query_mat = lower_bound(w_query)
    key_projection_matrix = lower_bound(key_weight)
    value_projection_matrix = lower_bound(value_weight)
    out_mat = lower_bound(w_out)
    gate_mat = lower_bound(w_gate)
    up_mat = lower_bound(w_up)
    down_mat = lower_bound(w_down)
    hidden_state = inputs
    for recursion in range(RECUR):
        current_active = active_all[recursion]
        normalized_input = lower_bound(rms_norm(hidden_state, attn_gain))
        query_rows = lower_bound(apply_rotation(lower_bound_backward(matrix_product(normalized_input, query_mat)).reshape(count_of_rows, QUERY_HEADS, HEAD_SIZE), cosine_table, sine_table))
        rotated_key_rows = lower_bound(apply_rotation(lower_bound_backward(matrix_product(normalized_input, key_projection_matrix)).reshape(count_of_rows, KEY_VALUE_HEADS, HEAD_SIZE), cosine_table, sine_table))
        value_rows = lower_bound(lower_bound_backward(matrix_product(normalized_input, value_projection_matrix))).reshape(count_of_rows, KEY_VALUE_HEADS, HEAD_SIZE)
        attention_output = apply_attention(query_rows.reshape(count_of_rows, KEY_VALUE_HEADS, query_groupings, HEAD_SIZE), rotated_key_rows, value_rows, current_active, index_of_span)
        attention_output = lower_bound(lower_bound_backward(attention_output))
        branch = lower_bound_backward(matrix_product(attention_output, out_mat))
        middle = hidden_state + branch
        second = lower_bound(rms_norm(middle, ffn_gain))
        gate_value = lower_bound_backward(matrix_product(second, gate_mat))
        up_value = lower_bound_backward(matrix_product(second, up_mat))
        hidden = lower_bound(jax.nn.silu(gate_value) * up_value)
        ffn_out = lower_bound_backward(matrix_product(hidden, down_mat))
        weight_gate = jax.nn.sigmoid(matrix_product(hidden_state, router[recursion]))
        hidden_state = hidden_state + (current_active * weight_gate)[:, None] * (branch + ffn_out)
    return hidden_state

def reference(tokens, depths, seq_spans, cotangent, w_query, key_weight, value_weight, w_out, w_gate, w_up, w_down, attn_gain, ffn_gain, router):
    target_tokens = ((MODEL_WIDTH, QUERY_HEADS * HEAD_SIZE), (MODEL_WIDTH, KEY_VALUE_HEADS * HEAD_SIZE), (MODEL_WIDTH, KEY_VALUE_HEADS * HEAD_SIZE), (QUERY_HEADS * HEAD_SIZE, MODEL_WIDTH), (MODEL_WIDTH, FEEDFORWARD_UNITS), (MODEL_WIDTH, FEEDFORWARD_UNITS), (FEEDFORWARD_UNITS, MODEL_WIDTH))
    flats = (w_query, key_weight, value_weight, w_out, w_gate, w_up, w_down)
    matrices = tuple((flat_one.reshape(target) for flat_one, target in zip(flats, target_tokens)))
    parameters = matrices + (attn_gain, ffn_gain, router)
    step_ids = jnp.arange(RECUR, dtype=jnp.int32)

    def one_group(totals, element):
        group_tokens, group_depths, group_lengths, group_cot = element
        index_of_span = span_table(group_lengths, N_SEQ)
        active_all = (group_depths[None, :] > step_ids[:, None]).astype(jnp.float32)

        def run_block(inputs, *attention_weights):
            return forward(inputs, *attention_weights, active_all, index_of_span)
        result, pullback = jax.vjp(run_block, group_tokens.astype(jnp.float32), *parameters)
        gradients = pullback(group_cot.astype(jnp.float32))
        totals = tuple((total_old + new_grad for total_old, new_grad in zip(totals, gradients[1:])))
        return (totals, (result.astype(jnp.bfloat16), gradients[0]))
    initial = tuple((jnp.zeros_like(param_one) for param_one in parameters))
    totals, (outputs, input_grads) = lax.scan(one_group, initial, (tokens, depths, seq_spans, cotangent))
    return (outputs, input_grads, totals[0].reshape(-1), totals[1].reshape(-1), totals[2].reshape(-1), totals[3].reshape(-1), totals[4].reshape(-1), totals[5].reshape(-1), totals[6].reshape(-1), totals[7], totals[8], totals[9])
```

```python
import jax
import jax.numpy as jnp
from jax import lax
from jax.experimental import pallas as pl
from jax.experimental.pallas import tpu as pltpu
from jax.sharding import PartitionSpec as P

MODEL_WIDTH = 960
QUERY_HEADS = 15
KEY_VALUE_HEADS = 5
HEAD_SIZE = 64
FEEDFORWARD_UNITS = 2560
LOGC = 5
RECUR = 3
OWN_ROWS = 30
PADDED_ROWS = 32
PADDED_WIDTH = 1024


highest = lax.Precision.HIGHEST
epsilon = 1e-06
masked_score = -1e30


def passed_along(value, axis, steps):
    count = lax.axis_size(axis)
    initial, last = (max(0, -steps), min(count, count - steps))
    return lax.ppermute(value, axis, [(source, source + steps) for source in range(initial, last)])


def for_sending(x):

    def short(part):
        return part.astype(jnp.bfloat16) if part.dtype == jnp.float32 else part

    return jax.tree.map(short, x)


def unscaled_product(left, right):
    return jnp.dot(left, right, preferred_element_type=jnp.float32)


def left_product(left, right):
    return lax.dot_general(
        left, right, (((0,), (0,)), ((), ())), preferred_element_type=jnp.float32
    )


def right_product(left, right):
    return lax.dot_general(
        left, right, (((1,), (1,)), ((), ())), preferred_element_type=jnp.float32
    )


def rms_parts(vectors, gain):
    inv_rms = lax.rsqrt(jnp.mean(vectors * vectors, axis=-1, keepdims=True) + epsilon)
    normal_part = vectors * inv_rms
    return (normal_part * gain, normal_part, inv_rms)


def rms_backward(upstream, normal_part, inv_rms, gain):
    gain_grad = jnp.sum(upstream * normal_part, axis=0)
    scaled = upstream * gain
    inner = jnp.mean(scaled * normal_part, axis=-1, keepdims=True)
    return (inv_rms * (scaled - normal_part * inner), gain_grad)


def angle_tables(positions, width):
    half_width = width // 2
    frequency = 10000.0 ** (-jnp.arange(half_width, dtype=jnp.float32) / half_width)
    angle_grid = positions[:, None] * frequency[None, :]
    return (jnp.cos(angle_grid)[:, None, :], jnp.sin(angle_grid)[:, None, :])


def apply_rotation(vectors, cosine_table, sine_table):
    half_width = vectors.shape[-1] // 2
    front_half = vectors[..., :half_width]
    back_half = vectors[..., half_width:]
    return jnp.concatenate(
        [
            front_half * cosine_table - back_half * sine_table,
            back_half * cosine_table + front_half * sine_table,
        ],
        axis=-1,
    )


def masked_scores(query_b, keys_win, allowed):
    scores = (
        jnp.einsum("qgjd,kgd->gjqk", query_b, keys_win, preferred_element_type=jnp.float32) * 0.125
    )
    return jnp.where(allowed[None, None], scores, masked_score)


def per_device(
    tokens,
    depths,
    seq_spans,
    cotangent,
    w_query,
    key_weight,
    value_weight,
    w_out,
    w_gate,
    w_up,
    w_down,
    attn_gain,
    ffn_gain,
    router,
):
    narrow_float_type = jnp.bfloat16
    wide_float_type = jnp.float32
    count_of_rows = tokens.shape[1]
    query_groupings = QUERY_HEADS // KEY_VALUE_HEADS
    chain = lax.axis_size("seq")
    most_spans = min(2**LOGC, chain // 2)
    depth_levels = (most_spans - 1).bit_length()
    extra_rows = ((1 << depth_levels) - most_spans) * count_of_rows
    window = most_spans * count_of_rows
    target_tokens = (
        (MODEL_WIDTH, QUERY_HEADS * HEAD_SIZE),
        (MODEL_WIDTH, KEY_VALUE_HEADS * HEAD_SIZE),
        (MODEL_WIDTH, KEY_VALUE_HEADS * HEAD_SIZE),
        (QUERY_HEADS * HEAD_SIZE, MODEL_WIDTH),
        (MODEL_WIDTH, FEEDFORWARD_UNITS),
        (MODEL_WIDTH, FEEDFORWARD_UNITS),
        (FEEDFORWARD_UNITS, MODEL_WIDTH),
    )
    fetched = (
        lax.all_gather(w_query.astype(narrow_float_type), ("seq", "rep"), axis=0, tiled=True),
        lax.all_gather(key_weight.astype(narrow_float_type), ("seq", "rep"), axis=0, tiled=True),
        lax.all_gather(value_weight.astype(narrow_float_type), ("seq", "rep"), axis=0, tiled=True),
        lax.all_gather(w_out.astype(narrow_float_type), ("seq", "rep"), axis=0, tiled=True),
        lax.all_gather(w_gate.astype(narrow_float_type), ("seq", "rep"), axis=0, tiled=True),
        lax.all_gather(w_up.astype(narrow_float_type), ("seq", "rep"), axis=0, tiled=True),
        lax.all_gather(w_down.astype(narrow_float_type), ("seq", "rep"), axis=0, tiled=True),
    )
    attention_weights = tuple(
        (gathered.reshape(target) for gathered, target in zip(fetched, target_tokens))
    )
    place = lax.axis_index("seq")
    lengths = seq_spans[0]
    seq_ends = jnp.cumsum(lengths)
    span_ids = jnp.arange(chain, dtype=jnp.int32)
    owners = jnp.sum((seq_ends[None, :] <= span_ids[:, None]).astype(jnp.int32), axis=1)
    seq_starts = seq_ends - lengths
    numbers = jnp.arange(lengths.shape[0], dtype=jnp.int32)
    first_span = jnp.sum(
        jnp.where(numbers[None, :] == owners[:, None], seq_starts[None, :], 0), axis=1
    )
    index_of_span = jnp.sum(jnp.where(span_ids == place, span_ids - first_span, 0))
    positions = (index_of_span * count_of_rows + jnp.arange(count_of_rows, dtype=jnp.int32)).astype(
        wide_float_type
    )
    cosine_table, sine_table = angle_tables(positions, HEAD_SIZE)
    row_ids = jnp.arange(count_of_rows, dtype=jnp.int32)
    col_ids = jnp.arange(window, dtype=jnp.int32)
    offsets = most_spans - 1 - col_ids // count_of_rows
    local_col = col_ids - (most_spans - 1) * count_of_rows
    causal = jnp.where(offsets[None, :] == 0, local_col[None, :] <= row_ids[:, None], True)
    diagonal = (offsets[None, :] == 0) & (local_col[None, :] == row_ids[:, None])
    span_ok = (index_of_span >= offsets)[None, :]
    active_all = (depths[0][None, :] > jnp.arange(RECUR, dtype=jnp.int32)[:, None]).astype(
        wide_float_type
    )
    hidden_state = tokens[0].astype(wide_float_type)
    saved = []
    for recursion in range(RECUR):
        current_active = active_all[recursion]
        normalized_input, normal_a, inv_a = rms_parts(hidden_state, attn_gain)
        normalized_input_copy = normalized_input.astype(narrow_float_type)
        raw_query = unscaled_product(normalized_input_copy, attention_weights[0]).reshape(
            count_of_rows, QUERY_HEADS, HEAD_SIZE
        )
        query_b = (
            apply_rotation(raw_query, cosine_table, sine_table)
            .astype(narrow_float_type)
            .reshape(count_of_rows, KEY_VALUE_HEADS, query_groupings, HEAD_SIZE)
        )
        unrotated_key = unscaled_product(normalized_input_copy, attention_weights[1]).reshape(
            count_of_rows, KEY_VALUE_HEADS, HEAD_SIZE
        )
        key_b = apply_rotation(unrotated_key, cosine_table, sine_table).astype(narrow_float_type)
        value_copy = (
            unscaled_product(normalized_input_copy, attention_weights[2])
            .astype(narrow_float_type)
            .reshape(count_of_rows, KEY_VALUE_HEADS, HEAD_SIZE)
        )
        active_b = current_active.astype(narrow_float_type)
        keys_win = key_b
        values_win = value_copy
        active_win = active_b
        for level in range(depth_levels):
            far_key, far_value, far_active = passed_along(
                (keys_win, values_win, active_win), "seq", 1 << level
            )
            keys_win = jnp.concatenate([far_key, keys_win], axis=0)
            values_win = jnp.concatenate([far_value, values_win], axis=0)
            active_win = jnp.concatenate([far_active, active_win], axis=0)
        allowed = span_ok & causal & ((active_win > 0)[None, :] | diagonal)
        scores = masked_scores(query_b, keys_win, allowed)
        row_max = jnp.max(scores, axis=-1, keepdims=True)
        expon = jnp.exp(scores - row_max)
        row_total = jnp.sum(expon, axis=-1, keepdims=True)
        probs_b = (expon / row_total).astype(narrow_float_type)
        log_total = row_max + jnp.log(row_total)
        attended_b = (
            jnp.einsum(
                "gjqk,kgd->qgjd", probs_b, values_win, preferred_element_type=wide_float_type
            )
            .astype(narrow_float_type)
            .reshape(count_of_rows, QUERY_HEADS * HEAD_SIZE)
        )
        branch = unscaled_product(attended_b, attention_weights[3])
        middle = hidden_state + branch
        second, normal_z, inv_z = rms_parts(middle, ffn_gain)
        second_b = second.astype(narrow_float_type)
        gate_value = unscaled_product(second_b, attention_weights[4])
        up_value = unscaled_product(second_b, attention_weights[5])
        hidden_b = (jax.nn.silu(gate_value) * up_value).astype(narrow_float_type)
        ffn_out = unscaled_product(hidden_b, attention_weights[6])
        weight_gate = jax.nn.sigmoid(jnp.dot(hidden_state, router[recursion], precision=highest))
        saved.append(
            (
                hidden_state,
                normalized_input_copy,
                normal_a,
                inv_a,
                query_b,
                keys_win,
                values_win,
                allowed,
                log_total,
                attended_b,
                branch,
                normal_z,
                inv_z,
                second_b,
                gate_value,
                up_value,
                hidden_b,
                ffn_out,
                weight_gate,
                current_active,
            )
        )
        hidden_state = hidden_state + (current_active * weight_gate)[:, None] * (branch + ffn_out)
    output = hidden_state.astype(narrow_float_type)
    refetched = (
        lax.all_gather(w_query.astype(narrow_float_type), ("seq", "rep"), axis=0, tiled=True),
        lax.all_gather(key_weight.astype(narrow_float_type), ("seq", "rep"), axis=0, tiled=True),
        lax.all_gather(value_weight.astype(narrow_float_type), ("seq", "rep"), axis=0, tiled=True),
        lax.all_gather(w_out.astype(narrow_float_type), ("seq", "rep"), axis=0, tiled=True),
        lax.all_gather(w_gate.astype(narrow_float_type), ("seq", "rep"), axis=0, tiled=True),
        lax.all_gather(w_up.astype(narrow_float_type), ("seq", "rep"), axis=0, tiled=True),
        lax.all_gather(w_down.astype(narrow_float_type), ("seq", "rep"), axis=0, tiled=True),
    )
    back_weights = tuple(
        (gathered.reshape(target) for gathered, target in zip(refetched, target_tokens))
    )
    master_shapes = (w_query, key_weight, value_weight, w_out, w_gate, w_up, w_down)
    shares = tuple((jnp.zeros_like(master) for master in master_shapes))
    gain_a_total = jnp.zeros((MODEL_WIDTH,), wide_float_type)
    gain_f_total = jnp.zeros((MODEL_WIDTH,), wide_float_type)
    router_rows = [None] * RECUR
    grad_state = cotangent[0].astype(wide_float_type)
    for recursion in reversed(range(RECUR)):
        (
            state_in,
            normalized_input_copy,
            normal_a,
            inv_a,
            query_b,
            keys_win,
            values_win,
            allowed,
            log_total,
            attended_b,
            branch,
            normal_z,
            inv_z,
            second_b,
            gate_value,
            up_value,
            hidden_b,
            ffn_out,
            weight_gate,
            current_active,
        ) = saved[recursion]
        mixing = current_active * weight_gate
        grad_delta = mixing[:, None] * grad_state
        grad_mix = jnp.sum(grad_state * (branch + ffn_out), axis=-1)
        grad_logit = current_active * grad_mix * weight_gate * (1.0 - weight_gate)
        router_rows[recursion] = jnp.dot(grad_logit, state_in, precision=highest)
        grad_next = grad_state + grad_logit[:, None] * router[recursion][None, :]
        ffn_grad_b = grad_delta.astype(narrow_float_type)
        grad_hidden = right_product(ffn_grad_b, back_weights[6])
        d_down = left_product(hidden_b, ffn_grad_b)
        sigmoid_gate = jax.nn.sigmoid(gate_value)
        grad_gate_b = (
            grad_hidden * up_value * sigmoid_gate * (1.0 + gate_value * (1.0 - sigmoid_gate))
        ).astype(narrow_float_type)
        grad_up_b = (grad_hidden * gate_value * sigmoid_gate).astype(narrow_float_type)
        grad_second = right_product(grad_gate_b, back_weights[4]) + right_product(
            grad_up_b, back_weights[5]
        )
        d_gate = left_product(second_b, grad_gate_b)
        d_up = left_product(second_b, grad_up_b)
        grad_middle, gain_f_part = rms_backward(grad_second, normal_z, inv_z, ffn_gain)
        gain_f_total = gain_f_total + gain_f_part
        grad_branch_b = (grad_delta + grad_middle).astype(narrow_float_type)
        grad_attended_b = (
            right_product(grad_branch_b, back_weights[3])
            .astype(narrow_float_type)
            .reshape(count_of_rows, KEY_VALUE_HEADS, query_groupings, HEAD_SIZE)
        )
        d_out = left_product(attended_b, grad_branch_b)
        grad_next = grad_next + grad_middle
        scores = masked_scores(query_b, keys_win, allowed)
        probs = jnp.exp(scores - log_total)
        probs_b = probs.astype(narrow_float_type)
        grad_probs = jnp.einsum(
            "qgjd,kgd->gjqk", grad_attended_b, values_win, preferred_element_type=wide_float_type
        )
        row_dot = jnp.sum(probs * grad_probs, axis=-1, keepdims=True)
        grad_scores_b = (probs * (grad_probs - row_dot)).astype(narrow_float_type)
        grad_queries = (
            jnp.einsum(
                "gjqk,kgd->qgjd", grad_scores_b, keys_win, preferred_element_type=wide_float_type
            )
            * 0.125
        )
        grad_keys = (
            jnp.einsum(
                "gjqk,qgjd->kgd", grad_scores_b, query_b, preferred_element_type=wide_float_type
            )
            * 0.125
        )
        grad_values = jnp.einsum(
            "gjqk,qgjd->kgd", probs_b, grad_attended_b, preferred_element_type=wide_float_type
        )
        extra_zero_rows = jnp.zeros((extra_rows, KEY_VALUE_HEADS, HEAD_SIZE), wide_float_type)
        local_span_keys = jnp.concatenate([extra_zero_rows, grad_keys], axis=0)
        local_span_values = jnp.concatenate([extra_zero_rows, grad_values], axis=0)
        for level in reversed(range(depth_levels)):
            older_rows = (1 << level) * count_of_rows
            back_keys, back_values = passed_along(
                (
                    for_sending(local_span_keys[:older_rows]),
                    for_sending(local_span_values[:older_rows]),
                ),
                "seq",
                -(1 << level),
            )
            local_span_keys = local_span_keys[older_rows:] + back_keys
            local_span_values = local_span_values[older_rows:] + back_values
        grad_query_b = (
            apply_rotation(
                grad_queries.reshape(count_of_rows, QUERY_HEADS, HEAD_SIZE),
                cosine_table,
                -sine_table,
            )
            .astype(narrow_float_type)
            .reshape(count_of_rows, QUERY_HEADS * HEAD_SIZE)
        )
        grad_key_b = (
            apply_rotation(local_span_keys, cosine_table, -sine_table)
            .astype(narrow_float_type)
            .reshape(count_of_rows, KEY_VALUE_HEADS * HEAD_SIZE)
        )
        value_gradient_copy = local_span_values.astype(narrow_float_type).reshape(
            count_of_rows, KEY_VALUE_HEADS * HEAD_SIZE
        )
        grad_normed = (
            right_product(grad_query_b, back_weights[0])
            + right_product(grad_key_b, back_weights[1])
            + right_product(value_gradient_copy, back_weights[2])
        )
        d_query = left_product(normalized_input_copy, grad_query_b)
        d_key = left_product(normalized_input_copy, grad_key_b)
        d_value = left_product(normalized_input_copy, value_gradient_copy)
        grad_input, gain_a_part = rms_backward(grad_normed, normal_a, inv_a, attn_gain)
        gain_a_total = gain_a_total + gain_a_part
        grad_state = grad_next + grad_input
        local_grads = (
            d_query.reshape(-1),
            d_key.reshape(-1),
            d_value.reshape(-1),
            d_out.reshape(-1),
            d_gate.reshape(-1),
            d_up.reshape(-1),
            d_down.reshape(-1),
        )
        summed = (
            lax.psum_scatter(local_grads[0], ("seq", "rep"), scatter_dimension=0, tiled=True),
            lax.psum_scatter(local_grads[1], ("seq", "rep"), scatter_dimension=0, tiled=True),
            lax.psum_scatter(local_grads[2], ("seq", "rep"), scatter_dimension=0, tiled=True),
            lax.psum_scatter(local_grads[3], ("seq", "rep"), scatter_dimension=0, tiled=True),
            lax.psum_scatter(local_grads[4], ("seq", "rep"), scatter_dimension=0, tiled=True),
            lax.psum_scatter(local_grads[5], ("seq", "rep"), scatter_dimension=0, tiled=True),
            lax.psum_scatter(local_grads[6], ("seq", "rep"), scatter_dimension=0, tiled=True),
        )
        shares = tuple((old_share + new_share for old_share, new_share in zip(shares, summed)))
    router_grad = jnp.stack(router_rows, axis=0)
    gain_a_sum, gain_f_sum, router_sum = lax.psum(
        (gain_a_total, gain_f_total, router_grad), ("seq", "rep")
    )
    return (
        output[None],
        grad_state[None],
        shares[0],
        shares[1],
        shares[2],
        shares[3],
        shares[4],
        shares[5],
        shares[6],
        gain_a_sum,
        gain_f_sum,
        router_sum,
    )


MESH = pl.DeviceIdType.MESH
N_Z = 4
BLOCKS = ((32, 2688), (32, 2560), (32, 2560), (80, 1024))
GATHER_ORDERS = ("uzw", "zuw", "uzw", "zuw")
REDUCE_ORDERS = ("zuw", "uzw", "zuw", "uzw")


def place():
    seq = lax.axis_index("seq")
    rep = lax.axis_index("rep")
    z, x, y, core = seq // 2, seq % 2, rep // 2, rep % 2
    return z, x + core * (y - x), y + core * (x - y), core


def device_of(z, u, w, core):
    x, y = u + core * (w - u), w + core * (u - w)
    return (z * 2 + x, y * 2 + core)


def block_of(z, u, w, core):
    seq, rep = device_of(z, u, w, core)
    return seq * 4 + rep


def remote(src, dst, send_sem, recv_sem, device):
    return pltpu.make_async_remote_copy(
        src_ref=src,
        dst_ref=dst,
        send_sem=send_sem,
        recv_sem=recv_sem,
        device_id=device,
        device_id_type=MESH,
    )


def gather_events():
    events = [("own", group) for group in range(4)]
    for step in range(6):
        for group in range(4):
            if GATHER_ORDERS[group] == "zuw":
                if 1 <= step <= 3:
                    events.append(("z", group, step, 0))
                if 1 <= step <= 4:
                    events.append(("u", group, step - 1))
                    events.append(("w", group, step - 1, 0))
                if 2 <= step <= 5:
                    events.append(("w", group, step - 2, 1))
            else:
                if step == 1:
                    events.append(("first", group))
                if 1 <= step <= 3:
                    events.append(("z", group, step, 0))
                if 2 <= step <= 4:
                    events.append(("z", group, step - 1, 1))
                if 1 <= step <= 4:
                    events.append(("w", group, step - 1, 0))
                if 2 <= step <= 5:
                    events.append(("w", group, step - 2, 1))
    return events


def gather_kernel(*refs):
    own, full = refs[:4], refs[4:8]
    recv_sem, z_sem, u_sem, w_sem, core_sem, local_sem = refs[8:]
    z, u, w, core = place()
    me = block_of(z, u, w, core)
    above, below = device_of(z + 1, u, w, core), device_of(z - 1, u, w, core)
    across_u, across_w = device_of(z, 1 - u, w, core), device_of(z, u, 1 - w, core)
    sibling = device_of(z, w, u, 1 - core)

    barrier = pltpu.get_barrier_semaphore()
    for device in (across_u, across_w, sibling):
        pl.semaphore_signal(barrier, inc=1, device_id=device, device_id_type=MESH)

    @pl.when(z < N_Z - 1)
    def _():
        pl.semaphore_signal(barrier, inc=1, device_id=above, device_id_type=MESH)

    @pl.when(z > 0)
    def _():
        pl.semaphore_signal(barrier, inc=1, device_id=below, device_id_type=MESH)

    pl.semaphore_wait(barrier, 4 + (z + 1) // 2 - z // 3 * 2)

    def rows(group, block):
        count = BLOCKS[group][0]
        return full[group].at[pl.ds(pl.multiple_of(block * count, 16), count)]

    def copy(group, block, src, send_sem, device):
        return remote(src, rows(group, block), send_sem, recv_sem.at[group, block], device)

    def send(group, block, src, ways, slot=0):
        if "z" in ways:

            @pl.when(z < N_Z - 1)
            def _():
                copy(group, block, src, z_sem.at[group, 0, slot], above).start()

            @pl.when(z > 0)
            def _():
                copy(group, block, src, z_sem.at[group, 1, slot], below).start()

        if "+" in ways:

            @pl.when(z < N_Z - 1)
            def _():
                copy(group, block, src, z_sem.at[group, 0, slot], above).start()

        if "-" in ways:

            @pl.when(z > 0)
            def _():
                copy(group, block, src, z_sem.at[group, 1, slot], below).start()

        if "u" in ways:
            copy(group, block, src, u_sem.at[group], across_u).start()
        if "w" in ways:
            copy(group, block, src, w_sem.at[group], across_w).start()
        if "c" in ways:
            copy(group, block, src, core_sem.at[group], sibling).start()

    def passed_on(group, block, ways, slot=0):
        copy(group, block, rows(group, block), core_sem.at[group], sibling).wait_recv()
        send(group, block, rows(group, block), ways, slot)

    def at_distance(step, action):
        if step == 0:
            action(z, "")
            return

        @pl.when(z - step >= 0)
        def _():
            action(z - step, "+")

        @pl.when(z + step < N_Z)
        def _():
            action(z + step, "-")

    def own_event(group):
        send(group, me, own[group], "zuwc")
        pltpu.make_async_copy(own[group], rows(group, me), local_sem.at[group]).start()

    def first_event(group):
        passed_on(group, block_of(z, 1 - u, w, core), "zwc", 1)

    def z_event(group, step, other):
        z_first = GATHER_ORDERS[group] == "zuw"
        column = 1 - u if other else u
        slot = step if z_first else 2 * step + other
        at_distance(
            step,
            lambda far, way: passed_on(
                group,
                block_of(far, column, w, core),
                way + ("uwc" if z_first else "wc"),
                slot,
            ),
        )

    def u_event(group, step):
        at_distance(
            step, lambda far, way: passed_on(group, block_of(far, 1 - u, w, core), "wc")
        )

    def w_event(group, step, other):
        column = 1 - u if other else u
        at_distance(
            step, lambda far, way: passed_on(group, block_of(far, column, 1 - w, core), "c")
        )

    actions = {"own": own_event, "first": first_event, "z": z_event, "u": u_event, "w": w_event}
    for event in gather_events():
        actions[event[0]](*event[1:])

    for group in range(4):
        z_first = GATHER_ORDERS[group] == "zuw"
        count = BLOCKS[group][0]
        pltpu.make_async_copy(own[group], rows(group, me), local_sem.at[group]).wait()

        @pl.loop(0, 16)
        def _(i):
            block = i * 2 + (1 - core)
            copy(group, block, rows(group, block), core_sem.at[group], sibling).wait_recv()

        for sem, sends in ((u_sem, 4 if z_first else 1), (w_sem, 8), (core_sem, 16)):
            part = full[group].at[pl.ds(0, sends * count)]
            remote(part, part, sem.at[group], recv_sem.at[group, 0], sibling).wait_send()
        for step in range(N_Z):
            for other in (0,) if z_first else (0, 1):
                slot = step if z_first else 2 * step + other

                @pl.when((z - step >= 0) & (z < N_Z - 1))
                def _():
                    copy(group, me, own[group], z_sem.at[group, 0, slot], above).wait_send()

                @pl.when((z + step < N_Z) & (z > 0))
                def _():
                    copy(group, me, own[group], z_sem.at[group, 1, slot], below).wait_send()


def gather_weights(packed):
    sems = pltpu.SemaphoreType.DMA
    return pl.pallas_call(
        gather_kernel,
        out_shape=[
            jax.ShapeDtypeStruct((32 * rows, columns), jnp.bfloat16) for rows, columns in BLOCKS
        ],
        in_specs=[pl.BlockSpec(memory_space=pl.ANY)] * 4,
        out_specs=[pl.BlockSpec(memory_space=pl.ANY)] * 4,
        scratch_shapes=[
            sems((4, 32)),
            sems((4, 2, 8)),
            sems((4,)),
            sems((4,)),
            sems((4,)),
            sems((4,)),
        ],
        compiler_params=pltpu.CompilerParams(
            collective_id=1, has_side_effects=True, vmem_limit_bytes=16 * 2**20
        ),
        name="gather_weights",
    )(*packed)


def reduce_events():
    events = [("small", -1)]

    def entry(group):
        return [("core", group, plane) for plane in range(4)] + [
            ("w", group, step) for step in (3, 2, 1, 0)
        ]

    def middle(group):
        kind = "u" if REDUCE_ORDERS[group] == "zuw" else "z_early"
        return [(kind, group, step) for step in (3, 2, 1, 0)]

    def last(group):
        if REDUCE_ORDERS[group] == "zuw":
            return [("z_late", group, step) for step in (3, 2, 1, 0)]
        return [("u_late", group)]

    for stage in (
        entry(0),
        entry(1),
        [("small", 0)],
        middle(0),
        entry(2),
        [("small", 1)],
        middle(1),
        last(0),
        [("small", 2)],
        entry(3),
        middle(2),
        [("small", 3)],
        last(1),
        middle(3),
        [("small", 4)],
        last(2),
        last(3),
    ):
        events += stage
    return events


def reduce_kernel(*refs):
    partial, small_in, final, small_out = refs[:4], refs[4], refs[5:9], refs[9]
    part, from_core, from_w, from_u, from_z = (refs[10 + 4 * i : 14 + 4 * i] for i in range(5))
    small_held, small_got = refs[30:32]
    (
        local_sem,
        core_send,
        core_recv,
        w_send,
        w_recv,
        u_send,
        u_recv,
        z_send,
        z_recv,
        small_send,
        small_recv,
    ) = refs[32:]
    z, u, w, core = place()
    me = block_of(z, u, w, core)
    above, below = device_of(z + 1, u, w, core), device_of(z - 1, u, w, core)
    across_u, across_w = device_of(z, 1 - u, w, core), device_of(z, u, 1 - w, core)
    sibling = device_of(z, w, u, 1 - core)
    near, far_z = z + 1 - 2 * (z % 2), (z + 2) % 4
    partners = (
        sibling,
        across_u,
        across_w,
        device_of(near, u, w, core),
        device_of(far_z, u, w, core),
    )
    middle_z = (z == 1) | (z == 2)

    barrier = pltpu.get_barrier_semaphore()
    for device in partners:
        pl.semaphore_signal(barrier, inc=1, device_id=device, device_id_type=MESH)

    @pl.when(middle_z)
    def _():
        pl.semaphore_signal(
            barrier, inc=1, device_id=device_of(3 - z, u, w, core), device_id_type=MESH
        )

    def plane_rows(group, ref, plane):
        count = 8 * BLOCKS[group][0]
        return ref.at[pl.ds(plane * count, count)]

    def load(group, plane):
        return pltpu.make_async_copy(
            plane_rows(group, partial[group], plane),
            plane_rows(group, part[group], plane),
            local_sem.at[group, plane],
        )

    for group in range(4):
        for plane in range(4):
            load(group, plane).start()

    pl.semaphore_wait(barrier, 5 + (z + 1) // 2 - z // 3 * 2)

    def rows(group, block):
        count = BLOCKS[group][0]
        return part[group].at[pl.ds(pl.multiple_of(block * count, 16), count)]

    def slot_of(far, column, line):
        return (far * 2 + column) * 2 + line

    def small_copy(i):
        return remote(
            small_held.at[i], small_got.at[i], small_send.at[i], small_recv.at[i], partners[i]
        )

    def small_event(i):
        if i < 0:
            small_held[0] = small_in[...]
            small_copy(0).start()
            return
        small_copy(i).wait_recv()
        total = small_held[i] + small_got[i]
        if i < 4:
            small_held[i + 1] = total
            small_copy(i + 1).start()
        else:
            small_out[...] = total

    def core_event(group, plane):
        load(group, plane).wait()
        for column in (0, 1):
            for line in (0, 1):
                slot = slot_of(plane, column, line)
                remote(
                    rows(group, block_of(plane, column, line, 1 - core)),
                    from_core[group].at[slot],
                    core_send.at[group],
                    core_recv.at[group, slot],
                    sibling,
                ).start()

    def wait_core(group, slot):
        held = from_core[group].at[slot]
        remote(held, held, core_send.at[group], core_recv.at[group, slot], sibling).wait_recv()

    def accumulate(group, block, terms):
        count = BLOCKS[group][0]
        first = pl.multiple_of(block * count, 16)

        @pl.loop(0, count // 16)
        def _(i):
            at = pl.multiple_of(i * 16, 16)
            total = part[group][pl.ds(first + at, 16), :].astype(jnp.float32)
            for ref, slot in terms:
                total = total + ref[slot, pl.ds(at, 16), :].astype(jnp.float32)
            part[group][pl.ds(first + at, 16), :] = total.astype(jnp.bfloat16)

    def at_distance(step, action):
        if step == 0:
            action(z, 0)
            return

        @pl.when(z + step < N_Z)
        def _():
            action(z + step, 1)

        @pl.when(z - step >= 0)
        def _():
            action(z - step, -1)

    def wait_w(group, slot):
        held = from_w[group].at[slot]
        remote(held, held, w_send.at[group], w_recv.at[group, slot], across_w).wait_recv()

    def w_event(group, step):
        def action(far, way, column):
            block, slot = block_of(far, column, 1 - w, core), slot_of(far, column, 1 - w)
            wait_core(group, slot)
            accumulate(group, block, [(from_core[group], slot)])
            remote(
                rows(group, block),
                from_w[group].at[far * 2 + column],
                w_send.at[group],
                w_recv.at[group, far * 2 + column],
                across_w,
            ).start()

        for column in (1 - u, u):
            at_distance(step, lambda far, way: action(far, way, column))

    def gathered(group, far, column):
        slot = slot_of(far, column, w)
        wait_core(group, slot)
        wait_w(group, far * 2 + column)
        return [(from_core[group], slot), (from_w[group], far * 2 + column)]

    def u_copy(group, src, slot):
        return remote(
            src, from_u[group].at[slot], u_send.at[group], u_recv.at[group, slot], across_u
        )

    def u_event(group, step):
        def action(far, way):
            block = block_of(far, 1 - u, w, core)
            accumulate(group, block, gathered(group, far, 1 - u))
            u_copy(group, rows(group, block), far).start()

        at_distance(step, action)

    def z_copy(group, block, way, slot):
        return remote(
            rows(group, block),
            from_z[group].at[way, slot],
            z_send.at[group, way, slot],
            z_recv.at[group, way, slot],
            below if way else above,
        )

    def z_take(group, block, way, slot):
        z_copy(group, block, way, slot).wait_recv()
        accumulate(group, block, [(from_z[group].at[way], slot)])

    def z_step(group, step, column, z_slot, terms_of):
        def action(far, way):
            block, slot = block_of(far, column, w, core), z_slot(far)
            accumulate(group, block, terms_of(far))
            if way >= 0:

                @pl.when(z > 0)
                def _():
                    z_take(group, block, 0, slot)

            if way <= 0:

                @pl.when(z < N_Z - 1)
                def _():
                    z_take(group, block, 1, slot)

            if way:
                z_copy(group, block, 0 if way > 0 else 1, slot).start()

        at_distance(step, action)

    def finish(group):
        count = BLOCKS[group][0]
        final[group][...] = part[group][
            pl.ds(pl.multiple_of(me * count, 16), count), :
        ].astype(jnp.float32)

    def z_late_event(group, step):
        def terms_of(far):
            terms = gathered(group, far, u)
            u_copy(group, from_u[group].at[far], far).wait_recv()
            return terms + [(from_u[group], far)]

        z_step(group, step, u, lambda far: far, terms_of)
        if step == 0:
            finish(group)

    def z_early_event(group, step):
        for column in (1 - u, u):
            z_step(
                group,
                step,
                column,
                lambda far: far * 2 + column,
                lambda far: gathered(group, far, column),
            )
            if step == 0 and column is not u:
                u_copy(group, rows(group, block_of(z, 1 - u, w, core)), 0).start()

    def u_late_event(group):
        u_copy(group, from_u[group].at[0], 0).wait_recv()
        accumulate(group, me, [(from_u[group], 0)])
        finish(group)

    actions = {
        "small": small_event,
        "core": core_event,
        "w": w_event,
        "u": u_event,
        "z_early": z_early_event,
        "z_late": z_late_event,
        "u_late": u_late_event,
    }
    for event in reduce_events():
        actions[event[0]](*event[1:])

    for group in range(4):
        z_first = REDUCE_ORDERS[group] == "zuw"
        count = BLOCKS[group][0]
        for sem, sends in ((core_send, 16), (w_send, 8), (u_send, 4 if z_first else 1)):
            rows_sent = part[group].at[pl.ds(0, sends * count)]
            remote(
                rows_sent, rows_sent, sem.at[group], core_recv.at[group, 0], sibling
            ).wait_send()
        for far in range(N_Z):
            for column in (0,) if z_first else (0, 1):
                slot = far if z_first else far * 2 + column

                @pl.when(z < far)
                def _():
                    z_copy(group, me, 0, slot).wait_send()

                @pl.when(z > far)
                def _():
                    z_copy(group, me, 1, slot).wait_send()

    for i in range(5):
        small_copy(i).wait_send()


def reduce_gradients(partials, small):
    narrow, sems = jnp.bfloat16, pltpu.SemaphoreType.DMA
    z_first = [order == "zuw" for order in REDUCE_ORDERS]
    scratch = [pltpu.VMEM((32 * rows, columns), narrow) for rows, columns in BLOCKS]
    scratch += [pltpu.VMEM((16, rows, columns), narrow) for rows, columns in BLOCKS]
    scratch += [pltpu.VMEM((8, rows, columns), narrow) for rows, columns in BLOCKS]
    scratch += [
        pltpu.VMEM((4 if first else 1, rows, columns), narrow)
        for (rows, columns), first in zip(BLOCKS, z_first)
    ]
    scratch += [
        pltpu.VMEM((2, 4 if first else 8, rows, columns), narrow)
        for (rows, columns), first in zip(BLOCKS, z_first)
    ]
    scratch += [pltpu.VMEM((5, 8, 1024), jnp.float32)] * 2
    scratch += [
        sems((4, 4)),
        sems((4,)),
        sems((4, 16)),
        sems((4,)),
        sems((4, 8)),
        sems((4,)),
        sems((4, 4)),
        sems((4, 2, 8)),
        sems((4, 2, 8)),
        sems((5,)),
        sems((5,)),
    ]
    return pl.pallas_call(
        reduce_kernel,
        out_shape=[jax.ShapeDtypeStruct(shape, jnp.float32) for shape in BLOCKS]
        + [jax.ShapeDtypeStruct((8, 1024), jnp.float32)],
        in_specs=[pl.BlockSpec(memory_space=pl.ANY)] * 4
        + [pl.BlockSpec(memory_space=pltpu.VMEM)],
        out_specs=[pl.BlockSpec(memory_space=pltpu.VMEM)] * 5,
        scratch_shapes=scratch,
        compiler_params=pltpu.CompilerParams(
            collective_id=2, has_side_effects=True, vmem_limit_bytes=58 * 2**20
        ),
        name="reduce_gradients",
    )(*partials, small)


def per_device_fast(
    tokens,
    depths,
    seq_spans,
    cotangent,
    w_query,
    key_weight,
    value_weight,
    w_out,
    w_gate,
    w_up,
    w_down,
    attn_gain,
    ffn_gain,
    router,
):
    narrow, wide = jnp.bfloat16, jnp.float32
    count_of_rows = tokens.shape[1]
    query_groupings = QUERY_HEADS // KEY_VALUE_HEADS
    chain = lax.axis_size("seq")
    most_spans = min(2**LOGC, chain // 2)
    depth_levels = (most_spans - 1).bit_length()
    extra_rows = ((1 << depth_levels) - most_spans) * count_of_rows
    window = most_spans * count_of_rows
    natural = jnp.arange(MODEL_WIDTH, dtype=jnp.int32)
    padded_at = (natural // OWN_ROWS) * PADDED_ROWS + natural % OWN_ROWS
    spread = (padded_at[:, None] == jnp.arange(PADDED_WIDTH, dtype=jnp.int32)[None, :]).astype(narrow)
    packed = pack_weights(
        spread, w_query, key_weight, value_weight, w_out, w_gate, w_up, w_down
    )
    attention_full, gate_full, up_full, down_full = gather_weights(packed)
    w_q = attention_full[:, :960]
    w_k = attention_full[:, 960:1280]
    w_v = attention_full[:, 1280:1600]
    w_o = attention_full[:, 1664:]

    def spread_vector(v):
        return jnp.dot(v, spread.astype(wide), precision=highest)

    gain_a, gain_f, routers = spread_vector(attn_gain), spread_vector(ffn_gain), spread_vector(router)

    def rms_parts_padded(vectors, gain):
        mean = jnp.sum(vectors * vectors, axis=-1, keepdims=True) / MODEL_WIDTH
        inv_rms = lax.rsqrt(mean + epsilon)
        normal_part = vectors * inv_rms
        return (normal_part * gain, normal_part, inv_rms)

    def rms_backward_padded(upstream, normal_part, inv_rms, gain):
        gain_grad = jnp.sum(upstream * normal_part, axis=0)
        scaled = upstream * gain
        inner = jnp.sum(scaled * normal_part, axis=-1, keepdims=True) / MODEL_WIDTH
        return (inv_rms * (scaled - normal_part * inner), gain_grad)

    place_index = lax.axis_index("seq")
    lengths = seq_spans[0]
    seq_ends = jnp.cumsum(lengths)
    span_ids = jnp.arange(chain, dtype=jnp.int32)
    owners = jnp.sum((seq_ends[None, :] <= span_ids[:, None]).astype(jnp.int32), axis=1)
    seq_starts = seq_ends - lengths
    numbers = jnp.arange(lengths.shape[0], dtype=jnp.int32)
    first_span = jnp.sum(
        jnp.where(numbers[None, :] == owners[:, None], seq_starts[None, :], 0), axis=1
    )
    index_of_span = jnp.sum(jnp.where(span_ids == place_index, span_ids - first_span, 0))
    positions = (index_of_span * count_of_rows + jnp.arange(count_of_rows, dtype=jnp.int32)).astype(
        wide
    )
    cosine_table, sine_table = angle_tables(positions, HEAD_SIZE)
    row_ids = jnp.arange(count_of_rows, dtype=jnp.int32)
    col_ids = jnp.arange(window, dtype=jnp.int32)
    offsets = most_spans - 1 - col_ids // count_of_rows
    local_col = col_ids - (most_spans - 1) * count_of_rows
    causal = jnp.where(offsets[None, :] == 0, local_col[None, :] <= row_ids[:, None], True)
    diagonal = (offsets[None, :] == 0) & (local_col[None, :] == row_ids[:, None])
    span_ok = (index_of_span >= offsets)[None, :]
    active_all = (depths[0][None, :] > jnp.arange(RECUR, dtype=jnp.int32)[:, None]).astype(wide)
    depth_win = depths[0].astype(narrow)
    for level in range(depth_levels):
        depth_win = jnp.concatenate([passed_along(depth_win, "seq", 1 << level), depth_win], axis=0)
    hidden_state = unscaled_product(tokens[0], spread)
    saved = []
    for recursion in range(RECUR):
        current_active = active_all[recursion]
        normalized, normal_a, inv_a = rms_parts_padded(hidden_state, gain_a)
        a_b = normalized.astype(narrow)
        raw_query = unscaled_product(a_b, w_q).reshape(count_of_rows, QUERY_HEADS, HEAD_SIZE)
        query_b = (
            apply_rotation(raw_query, cosine_table, sine_table)
            .astype(narrow)
            .reshape(count_of_rows, KEY_VALUE_HEADS, query_groupings, HEAD_SIZE)
        )
        unrotated_key = unscaled_product(a_b, w_k).reshape(
            count_of_rows, KEY_VALUE_HEADS, HEAD_SIZE
        )
        key_b = apply_rotation(unrotated_key, cosine_table, sine_table).astype(narrow)
        value_b = (
            unscaled_product(a_b, w_v)
            .astype(narrow)
            .reshape(count_of_rows, KEY_VALUE_HEADS, HEAD_SIZE)
        )
        pair = jnp.concatenate([key_b, value_b], axis=1)
        for level in range(depth_levels):
            pair = jnp.concatenate([passed_along(pair, "seq", 1 << level), pair], axis=0)
        keys_win, values_win = pair[:, :KEY_VALUE_HEADS], pair[:, KEY_VALUE_HEADS:]
        allowed = span_ok & causal & ((depth_win > recursion)[None, :] | diagonal)
        scores = masked_scores(query_b, keys_win, allowed)
        row_max = jnp.max(scores, axis=-1, keepdims=True)
        expon = jnp.exp(scores - row_max)
        row_total = jnp.sum(expon, axis=-1, keepdims=True)
        probs_b = (expon / row_total).astype(narrow)
        log_total = row_max + jnp.log(row_total)
        attended_b = (
            jnp.einsum("gjqk,kgd->qgjd", probs_b, values_win, preferred_element_type=wide)
            .astype(narrow)
            .reshape(count_of_rows, QUERY_HEADS * HEAD_SIZE)
        )
        attended_b = unscaled_product(attended_b, spread).astype(narrow)
        branch = unscaled_product(attended_b, w_o)
        middle = hidden_state + branch
        second, normal_z, inv_z = rms_parts_padded(middle, gain_f)
        second_b = second.astype(narrow)
        gate_value = unscaled_product(second_b, gate_full)
        up_value = unscaled_product(second_b, up_full)
        hidden_b = (jax.nn.silu(gate_value) * up_value).astype(narrow)
        ffn_out = unscaled_product(hidden_b, down_full)
        weight_gate = jax.nn.sigmoid(jnp.dot(hidden_state, routers[recursion], precision=highest))
        saved.append(
            (
                hidden_state,
                a_b,
                normal_a,
                inv_a,
                query_b,
                keys_win,
                values_win,
                allowed,
                log_total,
                attended_b,
                branch,
                normal_z,
                inv_z,
                second_b,
                gate_value,
                up_value,
                hidden_b,
                ffn_out,
                weight_gate,
                current_active,
            )
        )
        hidden_state = hidden_state + (current_active * weight_gate)[:, None] * (branch + ffn_out)
    output = right_product(hidden_state.astype(narrow), spread).astype(narrow)
    gain_a_total = jnp.zeros((PADDED_WIDTH,), wide)
    gain_f_total = jnp.zeros((PADDED_WIDTH,), wide)
    router_rows = [None] * RECUR
    factors = []
    grad_state = unscaled_product(cotangent[0], spread)
    for recursion in reversed(range(RECUR)):
        (
            state_in,
            a_b,
            normal_a,
            inv_a,
            query_b,
            keys_win,
            values_win,
            allowed,
            log_total,
            attended_b,
            branch,
            normal_z,
            inv_z,
            second_b,
            gate_value,
            up_value,
            hidden_b,
            ffn_out,
            weight_gate,
            current_active,
        ) = saved[recursion]
        mixing = current_active * weight_gate
        grad_delta = mixing[:, None] * grad_state
        grad_mix = jnp.sum(grad_state * (branch + ffn_out), axis=-1)
        grad_logit = current_active * grad_mix * weight_gate * (1.0 - weight_gate)
        router_rows[recursion] = jnp.dot(grad_logit, state_in, precision=highest)
        grad_next = grad_state + grad_logit[:, None] * routers[recursion][None, :]
        ffn_grad_b = grad_delta.astype(narrow)
        grad_hidden = right_product(ffn_grad_b, down_full)
        sigmoid_gate = jax.nn.sigmoid(gate_value)
        grad_gate_b = (
            grad_hidden * up_value * sigmoid_gate * (1.0 + gate_value * (1.0 - sigmoid_gate))
        ).astype(narrow)
        grad_up_b = (grad_hidden * gate_value * sigmoid_gate).astype(narrow)
        grad_second = right_product(grad_gate_b, gate_full) + right_product(grad_up_b, up_full)
        grad_middle, gain_f_part = rms_backward_padded(grad_second, normal_z, inv_z, gain_f)
        gain_f_total = gain_f_total + gain_f_part
        grad_branch_b = (grad_delta + grad_middle).astype(narrow)
        grad_attended_b = right_product(
            right_product(grad_branch_b, w_o).astype(narrow), spread
        ).astype(narrow).reshape(count_of_rows, KEY_VALUE_HEADS, query_groupings, HEAD_SIZE)
        grad_next = grad_next + grad_middle
        scores = masked_scores(query_b, keys_win, allowed)
        probs = jnp.exp(scores - log_total)
        probs_b = probs.astype(narrow)
        grad_probs = jnp.einsum(
            "qgjd,kgd->gjqk", grad_attended_b, values_win, preferred_element_type=wide
        )
        row_dot = jnp.sum(probs * grad_probs, axis=-1, keepdims=True)
        grad_scores_b = (probs * (grad_probs - row_dot)).astype(narrow)
        grad_queries = (
            jnp.einsum("gjqk,kgd->qgjd", grad_scores_b, keys_win, preferred_element_type=wide)
            * 0.125
        )
        grad_keys = (
            jnp.einsum("gjqk,qgjd->kgd", grad_scores_b, query_b, preferred_element_type=wide)
            * 0.125
        )
        grad_values = jnp.einsum(
            "gjqk,qgjd->kgd", probs_b, grad_attended_b, preferred_element_type=wide
        )
        local_pair = jnp.concatenate(
            [
                jnp.zeros((extra_rows, 2 * KEY_VALUE_HEADS, HEAD_SIZE), wide),
                jnp.concatenate([grad_keys, grad_values], axis=1),
            ],
            axis=0,
        )
        for level in reversed(range(depth_levels)):
            older_rows = (1 << level) * count_of_rows
            back = passed_along(for_sending(local_pair[:older_rows]), "seq", -(1 << level))
            local_pair = local_pair[older_rows:] + back
        grad_query_b = (
            apply_rotation(
                grad_queries.reshape(count_of_rows, QUERY_HEADS, HEAD_SIZE),
                cosine_table,
                -sine_table,
            )
            .astype(narrow)
            .reshape(count_of_rows, QUERY_HEADS * HEAD_SIZE)
        )
        grad_key_b = (
            apply_rotation(local_pair[:, :KEY_VALUE_HEADS], cosine_table, -sine_table)
            .astype(narrow)
            .reshape(count_of_rows, KEY_VALUE_HEADS * HEAD_SIZE)
        )
        grad_value_b = (
            local_pair[:, KEY_VALUE_HEADS:]
            .astype(narrow)
            .reshape(count_of_rows, KEY_VALUE_HEADS * HEAD_SIZE)
        )
        grad_qkv_b = jnp.concatenate([grad_query_b, grad_key_b, grad_value_b], axis=1)
        grad_normed = right_product(grad_qkv_b, attention_full[:, :1600])
        grad_input, gain_a_part = rms_backward_padded(grad_normed, normal_a, inv_a, gain_a)
        gain_a_total = gain_a_total + gain_a_part
        grad_state = grad_next + grad_input
        factors.append(
            (a_b, grad_qkv_b, attended_b, grad_branch_b, second_b, grad_gate_b, grad_up_b, hidden_b, ffn_grad_b)
        )
    a_all, qkv_all, o_all, t_all, b_all, gate_all, up_all, hidden_all, f_all = (
        jnp.concatenate(parts, axis=0) for parts in zip(*factors)
    )
    d_qkv = left_product(a_all, jnp.pad(qkv_all, ((0, 0), (0, 64))))
    partials = (
        jnp.concatenate([d_qkv, left_product(o_all, t_all)], axis=1).astype(narrow),
        left_product(b_all, gate_all).astype(narrow),
        left_product(b_all, up_all).astype(narrow),
        left_product(hidden_all, f_all).astype(narrow),
    )
    small = jnp.concatenate(
        [jnp.stack([gain_a_total, gain_f_total]), jnp.stack(router_rows), jnp.zeros((3, PADDED_WIDTH), wide)]
    )
    attention_sum, gate_sum, up_sum, down_sum, small_sum = reduce_gradients(partials, small)

    def gather_columns(x):
        return x.reshape(x.shape[0], 32, PADDED_ROWS)[:, :, :OWN_ROWS].reshape(x.shape[0], MODEL_WIDTH)

    small_natural = gather_columns(small_sum)
    own = attention_sum[:OWN_ROWS]
    return (
        output[None],
        gather_columns(grad_state)[None],
        own[:, :960].reshape(-1),
        own[:, 960:1280].reshape(-1),
        own[:, 1280:1600].reshape(-1),
        gather_columns(own[:, 1664:]).reshape(-1),
        gate_sum[:OWN_ROWS].reshape(-1),
        up_sum[:OWN_ROWS].reshape(-1),
        gather_columns(down_sum).reshape(-1),
        small_natural[0],
        small_natural[1],
        small_natural[2:5],
    )


def pack_weights(spread, w_query, key_weight, value_weight, w_out, w_gate, w_up, w_down):
    narrow = jnp.bfloat16

    def rows(flat):
        return flat.astype(narrow).reshape(OWN_ROWS, -1)

    attention = jnp.concatenate(
        [
            rows(w_query),
            rows(key_weight),
            rows(value_weight),
            jnp.zeros((OWN_ROWS, 64), narrow),
            unscaled_product(rows(w_out), spread).astype(narrow),
        ],
        axis=1,
    )
    extra = ((0, PADDED_ROWS - OWN_ROWS), (0, 0))
    return (
        jnp.pad(attention, extra),
        jnp.pad(rows(w_gate), extra),
        jnp.pad(rows(w_up), extra),
        unscaled_product(w_down.astype(narrow).reshape(-1, MODEL_WIDTH), spread).astype(narrow),
    )


def solution(mesh):
    fits = mesh.shape["seq"] == 8 and mesh.shape["rep"] == 4
    placed = (
        P("rep", "seq", None),
        P("rep", "seq"),
        P("rep", None),
        P("rep", "seq", None),
        P(("seq", "rep")),
        P(("seq", "rep")),
        P(("seq", "rep")),
        P(("seq", "rep")),
        P(("seq", "rep")),
        P(("seq", "rep")),
        P(("seq", "rep")),
        P(),
        P(),
        P(),
    )
    return jax.shard_map(
        per_device_fast if fits else per_device,
        mesh=mesh,
        in_specs=placed,
        out_specs=(
            P("rep", "seq", None),
            P("rep", "seq", None),
            P(("seq", "rep")),
            P(("seq", "rep")),
            P(("seq", "rep")),
            P(("seq", "rep")),
            P(("seq", "rep")),
            P(("seq", "rep")),
            P(("seq", "rep")),
            P(),
            P(),
            P(),
        ),
        check_vma=False,
    )
```

```python
import jax
import jax.numpy as jnp
import numpy as np
from jax import lax
from jax.experimental import pallas as pl
from jax.experimental.pallas import tpu as pltpu
from jax.sharding import PartitionSpec as P

MODEL_WIDTH = 960
QUERY_HEADS = 15
KEY_VALUE_HEADS = 5
HEAD_SIZE = 64
FEEDFORWARD_UNITS = 2560
LOGC = 5
RECUR = 3
OWN_ROWS = 30
PADDED_ROWS = 32
PADDED_WIDTH = 1024


highest = lax.Precision.HIGHEST
epsilon = 1e-06
masked_score = -1e30


def passed_along(value, axis, steps):
    count = lax.axis_size(axis)
    initial, last = (max(0, -steps), min(count, count - steps))
    return lax.ppermute(value, axis, [(source, source + steps) for source in range(initial, last)])


def for_sending(x):

    def short(part):
        return part.astype(jnp.bfloat16) if part.dtype == jnp.float32 else part

    return jax.tree.map(short, x)


def unscaled_product(left, right):
    return jnp.dot(left, right, preferred_element_type=jnp.float32)


def left_product(left, right):
    return lax.dot_general(
        left, right, (((0,), (0,)), ((), ())), preferred_element_type=jnp.float32
    )


def right_product(left, right):
    return lax.dot_general(
        left, right, (((1,), (1,)), ((), ())), preferred_element_type=jnp.float32
    )


def rms_parts(vectors, gain):
    inv_rms = lax.rsqrt(jnp.mean(vectors * vectors, axis=-1, keepdims=True) + epsilon)
    normal_part = vectors * inv_rms
    return (normal_part * gain, normal_part, inv_rms)


def rms_backward(upstream, normal_part, inv_rms, gain):
    gain_grad = jnp.sum(upstream * normal_part, axis=0)
    scaled = upstream * gain
    inner = jnp.mean(scaled * normal_part, axis=-1, keepdims=True)
    return (inv_rms * (scaled - normal_part * inner), gain_grad)


def angle_tables(positions, width):
    half_width = width // 2
    frequency = 10000.0 ** (-jnp.arange(half_width, dtype=jnp.float32) / half_width)
    angle_grid = positions[:, None] * frequency[None, :]
    return (jnp.cos(angle_grid)[:, None, :], jnp.sin(angle_grid)[:, None, :])


def apply_rotation(vectors, cosine_table, sine_table):
    half_width = vectors.shape[-1] // 2
    front_half = vectors[..., :half_width]
    back_half = vectors[..., half_width:]
    return jnp.concatenate(
        [
            front_half * cosine_table - back_half * sine_table,
            back_half * cosine_table + front_half * sine_table,
        ],
        axis=-1,
    )


def masked_scores(query_b, keys_win, allowed):
    scores = (
        jnp.einsum("qgjd,kgd->gjqk", query_b, keys_win, preferred_element_type=jnp.float32) * 0.125
    )
    return jnp.where(allowed[None, None], scores, masked_score)


def per_device(
    tokens,
    depths,
    seq_spans,
    cotangent,
    w_query,
    key_weight,
    value_weight,
    w_out,
    w_gate,
    w_up,
    w_down,
    attn_gain,
    ffn_gain,
    router,
):
    narrow_float_type = jnp.bfloat16
    wide_float_type = jnp.float32
    count_of_rows = tokens.shape[1]
    query_groupings = QUERY_HEADS // KEY_VALUE_HEADS
    chain = lax.axis_size("seq")
    most_spans = min(2**LOGC, chain // 2)
    depth_levels = (most_spans - 1).bit_length()
    extra_rows = ((1 << depth_levels) - most_spans) * count_of_rows
    window = most_spans * count_of_rows
    target_tokens = (
        (MODEL_WIDTH, QUERY_HEADS * HEAD_SIZE),
        (MODEL_WIDTH, KEY_VALUE_HEADS * HEAD_SIZE),
        (MODEL_WIDTH, KEY_VALUE_HEADS * HEAD_SIZE),
        (QUERY_HEADS * HEAD_SIZE, MODEL_WIDTH),
        (MODEL_WIDTH, FEEDFORWARD_UNITS),
        (MODEL_WIDTH, FEEDFORWARD_UNITS),
        (FEEDFORWARD_UNITS, MODEL_WIDTH),
    )
    fetched = (
        lax.all_gather(w_query.astype(narrow_float_type), ("seq", "rep"), axis=0, tiled=True),
        lax.all_gather(key_weight.astype(narrow_float_type), ("seq", "rep"), axis=0, tiled=True),
        lax.all_gather(value_weight.astype(narrow_float_type), ("seq", "rep"), axis=0, tiled=True),
        lax.all_gather(w_out.astype(narrow_float_type), ("seq", "rep"), axis=0, tiled=True),
        lax.all_gather(w_gate.astype(narrow_float_type), ("seq", "rep"), axis=0, tiled=True),
        lax.all_gather(w_up.astype(narrow_float_type), ("seq", "rep"), axis=0, tiled=True),
        lax.all_gather(w_down.astype(narrow_float_type), ("seq", "rep"), axis=0, tiled=True),
    )
    attention_weights = tuple(
        (gathered.reshape(target) for gathered, target in zip(fetched, target_tokens))
    )
    place = lax.axis_index("seq")
    lengths = seq_spans[0]
    seq_ends = jnp.cumsum(lengths)
    span_ids = jnp.arange(chain, dtype=jnp.int32)
    owners = jnp.sum((seq_ends[None, :] <= span_ids[:, None]).astype(jnp.int32), axis=1)
    seq_starts = seq_ends - lengths
    numbers = jnp.arange(lengths.shape[0], dtype=jnp.int32)
    first_span = jnp.sum(
        jnp.where(numbers[None, :] == owners[:, None], seq_starts[None, :], 0), axis=1
    )
    index_of_span = jnp.sum(jnp.where(span_ids == place, span_ids - first_span, 0))
    positions = (index_of_span * count_of_rows + jnp.arange(count_of_rows, dtype=jnp.int32)).astype(
        wide_float_type
    )
    cosine_table, sine_table = angle_tables(positions, HEAD_SIZE)
    row_ids = jnp.arange(count_of_rows, dtype=jnp.int32)
    col_ids = jnp.arange(window, dtype=jnp.int32)
    offsets = most_spans - 1 - col_ids // count_of_rows
    local_col = col_ids - (most_spans - 1) * count_of_rows
    causal = jnp.where(offsets[None, :] == 0, local_col[None, :] <= row_ids[:, None], True)
    diagonal = (offsets[None, :] == 0) & (local_col[None, :] == row_ids[:, None])
    span_ok = (index_of_span >= offsets)[None, :]
    active_all = (depths[0][None, :] > jnp.arange(RECUR, dtype=jnp.int32)[:, None]).astype(
        wide_float_type
    )
    hidden_state = tokens[0].astype(wide_float_type)
    saved = []
    for recursion in range(RECUR):
        current_active = active_all[recursion]
        normalized_input, normal_a, inv_a = rms_parts(hidden_state, attn_gain)
        normalized_input_copy = normalized_input.astype(narrow_float_type)
        raw_query = unscaled_product(normalized_input_copy, attention_weights[0]).reshape(
            count_of_rows, QUERY_HEADS, HEAD_SIZE
        )
        query_b = (
            apply_rotation(raw_query, cosine_table, sine_table)
            .astype(narrow_float_type)
            .reshape(count_of_rows, KEY_VALUE_HEADS, query_groupings, HEAD_SIZE)
        )
        unrotated_key = unscaled_product(normalized_input_copy, attention_weights[1]).reshape(
            count_of_rows, KEY_VALUE_HEADS, HEAD_SIZE
        )
        key_b = apply_rotation(unrotated_key, cosine_table, sine_table).astype(narrow_float_type)
        value_copy = (
            unscaled_product(normalized_input_copy, attention_weights[2])
            .astype(narrow_float_type)
            .reshape(count_of_rows, KEY_VALUE_HEADS, HEAD_SIZE)
        )
        active_b = current_active.astype(narrow_float_type)
        keys_win = key_b
        values_win = value_copy
        active_win = active_b
        for level in range(depth_levels):
            far_key, far_value, far_active = passed_along(
                (keys_win, values_win, active_win), "seq", 1 << level
            )
            keys_win = jnp.concatenate([far_key, keys_win], axis=0)
            values_win = jnp.concatenate([far_value, values_win], axis=0)
            active_win = jnp.concatenate([far_active, active_win], axis=0)
        allowed = span_ok & causal & ((active_win > 0)[None, :] | diagonal)
        scores = masked_scores(query_b, keys_win, allowed)
        row_max = jnp.max(scores, axis=-1, keepdims=True)
        expon = jnp.exp(scores - row_max)
        row_total = jnp.sum(expon, axis=-1, keepdims=True)
        probs_b = (expon / row_total).astype(narrow_float_type)
        log_total = row_max + jnp.log(row_total)
        attended_b = (
            jnp.einsum(
                "gjqk,kgd->qgjd", probs_b, values_win, preferred_element_type=wide_float_type
            )
            .astype(narrow_float_type)
            .reshape(count_of_rows, QUERY_HEADS * HEAD_SIZE)
        )
        branch = unscaled_product(attended_b, attention_weights[3])
        middle = hidden_state + branch
        second, normal_z, inv_z = rms_parts(middle, ffn_gain)
        second_b = second.astype(narrow_float_type)
        gate_value = unscaled_product(second_b, attention_weights[4])
        up_value = unscaled_product(second_b, attention_weights[5])
        hidden_b = (jax.nn.silu(gate_value) * up_value).astype(narrow_float_type)
        ffn_out = unscaled_product(hidden_b, attention_weights[6])
        weight_gate = jax.nn.sigmoid(jnp.dot(hidden_state, router[recursion], precision=highest))
        saved.append(
            (
                hidden_state,
                normalized_input_copy,
                normal_a,
                inv_a,
                query_b,
                keys_win,
                values_win,
                allowed,
                log_total,
                attended_b,
                branch,
                normal_z,
                inv_z,
                second_b,
                gate_value,
                up_value,
                hidden_b,
                ffn_out,
                weight_gate,
                current_active,
            )
        )
        hidden_state = hidden_state + (current_active * weight_gate)[:, None] * (branch + ffn_out)
    output = hidden_state.astype(narrow_float_type)
    refetched = (
        lax.all_gather(w_query.astype(narrow_float_type), ("seq", "rep"), axis=0, tiled=True),
        lax.all_gather(key_weight.astype(narrow_float_type), ("seq", "rep"), axis=0, tiled=True),
        lax.all_gather(value_weight.astype(narrow_float_type), ("seq", "rep"), axis=0, tiled=True),
        lax.all_gather(w_out.astype(narrow_float_type), ("seq", "rep"), axis=0, tiled=True),
        lax.all_gather(w_gate.astype(narrow_float_type), ("seq", "rep"), axis=0, tiled=True),
        lax.all_gather(w_up.astype(narrow_float_type), ("seq", "rep"), axis=0, tiled=True),
        lax.all_gather(w_down.astype(narrow_float_type), ("seq", "rep"), axis=0, tiled=True),
    )
    back_weights = tuple(
        (gathered.reshape(target) for gathered, target in zip(refetched, target_tokens))
    )
    master_shapes = (w_query, key_weight, value_weight, w_out, w_gate, w_up, w_down)
    shares = tuple((jnp.zeros_like(master) for master in master_shapes))
    gain_a_total = jnp.zeros((MODEL_WIDTH,), wide_float_type)
    gain_f_total = jnp.zeros((MODEL_WIDTH,), wide_float_type)
    router_rows = [None] * RECUR
    grad_state = cotangent[0].astype(wide_float_type)
    for recursion in reversed(range(RECUR)):
        (
            state_in,
            normalized_input_copy,
            normal_a,
            inv_a,
            query_b,
            keys_win,
            values_win,
            allowed,
            log_total,
            attended_b,
            branch,
            normal_z,
            inv_z,
            second_b,
            gate_value,
            up_value,
            hidden_b,
            ffn_out,
            weight_gate,
            current_active,
        ) = saved[recursion]
        mixing = current_active * weight_gate
        grad_delta = mixing[:, None] * grad_state
        grad_mix = jnp.sum(grad_state * (branch + ffn_out), axis=-1)
        grad_logit = current_active * grad_mix * weight_gate * (1.0 - weight_gate)
        router_rows[recursion] = jnp.dot(grad_logit, state_in, precision=highest)
        grad_next = grad_state + grad_logit[:, None] * router[recursion][None, :]
        ffn_grad_b = grad_delta.astype(narrow_float_type)
        grad_hidden = right_product(ffn_grad_b, back_weights[6])
        d_down = left_product(hidden_b, ffn_grad_b)
        sigmoid_gate = jax.nn.sigmoid(gate_value)
        grad_gate_b = (
            grad_hidden * up_value * sigmoid_gate * (1.0 + gate_value * (1.0 - sigmoid_gate))
        ).astype(narrow_float_type)
        grad_up_b = (grad_hidden * gate_value * sigmoid_gate).astype(narrow_float_type)
        grad_second = right_product(grad_gate_b, back_weights[4]) + right_product(
            grad_up_b, back_weights[5]
        )
        d_gate = left_product(second_b, grad_gate_b)
        d_up = left_product(second_b, grad_up_b)
        grad_middle, gain_f_part = rms_backward(grad_second, normal_z, inv_z, ffn_gain)
        gain_f_total = gain_f_total + gain_f_part
        grad_branch_b = (grad_delta + grad_middle).astype(narrow_float_type)
        grad_attended_b = (
            right_product(grad_branch_b, back_weights[3])
            .astype(narrow_float_type)
            .reshape(count_of_rows, KEY_VALUE_HEADS, query_groupings, HEAD_SIZE)
        )
        d_out = left_product(attended_b, grad_branch_b)
        grad_next = grad_next + grad_middle
        scores = masked_scores(query_b, keys_win, allowed)
        probs = jnp.exp(scores - log_total)
        probs_b = probs.astype(narrow_float_type)
        grad_probs = jnp.einsum(
            "qgjd,kgd->gjqk", grad_attended_b, values_win, preferred_element_type=wide_float_type
        )
        row_dot = jnp.sum(probs * grad_probs, axis=-1, keepdims=True)
        grad_scores_b = (probs * (grad_probs - row_dot)).astype(narrow_float_type)
        grad_queries = (
            jnp.einsum(
                "gjqk,kgd->qgjd", grad_scores_b, keys_win, preferred_element_type=wide_float_type
            )
            * 0.125
        )
        grad_keys = (
            jnp.einsum(
                "gjqk,qgjd->kgd", grad_scores_b, query_b, preferred_element_type=wide_float_type
            )
            * 0.125
        )
        grad_values = jnp.einsum(
            "gjqk,qgjd->kgd", probs_b, grad_attended_b, preferred_element_type=wide_float_type
        )
        extra_zero_rows = jnp.zeros((extra_rows, KEY_VALUE_HEADS, HEAD_SIZE), wide_float_type)
        local_span_keys = jnp.concatenate([extra_zero_rows, grad_keys], axis=0)
        local_span_values = jnp.concatenate([extra_zero_rows, grad_values], axis=0)
        for level in reversed(range(depth_levels)):
            older_rows = (1 << level) * count_of_rows
            back_keys, back_values = passed_along(
                (
                    for_sending(local_span_keys[:older_rows]),
                    for_sending(local_span_values[:older_rows]),
                ),
                "seq",
                -(1 << level),
            )
            local_span_keys = local_span_keys[older_rows:] + back_keys
            local_span_values = local_span_values[older_rows:] + back_values
        grad_query_b = (
            apply_rotation(
                grad_queries.reshape(count_of_rows, QUERY_HEADS, HEAD_SIZE),
                cosine_table,
                -sine_table,
            )
            .astype(narrow_float_type)
            .reshape(count_of_rows, QUERY_HEADS * HEAD_SIZE)
        )
        grad_key_b = (
            apply_rotation(local_span_keys, cosine_table, -sine_table)
            .astype(narrow_float_type)
            .reshape(count_of_rows, KEY_VALUE_HEADS * HEAD_SIZE)
        )
        value_gradient_copy = local_span_values.astype(narrow_float_type).reshape(
            count_of_rows, KEY_VALUE_HEADS * HEAD_SIZE
        )
        grad_normed = (
            right_product(grad_query_b, back_weights[0])
            + right_product(grad_key_b, back_weights[1])
            + right_product(value_gradient_copy, back_weights[2])
        )
        d_query = left_product(normalized_input_copy, grad_query_b)
        d_key = left_product(normalized_input_copy, grad_key_b)
        d_value = left_product(normalized_input_copy, value_gradient_copy)
        grad_input, gain_a_part = rms_backward(grad_normed, normal_a, inv_a, attn_gain)
        gain_a_total = gain_a_total + gain_a_part
        grad_state = grad_next + grad_input
        local_grads = (
            d_query.reshape(-1),
            d_key.reshape(-1),
            d_value.reshape(-1),
            d_out.reshape(-1),
            d_gate.reshape(-1),
            d_up.reshape(-1),
            d_down.reshape(-1),
        )
        summed = (
            lax.psum_scatter(local_grads[0], ("seq", "rep"), scatter_dimension=0, tiled=True),
            lax.psum_scatter(local_grads[1], ("seq", "rep"), scatter_dimension=0, tiled=True),
            lax.psum_scatter(local_grads[2], ("seq", "rep"), scatter_dimension=0, tiled=True),
            lax.psum_scatter(local_grads[3], ("seq", "rep"), scatter_dimension=0, tiled=True),
            lax.psum_scatter(local_grads[4], ("seq", "rep"), scatter_dimension=0, tiled=True),
            lax.psum_scatter(local_grads[5], ("seq", "rep"), scatter_dimension=0, tiled=True),
            lax.psum_scatter(local_grads[6], ("seq", "rep"), scatter_dimension=0, tiled=True),
        )
        shares = tuple((old_share + new_share for old_share, new_share in zip(shares, summed)))
    router_grad = jnp.stack(router_rows, axis=0)
    gain_a_sum, gain_f_sum, router_sum = lax.psum(
        (gain_a_total, gain_f_total, router_grad), ("seq", "rep")
    )
    return (
        output[None],
        grad_state[None],
        shares[0],
        shares[1],
        shares[2],
        shares[3],
        shares[4],
        shares[5],
        shares[6],
        gain_a_sum,
        gain_f_sum,
        router_sum,
    )


MESH = pl.DeviceIdType.MESH
N_Z = 4
BLOCKS = ((32, 2816), (32, 2560), (32, 2560), (80, 1024))
GATHER_ORDERS = ("uzw", "zuw", "uzw", "zuw")
REDUCE_ORDERS = ("zuw", "uzw", "zuw", "uzw")


def place():
    seq = lax.axis_index("seq")
    rep = lax.axis_index("rep")
    z, x, y, core = seq // 2, seq % 2, rep // 2, rep % 2
    return z, x + core * (y - x), y + core * (x - y), core


def device_of(z, u, w, core):
    x, y = u + core * (w - u), w + core * (u - w)
    return (z * 2 + x, y * 2 + core)


def block_of(z, u, w, core):
    seq, rep = device_of(z, u, w, core)
    return seq * 4 + rep


def remote(src, dst, send_sem, recv_sem, device):
    return pltpu.make_async_remote_copy(
        src_ref=src,
        dst_ref=dst,
        send_sem=send_sem,
        recv_sem=recv_sem,
        device_id=device,
        device_id_type=MESH,
    )


def gather_events():
    events = [("own", group) for group in range(4)]
    for step in range(6):
        for group in range(4):
            if GATHER_ORDERS[group] == "zuw":
                if 1 <= step <= 3:
                    events.append(("z", group, step, 0))
                if 1 <= step <= 4:
                    events.append(("u", group, step - 1))
                    events.append(("w", group, step - 1, 0))
                if 2 <= step <= 5:
                    events.append(("w", group, step - 2, 1))
            else:
                if step == 1:
                    events.append(("first", group))
                if 1 <= step <= 3:
                    events.append(("z", group, step, 0))
                if 2 <= step <= 4:
                    events.append(("z", group, step - 1, 1))
                if 1 <= step <= 4:
                    events.append(("w", group, step - 1, 0))
                if 2 <= step <= 5:
                    events.append(("w", group, step - 2, 1))
    return events


def gather_kernel(*refs):
    own, full = refs[:4], refs[4:8]
    recv_sem, z_sem, u_sem, w_sem, core_sem, local_sem = refs[8:]
    z, u, w, core = place()
    me = block_of(z, u, w, core)
    above, below = device_of(z + 1, u, w, core), device_of(z - 1, u, w, core)
    across_u, across_w = device_of(z, 1 - u, w, core), device_of(z, u, 1 - w, core)
    sibling = device_of(z, w, u, 1 - core)

    barrier = pltpu.get_barrier_semaphore()
    for device in (across_u, across_w, sibling):
        pl.semaphore_signal(barrier, inc=1, device_id=device, device_id_type=MESH)

    @pl.when(z < N_Z - 1)
    def _():
        pl.semaphore_signal(barrier, inc=1, device_id=above, device_id_type=MESH)

    @pl.when(z > 0)
    def _():
        pl.semaphore_signal(barrier, inc=1, device_id=below, device_id_type=MESH)

    pl.semaphore_wait(barrier, 4 + (z + 1) // 2 - z // 3 * 2)

    def rows(group, block):
        count = BLOCKS[group][0]
        return full[group].at[pl.ds(pl.multiple_of(block * count, 16), count)]

    def copy(group, block, src, send_sem, device):
        return remote(src, rows(group, block), send_sem, recv_sem.at[group, block], device)

    def send(group, block, src, ways, slot=0):
        if "z" in ways:

            @pl.when(z < N_Z - 1)
            def _():
                copy(group, block, src, z_sem.at[group, 0, slot], above).start()

            @pl.when(z > 0)
            def _():
                copy(group, block, src, z_sem.at[group, 1, slot], below).start()

        if "+" in ways:

            @pl.when(z < N_Z - 1)
            def _():
                copy(group, block, src, z_sem.at[group, 0, slot], above).start()

        if "-" in ways:

            @pl.when(z > 0)
            def _():
                copy(group, block, src, z_sem.at[group, 1, slot], below).start()

        if "u" in ways:
            copy(group, block, src, u_sem.at[group], across_u).start()
        if "w" in ways:
            copy(group, block, src, w_sem.at[group], across_w).start()
        if "c" in ways:
            copy(group, block, src, core_sem.at[group], sibling).start()

    def passed_on(group, block, ways, slot=0):
        copy(group, block, rows(group, block), core_sem.at[group], sibling).wait_recv()
        send(group, block, rows(group, block), ways, slot)

    def at_distance(step, action):
        if step == 0:
            action(z, "")
            return

        @pl.when(z - step >= 0)
        def _():
            action(z - step, "+")

        @pl.when(z + step < N_Z)
        def _():
            action(z + step, "-")

    def own_event(group):
        send(group, me, own[group], "zuwc")
        pltpu.make_async_copy(own[group], rows(group, me), local_sem.at[group]).start()

    def first_event(group):
        passed_on(group, block_of(z, 1 - u, w, core), "zwc", 1)

    def z_event(group, step, other):
        z_first = GATHER_ORDERS[group] == "zuw"
        column = 1 - u if other else u
        slot = step if z_first else 2 * step + other
        at_distance(
            step,
            lambda far, way: passed_on(
                group,
                block_of(far, column, w, core),
                way + ("uwc" if z_first else "wc"),
                slot,
            ),
        )

    def u_event(group, step):
        at_distance(
            step, lambda far, way: passed_on(group, block_of(far, 1 - u, w, core), "wc")
        )

    def w_event(group, step, other):
        column = 1 - u if other else u
        at_distance(
            step, lambda far, way: passed_on(group, block_of(far, column, 1 - w, core), "c")
        )

    actions = {"own": own_event, "first": first_event, "z": z_event, "u": u_event, "w": w_event}
    for event in gather_events():
        actions[event[0]](*event[1:])

    for group in range(4):
        z_first = GATHER_ORDERS[group] == "zuw"
        count = BLOCKS[group][0]
        pltpu.make_async_copy(own[group], rows(group, me), local_sem.at[group]).wait()

        @pl.loop(0, 16)
        def _(i):
            block = i * 2 + (1 - core)
            copy(group, block, rows(group, block), core_sem.at[group], sibling).wait_recv()

        for sem, sends in ((u_sem, 4 if z_first else 1), (w_sem, 8), (core_sem, 16)):
            part = full[group].at[pl.ds(0, sends * count)]
            remote(part, part, sem.at[group], recv_sem.at[group, 0], sibling).wait_send()
        for step in range(N_Z):
            for other in (0,) if z_first else (0, 1):
                slot = step if z_first else 2 * step + other

                @pl.when((z - step >= 0) & (z < N_Z - 1))
                def _():
                    copy(group, me, own[group], z_sem.at[group, 0, slot], above).wait_send()

                @pl.when((z + step < N_Z) & (z > 0))
                def _():
                    copy(group, me, own[group], z_sem.at[group, 1, slot], below).wait_send()


def gather_weights(packed):
    sems = pltpu.SemaphoreType.DMA
    return pl.pallas_call(
        gather_kernel,
        out_shape=[
            jax.ShapeDtypeStruct((32 * rows, columns), jnp.bfloat16) for rows, columns in BLOCKS
        ],
        in_specs=[pl.BlockSpec(memory_space=pl.ANY)] * 4,
        out_specs=[pl.BlockSpec(memory_space=pl.ANY)] * 4,
        scratch_shapes=[
            sems((4, 32)),
            sems((4, 2, 8)),
            sems((4,)),
            sems((4,)),
            sems((4,)),
            sems((4,)),
        ],
        compiler_params=pltpu.CompilerParams(
            collective_id=1, has_side_effects=True, vmem_limit_bytes=16 * 2**20
        ),
        name="gather_weights",
    )(*packed)


def reduce_events():
    events = [("small", -1)]

    def entry(group):
        return [("core", group, plane) for plane in range(4)] + [
            ("w", group, step) for step in (3, 2, 1, 0)
        ]

    def middle(group):
        kind = "u" if REDUCE_ORDERS[group] == "zuw" else "z_early"
        return [(kind, group, step) for step in (3, 2, 1, 0)]

    def last(group):
        if REDUCE_ORDERS[group] == "zuw":
            return [("z_late", group, step) for step in (3, 2, 1, 0)]
        return [("u_late", group)]

    for stage in (
        entry(0),
        entry(1),
        [("small", 0)],
        middle(0),
        entry(2),
        [("small", 1)],
        middle(1),
        last(0),
        [("small", 2)],
        entry(3),
        middle(2),
        [("small", 3)],
        last(1),
        middle(3),
        [("small", 4)],
        last(2),
        last(3),
    ):
        events += stage
    return events


def reduce_kernel(*refs):
    partial, small_in, final, small_out = refs[:4], refs[4], refs[5:9], refs[9]
    part, from_core, from_w, from_u, from_z = (refs[10 + 4 * i : 14 + 4 * i] for i in range(5))
    small_held, small_got = refs[30:32]
    (
        local_sem,
        core_send,
        core_recv,
        w_send,
        w_recv,
        u_send,
        u_recv,
        z_send,
        z_recv,
        small_send,
        small_recv,
    ) = refs[32:]
    z, u, w, core = place()
    me = block_of(z, u, w, core)
    above, below = device_of(z + 1, u, w, core), device_of(z - 1, u, w, core)
    across_u, across_w = device_of(z, 1 - u, w, core), device_of(z, u, 1 - w, core)
    sibling = device_of(z, w, u, 1 - core)
    near, far_z = z + 1 - 2 * (z % 2), (z + 2) % 4
    partners = (
        sibling,
        across_u,
        across_w,
        device_of(near, u, w, core),
        device_of(far_z, u, w, core),
    )
    middle_z = (z == 1) | (z == 2)

    barrier = pltpu.get_barrier_semaphore()
    for device in partners:
        pl.semaphore_signal(barrier, inc=1, device_id=device, device_id_type=MESH)

    @pl.when(middle_z)
    def _():
        pl.semaphore_signal(
            barrier, inc=1, device_id=device_of(3 - z, u, w, core), device_id_type=MESH
        )

    def plane_rows(group, ref, plane):
        count = 8 * BLOCKS[group][0]
        return ref.at[pl.ds(plane * count, count)]

    def load(group, plane):
        return pltpu.make_async_copy(
            plane_rows(group, partial[group], plane),
            plane_rows(group, part[group], plane),
            local_sem.at[group, plane],
        )

    for group in range(4):
        for plane in range(4):
            load(group, plane).start()

    pl.semaphore_wait(barrier, 5 + (z + 1) // 2 - z // 3 * 2)

    def rows(group, block):
        count = BLOCKS[group][0]
        return part[group].at[pl.ds(pl.multiple_of(block * count, 16), count)]

    def slot_of(far, column, line):
        return (far * 2 + column) * 2 + line

    def small_copy(i):
        return remote(
            small_held.at[i], small_got.at[i], small_send.at[i], small_recv.at[i], partners[i]
        )

    def small_event(i):
        if i < 0:
            small_held[0] = small_in[...]
            small_copy(0).start()
            return
        small_copy(i).wait_recv()
        total = small_held[i] + small_got[i]
        if i < 4:
            small_held[i + 1] = total
            small_copy(i + 1).start()
        else:
            small_out[...] = total

    def core_event(group, plane):
        load(group, plane).wait()
        for column in (0, 1):
            for line in (0, 1):
                slot = slot_of(plane, column, line)
                remote(
                    rows(group, block_of(plane, column, line, 1 - core)),
                    from_core[group].at[slot],
                    core_send.at[group],
                    core_recv.at[group, slot],
                    sibling,
                ).start()

    def wait_core(group, slot):
        held = from_core[group].at[slot]
        remote(held, held, core_send.at[group], core_recv.at[group, slot], sibling).wait_recv()

    def accumulate(group, block, terms):
        count = BLOCKS[group][0]
        first = pl.multiple_of(block * count, 16)

        @pl.loop(0, count // 16)
        def _(i):
            at = pl.multiple_of(i * 16, 16)
            total = part[group][pl.ds(first + at, 16), :].astype(jnp.float32)
            for ref, slot in terms:
                total = total + ref[slot, pl.ds(at, 16), :].astype(jnp.float32)
            part[group][pl.ds(first + at, 16), :] = total.astype(jnp.bfloat16)

    def at_distance(step, action):
        if step == 0:
            action(z, 0)
            return

        @pl.when(z + step < N_Z)
        def _():
            action(z + step, 1)

        @pl.when(z - step >= 0)
        def _():
            action(z - step, -1)

    def wait_w(group, slot):
        held = from_w[group].at[slot]
        remote(held, held, w_send.at[group], w_recv.at[group, slot], across_w).wait_recv()

    def w_event(group, step):
        def action(far, way, column):
            block, slot = block_of(far, column, 1 - w, core), slot_of(far, column, 1 - w)
            wait_core(group, slot)
            accumulate(group, block, [(from_core[group], slot)])
            remote(
                rows(group, block),
                from_w[group].at[far * 2 + column],
                w_send.at[group],
                w_recv.at[group, far * 2 + column],
                across_w,
            ).start()

        for column in (1 - u, u):
            at_distance(step, lambda far, way: action(far, way, column))

    def gathered(group, far, column):
        slot = slot_of(far, column, w)
        wait_core(group, slot)
        wait_w(group, far * 2 + column)
        return [(from_core[group], slot), (from_w[group], far * 2 + column)]

    def u_copy(group, src, slot):
        return remote(
            src, from_u[group].at[slot], u_send.at[group], u_recv.at[group, slot], across_u
        )

    def u_event(group, step):
        def action(far, way):
            block = block_of(far, 1 - u, w, core)
            accumulate(group, block, gathered(group, far, 1 - u))
            u_copy(group, rows(group, block), far).start()

        at_distance(step, action)

    def z_copy(group, block, way, slot):
        return remote(
            rows(group, block),
            from_z[group].at[way, slot],
            z_send.at[group, way, slot],
            z_recv.at[group, way, slot],
            below if way else above,
        )

    def z_take(group, block, way, slot):
        z_copy(group, block, way, slot).wait_recv()
        accumulate(group, block, [(from_z[group].at[way], slot)])

    def z_step(group, step, column, z_slot, terms_of):
        def action(far, way):
            block, slot = block_of(far, column, w, core), z_slot(far)
            accumulate(group, block, terms_of(far))
            if way >= 0:

                @pl.when(z > 0)
                def _():
                    z_take(group, block, 0, slot)

            if way <= 0:

                @pl.when(z < N_Z - 1)
                def _():
                    z_take(group, block, 1, slot)

            if way:
                z_copy(group, block, 0 if way > 0 else 1, slot).start()

        at_distance(step, action)

    def finish(group):
        count = BLOCKS[group][0]
        final[group][...] = part[group][
            pl.ds(pl.multiple_of(me * count, 16), count), :
        ].astype(jnp.float32)

    def z_late_event(group, step):
        def terms_of(far):
            terms = gathered(group, far, u)
            u_copy(group, from_u[group].at[far], far).wait_recv()
            return terms + [(from_u[group], far)]

        z_step(group, step, u, lambda far: far, terms_of)
        if step == 0:
            finish(group)

    def z_early_event(group, step):
        for column in (1 - u, u):
            z_step(
                group,
                step,
                column,
                lambda far: far * 2 + column,
                lambda far: gathered(group, far, column),
            )
            if step == 0 and column is not u:
                u_copy(group, rows(group, block_of(z, 1 - u, w, core)), 0).start()

    def u_late_event(group):
        u_copy(group, from_u[group].at[0], 0).wait_recv()
        accumulate(group, me, [(from_u[group], 0)])
        finish(group)

    actions = {
        "small": small_event,
        "core": core_event,
        "w": w_event,
        "u": u_event,
        "z_early": z_early_event,
        "z_late": z_late_event,
        "u_late": u_late_event,
    }
    for event in reduce_events():
        actions[event[0]](*event[1:])

    for group in range(4):
        z_first = REDUCE_ORDERS[group] == "zuw"
        count = BLOCKS[group][0]
        for sem, sends in ((core_send, 16), (w_send, 8), (u_send, 4 if z_first else 1)):
            rows_sent = part[group].at[pl.ds(0, sends * count)]
            remote(
                rows_sent, rows_sent, sem.at[group], core_recv.at[group, 0], sibling
            ).wait_send()
        for far in range(N_Z):
            for column in (0,) if z_first else (0, 1):
                slot = far if z_first else far * 2 + column

                @pl.when(z < far)
                def _():
                    z_copy(group, me, 0, slot).wait_send()

                @pl.when(z > far)
                def _():
                    z_copy(group, me, 1, slot).wait_send()

    for i in range(5):
        small_copy(i).wait_send()


def reduce_gradients(partials, small):
    narrow, sems = jnp.bfloat16, pltpu.SemaphoreType.DMA
    z_first = [order == "zuw" for order in REDUCE_ORDERS]
    scratch = [pltpu.VMEM((32 * rows, columns), narrow) for rows, columns in BLOCKS]
    scratch += [pltpu.VMEM((16, rows, columns), narrow) for rows, columns in BLOCKS]
    scratch += [pltpu.VMEM((8, rows, columns), narrow) for rows, columns in BLOCKS]
    scratch += [
        pltpu.VMEM((4 if first else 1, rows, columns), narrow)
        for (rows, columns), first in zip(BLOCKS, z_first)
    ]
    scratch += [
        pltpu.VMEM((2, 4 if first else 8, rows, columns), narrow)
        for (rows, columns), first in zip(BLOCKS, z_first)
    ]
    scratch += [pltpu.VMEM((5, 8, 1024), jnp.float32)] * 2
    scratch += [
        sems((4, 4)),
        sems((4,)),
        sems((4, 16)),
        sems((4,)),
        sems((4, 8)),
        sems((4,)),
        sems((4, 4)),
        sems((4, 2, 8)),
        sems((4, 2, 8)),
        sems((5,)),
        sems((5,)),
    ]
    return pl.pallas_call(
        reduce_kernel,
        out_shape=[jax.ShapeDtypeStruct(shape, jnp.float32) for shape in BLOCKS]
        + [jax.ShapeDtypeStruct((8, 1024), jnp.float32)],
        in_specs=[pl.BlockSpec(memory_space=pl.ANY)] * 4
        + [pl.BlockSpec(memory_space=pltpu.VMEM)],
        out_specs=[pl.BlockSpec(memory_space=pltpu.VMEM)] * 5,
        scratch_shapes=scratch,
        compiler_params=pltpu.CompilerParams(
            collective_id=2, has_side_effects=True, vmem_limit_bytes=58 * 2**20
        ),
        name="reduce_gradients",
    )(*partials, small)


Q_TILES = 9
O_AT, KV_AT, KV_WIDTH = 1792, 1152, 640
CHUNK = 512


def dot_nn(left, right):
    return jnp.dot(left, right, preferred_element_type=jnp.float32)


def dot_nt(left, right):
    return lax.dot_general(
        left, right, (((1,), (1,)), ((), ())), preferred_element_type=jnp.float32
    )


def span_of_device():
    seq = lax.axis_index("seq")
    rep = lax.axis_index("rep")
    z, x, y, core = seq // 2, seq % 2, rep // 2, rep % 2
    return z, (2 * x + y + x * (1 - 2 * y)) * 2 + core


def device_of_span(group, span):
    chip = span // 2
    x, y = chip // 2, (chip + 1) // 2 % 2
    return (group * 2 + x, y * 2 + span % 2)


def lanes(shape):
    return lax.broadcasted_iota(jnp.int32, shape, 1)


def rotated(value, cosine, sine):
    first = lanes(value.shape) % 64 < 32
    partner = jnp.where(first, pltpu.roll(value, 96, 1), pltpu.roll(value, 32, 1))
    return value * cosine + partner * sine


def block_kernel(*refs):
    (tokens, cotangent, meta, rope, turn, gains, places, wa_in, wg_in, wu_in, wd_in) = refs[:11]
    (output, input_grad, small, a_all, gqkv_all, o_all, gt_all, b_all, gg_all, gu_all, hidden_all, gf_all) = refs[11:23]
    (
        wa, wg, wu, wd, spread, o_spread, h_all, z_all, tf_all, gate_all, up_all, q_all, window,
        got, sending, depth_win, depth_at, bias_at, cos_at, sin_at, stats, o_at, dkv, grad, acc, gg_at, gu_at,
        load_sem, out_sem, kv_send, kv_recv, back_send, back_recv, depth_send, depth_recv,
    ) = refs[23:]
    narrow, wide = jnp.bfloat16, jnp.float32
    group, span = span_of_device()

    barrier = pltpu.get_barrier_semaphore()
    for away in (1, 2, 3):

        @pl.when(span + away < 8)
        def _():
            pl.semaphore_signal(
                barrier, inc=1, device_id=device_of_span(group, span + away), device_id_type=MESH
            )

        @pl.when(span - away >= 0)
        def _():
            pl.semaphore_signal(
                barrier, inc=1, device_id=device_of_span(group, span - away), device_id_type=MESH
            )

    loads = [
        pltpu.make_async_copy(src, dst, load_sem.at[i])
        for i, (src, dst) in enumerate(((wa_in, wa), (wg_in, wg), (wu_in, wu), (wd_in, wd)))
    ]
    for load in loads:
        load.start()

    depth_win[3] = jnp.broadcast_to(meta[0:1, :], (8, 128))
    for away in (1, 2, 3):

        @pl.when(span - away < 0)
        def _():
            depth_win[3 - away] = jnp.zeros((8, 128), wide)
            for recursion in range(RECUR):
                window[recursion, 3 - away] = jnp.zeros((128, KV_WIDTH), narrow)

    pl.semaphore_wait(barrier, 3 + span + span // 4 * (7 - 2 * span))

    def depth_copy(away, device):
        return remote(
            depth_win.at[3],
            depth_win.at[3 - away],
            depth_send.at[away - 1],
            depth_recv.at[away - 1],
            device,
        )

    def kv_copy(recursion, away, device):
        return remote(
            window.at[recursion, 3],
            window.at[recursion, 3 - away],
            kv_send.at[recursion, away - 1],
            kv_recv.at[recursion, away - 1],
            device,
        )

    def back_copy(recursion, away, device):
        return remote(
            sending.at[away - 1],
            got.at[recursion, away - 1],
            back_send.at[recursion, away - 1],
            back_recv.at[recursion, away - 1],
            device,
        )

    def stage_copies(recursion):
        return [
            pltpu.make_async_copy(gg_at, gg_all.at[recursion], out_sem.at[0]),
            pltpu.make_async_copy(gu_at, gu_all.at[recursion], out_sem.at[1]),
        ]

    def to_later(copy):
        for away in (1, 2, 3):

            @pl.when(span + away < 8)
            def _():
                copy(away, device_of_span(group, span + away)).start()

    def to_earlier(copy):
        for away in (1, 2, 3):

            @pl.when(span - away >= 0)
            def _():
                copy(away, device_of_span(group, span - away)).start()

    def wait_each(valid, waiting):
        for away in (1, 2, 3):

            @pl.when(valid(away))
            def _():
                waiting(away)

    def has_later(away):
        return span + away < 8

    def has_earlier(away):
        return span - away >= 0

    here = device_of_span(group, span)
    to_later(depth_copy)

    @pl.loop(0, MODEL_WIDTH // 64)
    def _(i):
        at = pl.multiple_of(i * 64, 64)
        rows = lax.broadcasted_iota(jnp.int32, (64, 1024), 0) + at
        spread[pl.ds(at, 64), :] = jnp.where(rows == places[0:1, :], 1.0, 0.0).astype(narrow)

    for tile in range(Q_TILES):
        at = lax.broadcasted_iota(jnp.int32, (128, 1024), 0)
        pair, part = tile // 3, tile % 3
        low, high = (6 * pair + part) * 64, (6 * pair + 3 + part) * 64 - 64
        if pair == 2:
            target = jnp.where(at < 64, -2, at + (12 + part) * 64 - 64)
        else:
            target = jnp.where(at < 64, at + low, at + high)
        o_spread[pl.ds(tile * 128, 128), :] = jnp.where(
            target == places[0:1, :], 1.0, 0.0
        ).astype(narrow)

    span_lane = meta[1:2, :]
    turn_cos = jnp.zeros((1, 128), wide)
    turn_sin = jnp.zeros((1, 128), wide)
    for k in range(4):
        turn_cos = turn_cos + jnp.where(span_lane == k, turn[k : k + 1, :], 0.0)
        turn_sin = turn_sin + jnp.where(span_lane == k, turn[8 + k : 9 + k, :], 0.0)
    cos_at[...] = turn_cos * rope[0] - turn_sin * rope[1]
    sign = jnp.where(lanes((128, 128)) % 64 < 32, -1.0, 1.0)
    sin_at[...] = sign * (turn_sin * rope[0] + turn_cos * rope[1])

    h_all[0] = dot_nn(tokens[...], spread[...])
    grad[...] = dot_nn(cotangent[...], spread[...])
    small[...] = jnp.zeros((8, 1024), wide)

    wait_each(has_earlier, lambda away: depth_copy(away, here).wait_recv())
    row = lax.broadcasted_iota(jnp.int32, (128, 128), 0)
    column = lanes((128, 128))
    ones = jnp.ones((128, 128), wide)
    for block in range(4):
        held = depth_win[block]
        depth_at[pl.ds(block * 128, 128), :] = dot_nn(
            jnp.where(row == column, jnp.broadcast_to(held[0:1, :], (128, 128)), 0.0), ones
        ).astype(narrow)

    def set_bias(recursion):
        level = recursion.astype(wide)
        for block in range(4):
            active = depth_at[pl.ds(block * 128, 128), :].astype(wide) > level
            if block == 3:
                allowed = (row == column) | (active & (row <= column))
            else:
                allowed = active & (span_lane >= 3 - block)
            bias_at[pl.ds(block * 128, 128), :] = jnp.where(allowed, 0.0, masked_score)

    def inverse_rms(value):
        return lax.rsqrt(
            jnp.sum(value * value, axis=-1, keepdims=True) / MODEL_WIDTH + epsilon
        )

    def active_column(recursion):
        own = depth_at[384:512, :].astype(wide)[:, 0:1]
        return jnp.where(own > recursion.astype(wide), 1.0, 0.0)

    def mixing_gate(recursion):
        logits = jnp.sum(
            h_all[recursion] * gains[pl.ds(2 + recursion, 1), :], axis=-1, keepdims=True
        )
        return jax.nn.sigmoid(logits)

    def halves(tile, pair, key_side):
        low = lanes(tile.shape) < 64
        zero = jnp.zeros_like(tile)
        if pair == 2:
            return jnp.where(low, tile, zero) if key_side else jnp.where(low, zero, tile)
        return jnp.concatenate([jnp.where(low, tile, zero), jnp.where(low, zero, tile)], axis=0)

    def key_tile(recursion, pair):
        parts = [window[recursion, b, :, pair * 128 : pair * 128 + 128] for b in range(4)]
        return jnp.concatenate(parts, axis=0)

    def value_tile(recursion, pair):
        at = 256 if pair == 2 else 384 + pair * 128
        parts = [window[recursion, b, :, at : at + 128] for b in range(4)]
        return jnp.concatenate(parts, axis=0)

    def biased(scores):
        bias = bias_at[...]
        if scores.shape[1] == 128:
            return scores + bias
        return scores + jnp.concatenate([bias, bias], axis=1)

    def joined(out, pair, key_side):
        if pair == 2:
            if key_side:
                out = jnp.where(row < 64, out, 0.0)
            return out.T
        return jnp.where(row < 64, out[:, :128], out[:, 128:]).T

    def attend(recursion):
        for pair in range(3):
            keys, values_t = key_tile(recursion, pair), value_tile(recursion, pair).T

            @pl.loop(0, 3)
            def _(part):
                at = pl.multiple_of((pair * 3 + part) * 128, 128)
                queries = halves(q_all[recursion, :, pl.ds(at, 128)], pair, True)
                scores = biased(dot_nt(keys, queries))
                top = jnp.max(scores, axis=0, keepdims=True)
                weight = jnp.exp(scores - top)
                inverse = 1.0 / jnp.sum(weight, axis=0, keepdims=True)
                width = scores.shape[1]
                stats[recursion, pair * 3 + part, 0:1, 0:width] = top
                stats[recursion, pair * 3 + part, 1:2, 0:width] = inverse
                out = dot_nn(values_t, (weight * inverse).astype(narrow))
                o_at[:, pl.ds(at, 128)] = joined(out, pair, False).astype(narrow)

    def attend_back(recursion):
        for pair in range(3):
            keys, values = key_tile(recursion, pair), value_tile(recursion, pair)
            keys_t = keys.T
            value_at = 256 if pair == 2 else 384 + pair * 128
            dkv[:, pair * 128 : pair * 128 + 128] = jnp.zeros((512, 128), wide)
            if pair < 2:
                dkv[:, value_at : value_at + 128] = jnp.zeros((512, 128), wide)

            @pl.loop(0, 3)
            def _(part):
                at = pl.multiple_of((pair * 3 + part) * 128, 128)
                queries = halves(q_all[recursion, :, pl.ds(at, 128)], pair, True)
                upstream = halves(o_at[:, pl.ds(at, 128)], pair, False)
                scores = biased(dot_nt(keys, queries))
                width = scores.shape[1]
                top = stats[recursion, pair * 3 + part, 0:1, 0:width]
                inverse = stats[recursion, pair * 3 + part, 1:2, 0:width]
                probs = jnp.exp(scores - top) * inverse
                grad_probs = dot_nt(values, upstream)
                inner = jnp.sum(probs * grad_probs, axis=0, keepdims=True)
                grad_scores = (probs * (grad_probs - inner)).astype(narrow)
                dkv[:, pair * 128 : pair * 128 + 128] += dot_nn(grad_scores, queries)
                dkv[:, value_at : value_at + 128] += dot_nn(probs.astype(narrow), upstream)
                out = dot_nn(keys_t, grad_scores)
                gqkv_all[recursion, :, pl.ds(at, 128)] = rotated(
                    joined(out, pair, True), cos_at[...] * 0.125, sin_at[...] * -0.125
                ).astype(narrow)

    def rotate_keys(value, sine):
        cosine = cos_at[...]
        low = lanes((128, 128)) < 64
        parts = []
        for tile in range(5):
            part = value[:, tile * 128 : tile * 128 + 128]
            if tile < 2:
                part = rotated(part, cosine, sine)
            elif tile == 2:
                part = jnp.where(low, rotated(part, cosine, sine), part)
            parts.append(part)
        return jnp.concatenate(parts, axis=1)

    @pl.loop(0, RECUR)
    def _(recursion):
        state = h_all[recursion]
        normal = state * inverse_rms(state)
        a_b = (normal * gains[0:1, :]).astype(narrow)
        a_all[recursion] = a_b

        @pl.when(recursion == 0)
        def _():
            loads[0].wait()

        pair_values = dot_nn(a_b, wa[:, KV_AT:O_AT])
        window[recursion, 3] = rotate_keys(pair_values, sin_at[...]).astype(narrow)
        to_later(lambda away, device: kv_copy(recursion, away, device))
        cosine, sine = cos_at[...] * 0.125, sin_at[...] * 0.125
        for first, width in ((0, 512), (512, 512), (1024, 128)):
            queries = dot_nn(a_all[recursion], wa[:, first : first + width])
            for at in range(0, width, 128):
                q_all[recursion, :, first + at : first + at + 128] = rotated(
                    queries[:, at : at + 128], cosine, sine
                ).astype(narrow)
        set_bias(recursion)
        wait_each(has_earlier, lambda away: kv_copy(recursion, away, here).wait_recv())
        attend(recursion)
        o_pad = dot_nn(o_at[...], o_spread[...]).astype(narrow)
        o_all[recursion] = o_pad
        branch = dot_nn(o_pad, wa[:, O_AT:])
        middle = h_all[recursion] + branch
        z_all[recursion] = middle
        b_b = (middle * inverse_rms(middle) * gains[1:2, :]).astype(narrow)
        b_all[recursion] = b_b
        acc[...] = branch

        @pl.when(recursion == 0)
        def _():
            for load in loads[1:]:
                load.wait()

        @pl.loop(0, FEEDFORWARD_UNITS // CHUNK)
        def _(j):
            at = pl.ds(pl.multiple_of(j * CHUNK, CHUNK), CHUNK)
            gate = dot_nn(b_all[recursion], wg[:, at])
            up = dot_nn(b_all[recursion], wu[:, at])
            gate_all[recursion, :, at] = gate
            up_all[recursion, :, at] = up
            hidden = (gate * jax.nn.sigmoid(gate) * up).astype(narrow)
            hidden_all[recursion, :, at] = hidden
            acc[...] += dot_nn(hidden, wd[at, :])

        tf_all[recursion] = acc[...]
        mixing = active_column(recursion) * mixing_gate(recursion)
        following = h_all[recursion] + mixing * acc[...]

        @pl.when(recursion < RECUR - 1)
        def _():
            h_all[recursion + 1] = following

        @pl.when(recursion == RECUR - 1)
        def _():
            output[...] = dot_nt(following.astype(narrow), spread[...]).astype(narrow)

    @pl.loop(0, RECUR)
    def _(i):
        recursion = RECUR - 1 - i
        router_row = gains[pl.ds(2 + recursion, 1), :]
        active, gate_value = active_column(recursion), mixing_gate(recursion)
        upstream = grad[...]
        grad_mix = jnp.sum(upstream * tf_all[recursion], axis=-1, keepdims=True)
        grad_logit = active * grad_mix * gate_value * (1.0 - gate_value)
        small[pl.ds(2 + recursion, 1), :] = jnp.sum(
            grad_logit * h_all[recursion], axis=0, keepdims=True
        )
        delta = (active * gate_value) * upstream
        gf_all[recursion] = delta.astype(narrow)
        grad[...] = upstream + grad_logit * router_row
        tf_all[recursion] = delta
        acc[...] = jnp.zeros((128, 1024), wide)

        @pl.when(recursion < RECUR - 1)
        def _():
            for copy in stage_copies(recursion + 1):
                copy.wait()

        @pl.loop(0, FEEDFORWARD_UNITS // CHUNK)
        def _(j):
            at = pl.ds(pl.multiple_of(j * CHUNK, CHUNK), CHUNK)
            grad_hidden = dot_nt(gf_all[recursion], wd[at, :])
            gate, up = gate_all[recursion, :, at], up_all[recursion, :, at]
            sigmoid = jax.nn.sigmoid(gate)
            grad_gate = (grad_hidden * up * sigmoid * (1.0 + gate * (1.0 - sigmoid))).astype(narrow)
            grad_up = (grad_hidden * gate * sigmoid).astype(narrow)
            gg_at[:, at] = grad_gate
            gu_at[:, at] = grad_up
            acc[...] += dot_nt(grad_gate, wg[:, at]) + dot_nt(grad_up, wu[:, at])

        for copy in stage_copies(recursion):
            copy.start()
        middle = z_all[recursion]
        inverse = inverse_rms(middle)
        normal = middle * inverse
        small[1:2, :] += jnp.sum(acc[...] * normal, axis=0, keepdims=True)
        scaled = acc[...] * gains[1:2, :]
        inner = jnp.sum(scaled * normal, axis=-1, keepdims=True) / MODEL_WIDTH
        grad_middle = inverse * (scaled - normal * inner)
        gt_b = (tf_all[recursion] + grad_middle).astype(narrow)
        gt_all[recursion] = gt_b
        grad[...] += grad_middle
        go_pad = dot_nt(gt_b, wa[:, O_AT:]).astype(narrow)
        o_at[...] = dot_nt(go_pad, o_spread[...]).astype(narrow)
        set_bias(recursion)
        attend_back(recursion)

        @pl.when(recursion < RECUR - 1)
        def _():
            wait_each(has_earlier, lambda away: back_copy(recursion + 1, away, here).wait_send())

        for away in (1, 2, 3):
            sending[away - 1] = dkv[
                (3 - away) * 128 : (4 - away) * 128, :
            ].astype(narrow)
        to_earlier(lambda away, device: back_copy(recursion, away, device))
        acc[...] = dot_nt(gqkv_all[recursion, :, :KV_AT], wa[:, :KV_AT])

        @pl.loop(1, 4)
        def _(away):
            @pl.when(span + away < 8)
            def _():
                back_copy(recursion, away, here).wait_recv()
                dkv[384:512, :] += got[recursion, away - 1].astype(wide)

        gqkv_all[recursion, :, KV_AT:] = rotate_keys(dkv[384:512, :], -sin_at[...]).astype(narrow)
        grad_normed = acc[...] + dot_nt(gqkv_all[recursion, :, KV_AT:], wa[:, KV_AT:O_AT])
        state = h_all[recursion]
        inverse = inverse_rms(state)
        normal = state * inverse
        small[0:1, :] += jnp.sum(grad_normed * normal, axis=0, keepdims=True)
        scaled = grad_normed * gains[0:1, :]
        inner = jnp.sum(scaled * normal, axis=-1, keepdims=True) / MODEL_WIDTH
        grad[...] += inverse * (scaled - normal * inner)

    for copy in stage_copies(0):
        copy.wait()
    total = grad[...]
    first = total.astype(narrow)
    rest = total - first.astype(wide)
    second = rest.astype(narrow)
    third = (rest - second.astype(wide)).astype(narrow)
    input_grad[...] = (
        dot_nt(first, spread[...]) + dot_nt(second, spread[...]) + dot_nt(third, spread[...])
    )

    wait_each(has_later, lambda away: depth_copy(away, here).wait_send())
    for recursion in range(RECUR):
        wait_each(has_later, lambda away: kv_copy(recursion, away, here).wait_send())
    wait_each(has_earlier, lambda away: back_copy(0, away, here).wait_send())


def run_block(tokens, cotangent, meta, gains, weights):
    narrow, wide, vmem, sems = jnp.bfloat16, jnp.float32, pltpu.VMEM, pltpu.SemaphoreType.DMA
    half = HEAD_SIZE // 2
    lane = np.arange(128) % half
    frequency = 10000.0 ** (-lane / half)
    angle = np.arange(128)[:, None] * frequency[None, :]
    rope = np.stack([np.cos(angle), np.sin(angle)]).astype(np.float32)
    jump = np.arange(4)[:, None] * 128.0 * frequency[None, :]
    turn = np.zeros((16, 128), np.float32)
    turn[:4], turn[8:12] = np.cos(jump), np.sin(jump)
    padded = np.arange(1024)
    natural = padded // PADDED_ROWS * OWN_ROWS + padded % PADDED_ROWS
    natural = np.where(padded % PADDED_ROWS < OWN_ROWS, natural, -1)
    places = np.broadcast_to(natural[None], (8, 1024)).astype(np.int32)
    outs = [((128, MODEL_WIDTH), narrow), ((128, MODEL_WIDTH), wide), ((8, 1024), wide)]
    outs += [
        ((RECUR, 128, width), narrow)
        for width in (1024, O_AT, 1024, 1024, 1024, 2560, 2560, 2560, 1024)
    ]
    scratch = [
        vmem((1024, 2816), narrow),
        vmem((1024, 2560), narrow),
        vmem((1024, 2560), narrow),
        vmem((2560, 1024), narrow),
        vmem((MODEL_WIDTH, 1024), narrow),
        vmem((KV_AT, 1024), narrow),
        vmem((RECUR, 128, 1024), wide),
        vmem((RECUR, 128, 1024), wide),
        vmem((RECUR, 128, 1024), wide),
        vmem((RECUR, 128, 2560), wide),
        vmem((RECUR, 128, 2560), wide),
        vmem((RECUR, 128, KV_AT), narrow),
        vmem((RECUR, 4, 128, KV_WIDTH), narrow),
        vmem((RECUR, 3, 128, KV_WIDTH), narrow),
        vmem((3, 128, KV_WIDTH), narrow),
        vmem((4, 8, 128), wide),
        vmem((512, 128), narrow),
        vmem((512, 128), wide),
        vmem((128, 128), wide),
        vmem((128, 128), wide),
        vmem((RECUR, Q_TILES, 2, 256), wide),
        vmem((128, KV_AT), narrow),
        vmem((512, KV_WIDTH), wide),
        vmem((128, 1024), wide),
        vmem((128, 1024), wide),
        vmem((128, 2560), narrow),
        vmem((128, 2560), narrow),
        sems((4,)),
        sems((2,)),
        sems((RECUR, 3)),
        sems((RECUR, 3)),
        sems((RECUR, 3)),
        sems((RECUR, 3)),
        sems((3,)),
        sems((3,)),
    ]
    here = pl.BlockSpec(memory_space=vmem)
    return pl.pallas_call(
        block_kernel,
        out_shape=[jax.ShapeDtypeStruct(shape, dtype) for shape, dtype in outs],
        in_specs=[here] * 7 + [pl.BlockSpec(memory_space=pl.ANY)] * 4,
        out_specs=[here] * 8 + [pl.BlockSpec(memory_space=pl.ANY)] * 2 + [here] * 2,
        scratch_shapes=scratch,
        compiler_params=pltpu.CompilerParams(
            collective_id=3, has_side_effects=True, vmem_limit_bytes=59 * 2**20
        ),
        name="run_block",
    )(tokens, cotangent, meta, rope, turn, gains, places, *weights)


HEAD_ORDER = (0, 3, 1, 4, 2, 5, 6, 9, 7, 10, 8, 11, 12, -1, 13, -1, 14, -1)


def moved(value, back=False):
    pairs = []
    for span in range(8):
        for group in range(4):
            seq, rep = device_of_span(group, span)
            pairs.append((span * 4 + group, seq * 4 + rep))
    if back:
        pairs = [(there, here) for here, there in pairs]
    return lax.ppermute(value, ("seq", "rep"), pairs)


def span_index(seq_spans):
    chain = lax.axis_size("seq")
    lengths = seq_spans[0]
    seq_ends = jnp.cumsum(lengths)
    own = lax.axis_index("seq")
    starts = seq_ends - lengths
    inside = (starts <= own) & (own < seq_ends)
    return own - jnp.sum(jnp.where(inside, starts, 0))


def per_device_fast(
    tokens,
    depths,
    seq_spans,
    cotangent,
    w_query,
    key_weight,
    value_weight,
    w_out,
    w_gate,
    w_up,
    w_down,
    attn_gain,
    ffn_gain,
    router,
):
    narrow, wide = jnp.bfloat16, jnp.float32
    natural = jnp.arange(MODEL_WIDTH, dtype=jnp.int32)
    padded_at = (natural // OWN_ROWS) * PADDED_ROWS + natural % OWN_ROWS
    spread = (padded_at[:, None] == jnp.arange(PADDED_WIDTH, dtype=jnp.int32)[None, :]).astype(narrow)
    packed = pack_weights(
        spread, w_query, key_weight, value_weight, w_out, w_gate, w_up, w_down
    )
    weights = gather_weights(packed)
    gains = jnp.concatenate([attn_gain[None], ffn_gain[None], router], axis=0)
    gains = jnp.pad(
        gains.reshape(5, 32, OWN_ROWS), ((0, 3), (0, 0), (0, PADDED_ROWS - OWN_ROWS))
    ).reshape(8, PADDED_WIDTH)
    index = span_index(seq_spans)
    meta = jnp.concatenate(
        [
            depths.astype(wide),
            jnp.broadcast_to(index.astype(wide), (1, 128)),
            jnp.zeros((6, 128), wide),
        ],
        axis=0,
    )
    (
        output,
        input_grad,
        small,
        a_all,
        qkv_all,
        o_all,
        t_all,
        b_all,
        gate_all,
        up_all,
        hidden_all,
        f_all,
    ) = run_block(moved(tokens[0]), moved(cotangent[0]), moved(meta), gains, weights)

    def contracted(left, right):
        return left_product(
            left.reshape(RECUR * 128, -1), right.reshape(RECUR * 128, -1)
        ).astype(narrow)

    partials = (
        jnp.concatenate([contracted(a_all, qkv_all), contracted(o_all, t_all)], axis=1),
        contracted(b_all, gate_all),
        contracted(b_all, up_all),
        contracted(hidden_all, f_all),
    )
    attention_sum, gate_sum, up_sum, down_sum, small_sum = reduce_gradients(partials, small)

    def gather_columns(x):
        return x.reshape(x.shape[0], 32, PADDED_ROWS)[:, :, :OWN_ROWS].reshape(x.shape[0], MODEL_WIDTH)

    small_natural = gather_columns(small_sum)
    own = attention_sum[:OWN_ROWS]
    heads = own[:, :KV_AT].reshape(OWN_ROWS, 18, HEAD_SIZE)
    d_query = jnp.stack([heads[:, HEAD_ORDER.index(head)] for head in range(QUERY_HEADS)], axis=1)
    d_value = jnp.concatenate([own[:, 1536:1792], own[:, 1472:1536]], axis=1)
    return (
        moved(output, True)[None],
        moved(input_grad, True)[None],
        d_query.reshape(-1),
        own[:, 1152:1472].reshape(-1),
        d_value.reshape(-1),
        gather_columns(own[:, O_AT:]).reshape(-1),
        gate_sum[:OWN_ROWS].reshape(-1),
        up_sum[:OWN_ROWS].reshape(-1),
        gather_columns(down_sum).reshape(-1),
        small_natural[0],
        small_natural[1],
        small_natural[2:5],
    )


def pack_weights(spread, w_query, key_weight, value_weight, w_out, w_gate, w_up, w_down):
    narrow = jnp.bfloat16

    def rows(flat):
        return flat.astype(narrow).reshape(OWN_ROWS, -1)

    heads = rows(w_query).reshape(OWN_ROWS, QUERY_HEADS, HEAD_SIZE)
    empty = jnp.zeros((OWN_ROWS, HEAD_SIZE), narrow)
    queries = [heads[:, head] if head >= 0 else empty for head in HEAD_ORDER]
    values = rows(value_weight)
    attention = jnp.concatenate(
        queries
        + [
            rows(key_weight),
            values[:, 256:],
            values[:, :256],
            unscaled_product(rows(w_out), spread).astype(narrow),
        ],
        axis=1,
    )
    extra = ((0, PADDED_ROWS - OWN_ROWS), (0, 0))
    return (
        jnp.pad(attention, extra),
        jnp.pad(rows(w_gate), extra),
        jnp.pad(rows(w_up), extra),
        unscaled_product(w_down.astype(narrow).reshape(-1, MODEL_WIDTH), spread).astype(narrow),
    )


def solution(mesh):
    fits = mesh.shape["seq"] == 8 and mesh.shape["rep"] == 4
    placed = (
        P("rep", "seq", None),
        P("rep", "seq"),
        P("rep", None),
        P("rep", "seq", None),
        P(("seq", "rep")),
        P(("seq", "rep")),
        P(("seq", "rep")),
        P(("seq", "rep")),
        P(("seq", "rep")),
        P(("seq", "rep")),
        P(("seq", "rep")),
        P(),
        P(),
        P(),
    )
    return jax.shard_map(
        per_device_fast if fits else per_device,
        mesh=mesh,
        in_specs=placed,
        out_specs=(
            P("rep", "seq", None),
            P("rep", "seq", None),
            P(("seq", "rep")),
            P(("seq", "rep")),
            P(("seq", "rep")),
            P(("seq", "rep")),
            P(("seq", "rep")),
            P(("seq", "rep")),
            P(("seq", "rep")),
            P(),
            P(),
            P(),
        ),
        check_vma=False,
    )
```

```python
import jax
import jax.numpy as jnp
import numpy as np
from jax import lax
from jax.experimental import pallas as pl
from jax.experimental.pallas import tpu as pltpu
from jax.sharding import PartitionSpec as P

MODEL_WIDTH = 960
QUERY_HEADS = 15
KEY_VALUE_HEADS = 5
HEAD_SIZE = 64
FEEDFORWARD_UNITS = 2560
LOGC = 5
RECUR = 3
OWN_ROWS = 30
PADDED_ROWS = 32
PADDED_WIDTH = 1024


highest = lax.Precision.HIGHEST
epsilon = 1e-06
masked_score = -1e30


def passed_along(value, axis, steps):
    count = lax.axis_size(axis)
    initial, last = (max(0, -steps), min(count, count - steps))
    return lax.ppermute(value, axis, [(source, source + steps) for source in range(initial, last)])


def for_sending(x):

    def short(part):
        return part.astype(jnp.bfloat16) if part.dtype == jnp.float32 else part

    return jax.tree.map(short, x)


def unscaled_product(left, right):
    return jnp.dot(left, right, preferred_element_type=jnp.float32)


def left_product(left, right):
    return lax.dot_general(
        left, right, (((0,), (0,)), ((), ())), preferred_element_type=jnp.float32
    )


def right_product(left, right):
    return lax.dot_general(
        left, right, (((1,), (1,)), ((), ())), preferred_element_type=jnp.float32
    )


def rms_parts(vectors, gain):
    inv_rms = lax.rsqrt(jnp.mean(vectors * vectors, axis=-1, keepdims=True) + epsilon)
    normal_part = vectors * inv_rms
    return (normal_part * gain, normal_part, inv_rms)


def rms_backward(upstream, normal_part, inv_rms, gain):
    gain_grad = jnp.sum(upstream * normal_part, axis=0)
    scaled = upstream * gain
    inner = jnp.mean(scaled * normal_part, axis=-1, keepdims=True)
    return (inv_rms * (scaled - normal_part * inner), gain_grad)


def angle_tables(positions, width):
    half_width = width // 2
    frequency = 10000.0 ** (-jnp.arange(half_width, dtype=jnp.float32) / half_width)
    angle_grid = positions[:, None] * frequency[None, :]
    return (jnp.cos(angle_grid)[:, None, :], jnp.sin(angle_grid)[:, None, :])


def apply_rotation(vectors, cosine_table, sine_table):
    half_width = vectors.shape[-1] // 2
    front_half = vectors[..., :half_width]
    back_half = vectors[..., half_width:]
    return jnp.concatenate(
        [
            front_half * cosine_table - back_half * sine_table,
            back_half * cosine_table + front_half * sine_table,
        ],
        axis=-1,
    )


def masked_scores(query_b, keys_win, allowed):
    scores = (
        jnp.einsum("qgjd,kgd->gjqk", query_b, keys_win, preferred_element_type=jnp.float32) * 0.125
    )
    return jnp.where(allowed[None, None], scores, masked_score)


def per_device(
    tokens,
    depths,
    seq_spans,
    cotangent,
    w_query,
    key_weight,
    value_weight,
    w_out,
    w_gate,
    w_up,
    w_down,
    attn_gain,
    ffn_gain,
    router,
):
    narrow_float_type = jnp.bfloat16
    wide_float_type = jnp.float32
    count_of_rows = tokens.shape[1]
    query_groupings = QUERY_HEADS // KEY_VALUE_HEADS
    chain = lax.axis_size("seq")
    most_spans = min(2**LOGC, chain // 2)
    depth_levels = (most_spans - 1).bit_length()
    extra_rows = ((1 << depth_levels) - most_spans) * count_of_rows
    window = most_spans * count_of_rows
    target_tokens = (
        (MODEL_WIDTH, QUERY_HEADS * HEAD_SIZE),
        (MODEL_WIDTH, KEY_VALUE_HEADS * HEAD_SIZE),
        (MODEL_WIDTH, KEY_VALUE_HEADS * HEAD_SIZE),
        (QUERY_HEADS * HEAD_SIZE, MODEL_WIDTH),
        (MODEL_WIDTH, FEEDFORWARD_UNITS),
        (MODEL_WIDTH, FEEDFORWARD_UNITS),
        (FEEDFORWARD_UNITS, MODEL_WIDTH),
    )
    fetched = (
        lax.all_gather(w_query.astype(narrow_float_type), ("seq", "rep"), axis=0, tiled=True),
        lax.all_gather(key_weight.astype(narrow_float_type), ("seq", "rep"), axis=0, tiled=True),
        lax.all_gather(value_weight.astype(narrow_float_type), ("seq", "rep"), axis=0, tiled=True),
        lax.all_gather(w_out.astype(narrow_float_type), ("seq", "rep"), axis=0, tiled=True),
        lax.all_gather(w_gate.astype(narrow_float_type), ("seq", "rep"), axis=0, tiled=True),
        lax.all_gather(w_up.astype(narrow_float_type), ("seq", "rep"), axis=0, tiled=True),
        lax.all_gather(w_down.astype(narrow_float_type), ("seq", "rep"), axis=0, tiled=True),
    )
    attention_weights = tuple(
        (gathered.reshape(target) for gathered, target in zip(fetched, target_tokens))
    )
    place = lax.axis_index("seq")
    lengths = seq_spans[0]
    seq_ends = jnp.cumsum(lengths)
    span_ids = jnp.arange(chain, dtype=jnp.int32)
    owners = jnp.sum((seq_ends[None, :] <= span_ids[:, None]).astype(jnp.int32), axis=1)
    seq_starts = seq_ends - lengths
    numbers = jnp.arange(lengths.shape[0], dtype=jnp.int32)
    first_span = jnp.sum(
        jnp.where(numbers[None, :] == owners[:, None], seq_starts[None, :], 0), axis=1
    )
    index_of_span = jnp.sum(jnp.where(span_ids == place, span_ids - first_span, 0))
    positions = (index_of_span * count_of_rows + jnp.arange(count_of_rows, dtype=jnp.int32)).astype(
        wide_float_type
    )
    cosine_table, sine_table = angle_tables(positions, HEAD_SIZE)
    row_ids = jnp.arange(count_of_rows, dtype=jnp.int32)
    col_ids = jnp.arange(window, dtype=jnp.int32)
    offsets = most_spans - 1 - col_ids // count_of_rows
    local_col = col_ids - (most_spans - 1) * count_of_rows
    causal = jnp.where(offsets[None, :] == 0, local_col[None, :] <= row_ids[:, None], True)
    diagonal = (offsets[None, :] == 0) & (local_col[None, :] == row_ids[:, None])
    span_ok = (index_of_span >= offsets)[None, :]
    active_all = (depths[0][None, :] > jnp.arange(RECUR, dtype=jnp.int32)[:, None]).astype(
        wide_float_type
    )
    hidden_state = tokens[0].astype(wide_float_type)
    saved = []
    for recursion in range(RECUR):
        current_active = active_all[recursion]
        normalized_input, normal_a, inv_a = rms_parts(hidden_state, attn_gain)
        normalized_input_copy = normalized_input.astype(narrow_float_type)
        raw_query = unscaled_product(normalized_input_copy, attention_weights[0]).reshape(
            count_of_rows, QUERY_HEADS, HEAD_SIZE
        )
        query_b = (
            apply_rotation(raw_query, cosine_table, sine_table)
            .astype(narrow_float_type)
            .reshape(count_of_rows, KEY_VALUE_HEADS, query_groupings, HEAD_SIZE)
        )
        unrotated_key = unscaled_product(normalized_input_copy, attention_weights[1]).reshape(
            count_of_rows, KEY_VALUE_HEADS, HEAD_SIZE
        )
        key_b = apply_rotation(unrotated_key, cosine_table, sine_table).astype(narrow_float_type)
        value_copy = (
            unscaled_product(normalized_input_copy, attention_weights[2])
            .astype(narrow_float_type)
            .reshape(count_of_rows, KEY_VALUE_HEADS, HEAD_SIZE)
        )
        active_b = current_active.astype(narrow_float_type)
        keys_win = key_b
        values_win = value_copy
        active_win = active_b
        for level in range(depth_levels):
            far_key, far_value, far_active = passed_along(
                (keys_win, values_win, active_win), "seq", 1 << level
            )
            keys_win = jnp.concatenate([far_key, keys_win], axis=0)
            values_win = jnp.concatenate([far_value, values_win], axis=0)
            active_win = jnp.concatenate([far_active, active_win], axis=0)
        allowed = span_ok & causal & ((active_win > 0)[None, :] | diagonal)
        scores = masked_scores(query_b, keys_win, allowed)
        row_max = jnp.max(scores, axis=-1, keepdims=True)
        expon = jnp.exp(scores - row_max)
        row_total = jnp.sum(expon, axis=-1, keepdims=True)
        probs_b = (expon / row_total).astype(narrow_float_type)
        log_total = row_max + jnp.log(row_total)
        attended_b = (
            jnp.einsum(
                "gjqk,kgd->qgjd", probs_b, values_win, preferred_element_type=wide_float_type
            )
            .astype(narrow_float_type)
            .reshape(count_of_rows, QUERY_HEADS * HEAD_SIZE)
        )
        branch = unscaled_product(attended_b, attention_weights[3])
        middle = hidden_state + branch
        second, normal_z, inv_z = rms_parts(middle, ffn_gain)
        second_b = second.astype(narrow_float_type)
        gate_value = unscaled_product(second_b, attention_weights[4])
        up_value = unscaled_product(second_b, attention_weights[5])
        hidden_b = (jax.nn.silu(gate_value) * up_value).astype(narrow_float_type)
        ffn_out = unscaled_product(hidden_b, attention_weights[6])
        weight_gate = jax.nn.sigmoid(jnp.dot(hidden_state, router[recursion], precision=highest))
        saved.append(
            (
                hidden_state,
                normalized_input_copy,
                normal_a,
                inv_a,
                query_b,
                keys_win,
                values_win,
                allowed,
                log_total,
                attended_b,
                branch,
                normal_z,
                inv_z,
                second_b,
                gate_value,
                up_value,
                hidden_b,
                ffn_out,
                weight_gate,
                current_active,
            )
        )
        hidden_state = hidden_state + (current_active * weight_gate)[:, None] * (branch + ffn_out)
    output = hidden_state.astype(narrow_float_type)
    refetched = (
        lax.all_gather(w_query.astype(narrow_float_type), ("seq", "rep"), axis=0, tiled=True),
        lax.all_gather(key_weight.astype(narrow_float_type), ("seq", "rep"), axis=0, tiled=True),
        lax.all_gather(value_weight.astype(narrow_float_type), ("seq", "rep"), axis=0, tiled=True),
        lax.all_gather(w_out.astype(narrow_float_type), ("seq", "rep"), axis=0, tiled=True),
        lax.all_gather(w_gate.astype(narrow_float_type), ("seq", "rep"), axis=0, tiled=True),
        lax.all_gather(w_up.astype(narrow_float_type), ("seq", "rep"), axis=0, tiled=True),
        lax.all_gather(w_down.astype(narrow_float_type), ("seq", "rep"), axis=0, tiled=True),
    )
    back_weights = tuple(
        (gathered.reshape(target) for gathered, target in zip(refetched, target_tokens))
    )
    master_shapes = (w_query, key_weight, value_weight, w_out, w_gate, w_up, w_down)
    shares = tuple((jnp.zeros_like(master) for master in master_shapes))
    gain_a_total = jnp.zeros((MODEL_WIDTH,), wide_float_type)
    gain_f_total = jnp.zeros((MODEL_WIDTH,), wide_float_type)
    router_rows = [None] * RECUR
    grad_state = cotangent[0].astype(wide_float_type)
    for recursion in reversed(range(RECUR)):
        (
            state_in,
            normalized_input_copy,
            normal_a,
            inv_a,
            query_b,
            keys_win,
            values_win,
            allowed,
            log_total,
            attended_b,
            branch,
            normal_z,
            inv_z,
            second_b,
            gate_value,
            up_value,
            hidden_b,
            ffn_out,
            weight_gate,
            current_active,
        ) = saved[recursion]
        mixing = current_active * weight_gate
        grad_delta = mixing[:, None] * grad_state
        grad_mix = jnp.sum(grad_state * (branch + ffn_out), axis=-1)
        grad_logit = current_active * grad_mix * weight_gate * (1.0 - weight_gate)
        router_rows[recursion] = jnp.dot(grad_logit, state_in, precision=highest)
        grad_next = grad_state + grad_logit[:, None] * router[recursion][None, :]
        ffn_grad_b = grad_delta.astype(narrow_float_type)
        grad_hidden = right_product(ffn_grad_b, back_weights[6])
        d_down = left_product(hidden_b, ffn_grad_b)
        sigmoid_gate = jax.nn.sigmoid(gate_value)
        grad_gate_b = (
            grad_hidden * up_value * sigmoid_gate * (1.0 + gate_value * (1.0 - sigmoid_gate))
        ).astype(narrow_float_type)
        grad_up_b = (grad_hidden * gate_value * sigmoid_gate).astype(narrow_float_type)
        grad_second = right_product(grad_gate_b, back_weights[4]) + right_product(
            grad_up_b, back_weights[5]
        )
        d_gate = left_product(second_b, grad_gate_b)
        d_up = left_product(second_b, grad_up_b)
        grad_middle, gain_f_part = rms_backward(grad_second, normal_z, inv_z, ffn_gain)
        gain_f_total = gain_f_total + gain_f_part
        grad_branch_b = (grad_delta + grad_middle).astype(narrow_float_type)
        grad_attended_b = (
            right_product(grad_branch_b, back_weights[3])
            .astype(narrow_float_type)
            .reshape(count_of_rows, KEY_VALUE_HEADS, query_groupings, HEAD_SIZE)
        )
        d_out = left_product(attended_b, grad_branch_b)
        grad_next = grad_next + grad_middle
        scores = masked_scores(query_b, keys_win, allowed)
        probs = jnp.exp(scores - log_total)
        probs_b = probs.astype(narrow_float_type)
        grad_probs = jnp.einsum(
            "qgjd,kgd->gjqk", grad_attended_b, values_win, preferred_element_type=wide_float_type
        )
        row_dot = jnp.sum(probs * grad_probs, axis=-1, keepdims=True)
        grad_scores_b = (probs * (grad_probs - row_dot)).astype(narrow_float_type)
        grad_queries = (
            jnp.einsum(
                "gjqk,kgd->qgjd", grad_scores_b, keys_win, preferred_element_type=wide_float_type
            )
            * 0.125
        )
        grad_keys = (
            jnp.einsum(
                "gjqk,qgjd->kgd", grad_scores_b, query_b, preferred_element_type=wide_float_type
            )
            * 0.125
        )
        grad_values = jnp.einsum(
            "gjqk,qgjd->kgd", probs_b, grad_attended_b, preferred_element_type=wide_float_type
        )
        extra_zero_rows = jnp.zeros((extra_rows, KEY_VALUE_HEADS, HEAD_SIZE), wide_float_type)
        local_span_keys = jnp.concatenate([extra_zero_rows, grad_keys], axis=0)
        local_span_values = jnp.concatenate([extra_zero_rows, grad_values], axis=0)
        for level in reversed(range(depth_levels)):
            older_rows = (1 << level) * count_of_rows
            back_keys, back_values = passed_along(
                (
                    for_sending(local_span_keys[:older_rows]),
                    for_sending(local_span_values[:older_rows]),
                ),
                "seq",
                -(1 << level),
            )
            local_span_keys = local_span_keys[older_rows:] + back_keys
            local_span_values = local_span_values[older_rows:] + back_values
        grad_query_b = (
            apply_rotation(
                grad_queries.reshape(count_of_rows, QUERY_HEADS, HEAD_SIZE),
                cosine_table,
                -sine_table,
            )
            .astype(narrow_float_type)
            .reshape(count_of_rows, QUERY_HEADS * HEAD_SIZE)
        )
        grad_key_b = (
            apply_rotation(local_span_keys, cosine_table, -sine_table)
            .astype(narrow_float_type)
            .reshape(count_of_rows, KEY_VALUE_HEADS * HEAD_SIZE)
        )
        value_gradient_copy = local_span_values.astype(narrow_float_type).reshape(
            count_of_rows, KEY_VALUE_HEADS * HEAD_SIZE
        )
        grad_normed = (
            right_product(grad_query_b, back_weights[0])
            + right_product(grad_key_b, back_weights[1])
            + right_product(value_gradient_copy, back_weights[2])
        )
        d_query = left_product(normalized_input_copy, grad_query_b)
        d_key = left_product(normalized_input_copy, grad_key_b)
        d_value = left_product(normalized_input_copy, value_gradient_copy)
        grad_input, gain_a_part = rms_backward(grad_normed, normal_a, inv_a, attn_gain)
        gain_a_total = gain_a_total + gain_a_part
        grad_state = grad_next + grad_input
        local_grads = (
            d_query.reshape(-1),
            d_key.reshape(-1),
            d_value.reshape(-1),
            d_out.reshape(-1),
            d_gate.reshape(-1),
            d_up.reshape(-1),
            d_down.reshape(-1),
        )
        summed = (
            lax.psum_scatter(local_grads[0], ("seq", "rep"), scatter_dimension=0, tiled=True),
            lax.psum_scatter(local_grads[1], ("seq", "rep"), scatter_dimension=0, tiled=True),
            lax.psum_scatter(local_grads[2], ("seq", "rep"), scatter_dimension=0, tiled=True),
            lax.psum_scatter(local_grads[3], ("seq", "rep"), scatter_dimension=0, tiled=True),
            lax.psum_scatter(local_grads[4], ("seq", "rep"), scatter_dimension=0, tiled=True),
            lax.psum_scatter(local_grads[5], ("seq", "rep"), scatter_dimension=0, tiled=True),
            lax.psum_scatter(local_grads[6], ("seq", "rep"), scatter_dimension=0, tiled=True),
        )
        shares = tuple((old_share + new_share for old_share, new_share in zip(shares, summed)))
    router_grad = jnp.stack(router_rows, axis=0)
    gain_a_sum, gain_f_sum, router_sum = lax.psum(
        (gain_a_total, gain_f_total, router_grad), ("seq", "rep")
    )
    return (
        output[None],
        grad_state[None],
        shares[0],
        shares[1],
        shares[2],
        shares[3],
        shares[4],
        shares[5],
        shares[6],
        gain_a_sum,
        gain_f_sum,
        router_sum,
    )


MESH = pl.DeviceIdType.MESH
N_Z = 4
BLOCKS = ((32, 2816), (32, 2560), (32, 2560), (80, 1024))
GATHER_ORDERS = ("uzw", "zuw", "uzw", "zuw")
REDUCE_ORDERS = ("uzw", "zuw", "uzw", "zuw")


def place():
    seq = lax.axis_index("seq")
    rep = lax.axis_index("rep")
    z, x, y, core = seq // 2, seq % 2, rep // 2, rep % 2
    return z, x + core * (y - x), y + core * (x - y), core


def device_of(z, u, w, core):
    x, y = u + core * (w - u), w + core * (u - w)
    return (z * 2 + x, y * 2 + core)


def block_of(z, u, w, core):
    seq, rep = device_of(z, u, w, core)
    return seq * 4 + rep


def remote(src, dst, send_sem, recv_sem, device):
    return pltpu.make_async_remote_copy(
        src_ref=src,
        dst_ref=dst,
        send_sem=send_sem,
        recv_sem=recv_sem,
        device_id=device,
        device_id_type=MESH,
    )


def gather_events():
    events = [("own", group) for group in range(4)]
    for step in range(6):
        for group in range(4):
            if GATHER_ORDERS[group] == "zuw":
                if 1 <= step <= 3:
                    events.append(("z", group, step, 0))
                if 1 <= step <= 4:
                    events.append(("u", group, step - 1))
                    events.append(("w", group, step - 1, 0))
                if 2 <= step <= 5:
                    events.append(("w", group, step - 2, 1))
            else:
                if step == 1:
                    events.append(("first", group))
                if 1 <= step <= 3:
                    events.append(("z", group, step, 0))
                if 2 <= step <= 4:
                    events.append(("z", group, step - 1, 1))
                if 1 <= step <= 4:
                    events.append(("w", group, step - 1, 0))
                if 2 <= step <= 5:
                    events.append(("w", group, step - 2, 1))
    return events


def move_partners():
    seq, rep = lax.axis_index("seq"), lax.axis_index("rep")
    return device_of_span(rep, seq), span_of_device()[::-1], (seq * 4 + rep + 31) // 32


def start_moves(leaving, arriving, send_sem, recv_sem, target, moves):
    for i, (src, dst) in enumerate(zip(leaving, arriving)):

        @pl.when(moves == 1)
        def _():
            remote(src, dst, send_sem.at[i], recv_sem.at[i], target).start()

        @pl.when(moves == 0)
        def _():
            pltpu.make_async_copy(src, dst, recv_sem.at[i]).start()


def wait_moves(leaving, arriving, send_sem, recv_sem, target, moves):
    for i, (src, dst) in enumerate(zip(leaving, arriving)):

        @pl.when(moves == 1)
        def _():
            remote(src, dst, send_sem.at[i], recv_sem.at[i], target).wait()

        @pl.when(moves == 0)
        def _():
            pltpu.make_async_copy(src, dst, recv_sem.at[i]).wait()


def set_meta(meta, depths, spans):
    own = lax.axis_index("seq")
    first, end = 0, 0
    for sequence in range(spans.shape[1]):
        end = end + spans[0, sequence]
        first = jnp.where(end <= own, end, first)
    row = lax.broadcasted_iota(jnp.int32, (8, 128), 0)
    values = jnp.where(row == 0, depths[...], jnp.where(row == 1, own - first, 0))
    meta[...] = values.astype(jnp.float32)


def gather_kernel(*refs):
    flat_in, tokens, depths, spans, places = refs[:7], refs[7], refs[8], refs[9], refs[10]
    full, arriving = refs[11:15], refs[15:17]
    flat, own, meta = refs[17:24], refs[24:28], refs[28]
    spread, tiles, natural, long_rows = refs[29:33]
    recv_sem, z_sem, u_sem, w_sem, core_sem, local_sem, move_send, move_recv, flat_sem = refs[33:]
    leaving = (tokens, meta)
    z, u, w, core = place()
    me = block_of(z, u, w, core)
    target, source, moves = move_partners()
    above, below = device_of(z + 1, u, w, core), device_of(z - 1, u, w, core)
    across_u, across_w = device_of(z, 1 - u, w, core), device_of(z, u, 1 - w, core)
    sibling = device_of(z, w, u, 1 - core)

    loads = [
        pltpu.make_async_copy(src, dst, flat_sem.at[i])
        for i, (src, dst) in enumerate(zip(flat_in, flat))
    ]
    for copy in loads:
        copy.start()
    barrier = pltpu.get_barrier_semaphore()
    for device in (across_u, across_w, sibling):
        pl.semaphore_signal(barrier, inc=1, device_id=device, device_id_type=MESH)

    @pl.when(moves == 1)
    def _():
        pl.semaphore_signal(barrier, inc=1, device_id=target, device_id_type=MESH)
        pl.semaphore_signal(barrier, inc=1, device_id=source, device_id_type=MESH)

    @pl.when(z < N_Z - 1)
    def _():
        pl.semaphore_signal(barrier, inc=1, device_id=above, device_id_type=MESH)

    @pl.when(z > 0)
    def _():
        pl.semaphore_signal(barrier, inc=1, device_id=below, device_id_type=MESH)

    fill_spread(spread, places)
    set_meta(meta, depths, spans)
    for copy in loads:
        copy.wait()
    pack_own(flat, own, spread, places, tiles, natural, long_rows)
    pl.semaphore_wait(barrier, 4 + (z + 1) // 2 - z // 3 * 2 + 2 * moves)

    def rows(group, block):
        count = BLOCKS[group][0]
        return full[group].at[pl.ds(pl.multiple_of(block * count, 16), count)]

    def copy(group, block, src, send_sem, device):
        return remote(src, rows(group, block), send_sem, recv_sem.at[group, block], device)

    def send(group, block, src, ways, slot=0):
        if "z" in ways:

            @pl.when(z < N_Z - 1)
            def _():
                copy(group, block, src, z_sem.at[group, 0, slot], above).start()

            @pl.when(z > 0)
            def _():
                copy(group, block, src, z_sem.at[group, 1, slot], below).start()

        if "+" in ways:

            @pl.when(z < N_Z - 1)
            def _():
                copy(group, block, src, z_sem.at[group, 0, slot], above).start()

        if "-" in ways:

            @pl.when(z > 0)
            def _():
                copy(group, block, src, z_sem.at[group, 1, slot], below).start()

        if "u" in ways:
            copy(group, block, src, u_sem.at[group], across_u).start()
        if "w" in ways:
            copy(group, block, src, w_sem.at[group], across_w).start()
        if "c" in ways:
            copy(group, block, src, core_sem.at[group], sibling).start()

    def passed_on(group, block, ways, slot=0):
        copy(group, block, rows(group, block), core_sem.at[group], sibling).wait_recv()
        send(group, block, rows(group, block), ways, slot)

    def at_distance(step, action):
        if step == 0:
            action(z, "")
            return

        @pl.when(z - step >= 0)
        def _():
            action(z - step, "+")

        @pl.when(z + step < N_Z)
        def _():
            action(z + step, "-")

    def own_event(group):
        send(group, me, own[group], "zuwc")
        pltpu.make_async_copy(own[group], rows(group, me), local_sem.at[group]).start()

    def first_event(group):
        passed_on(group, block_of(z, 1 - u, w, core), "zwc", 1)

    def z_event(group, step, other):
        z_first = GATHER_ORDERS[group] == "zuw"
        column = 1 - u if other else u
        slot = step if z_first else 2 * step + other
        at_distance(
            step,
            lambda far, way: passed_on(
                group,
                block_of(far, column, w, core),
                way + ("uwc" if z_first else "wc"),
                slot,
            ),
        )

    def u_event(group, step):
        at_distance(
            step, lambda far, way: passed_on(group, block_of(far, 1 - u, w, core), "wc")
        )

    def w_event(group, step, other):
        column = 1 - u if other else u
        at_distance(
            step, lambda far, way: passed_on(group, block_of(far, column, 1 - w, core), "c")
        )

    actions = {"own": own_event, "first": first_event, "z": z_event, "u": u_event, "w": w_event}
    for event in gather_events():
        if event == ("z", 0, 1, 0):
            start_moves(leaving, arriving, move_send, move_recv, target, moves)
        actions[event[0]](*event[1:])
    wait_moves(leaving, arriving, move_send, move_recv, target, moves)

    for group in range(4):
        z_first = GATHER_ORDERS[group] == "zuw"
        count = BLOCKS[group][0]
        pltpu.make_async_copy(own[group], rows(group, me), local_sem.at[group]).wait()

        @pl.loop(0, 16)
        def _(i):
            block = i * 2 + (1 - core)
            copy(group, block, rows(group, block), core_sem.at[group], sibling).wait_recv()

        for sem, sends in ((u_sem, 4 if z_first else 1), (w_sem, 8), (core_sem, 16)):
            part = full[group].at[pl.ds(0, sends * count)]
            remote(part, part, sem.at[group], recv_sem.at[group, 0], sibling).wait_send()
        for step in range(N_Z):
            for other in (0,) if z_first else (0, 1):
                slot = step if z_first else 2 * step + other

                @pl.when((z - step >= 0) & (z < N_Z - 1))
                def _():
                    copy(group, me, own[group], z_sem.at[group, 0, slot], above).wait_send()

                @pl.when((z + step < N_Z) & (z > 0))
                def _():
                    copy(group, me, own[group], z_sem.at[group, 1, slot], below).wait_send()


def gather_weights(flat, tokens, depths, spans):
    narrow, wide, vmem, sems = jnp.bfloat16, jnp.float32, pltpu.VMEM, pltpu.SemaphoreType.DMA
    anywhere, here = pl.BlockSpec(memory_space=pl.ANY), pl.BlockSpec(memory_space=vmem)
    flat = [x.reshape(-1, 128) for x in flat]
    return pl.pallas_call(
        gather_kernel,
        out_shape=[jax.ShapeDtypeStruct((32 * rows, columns), narrow) for rows, columns in BLOCKS]
        + [jax.ShapeDtypeStruct(tokens.shape, narrow), jax.ShapeDtypeStruct((8, 128), wide)],
        in_specs=[anywhere] * 8 + [here, pl.BlockSpec(memory_space=pltpu.SMEM), here],
        out_specs=[anywhere] * 6,
        scratch_shapes=[vmem(x.shape, wide) for x in flat]
        + [vmem(shape, narrow) for shape in BLOCKS]
        + [
            vmem((8, 128), wide),
            vmem((MODEL_WIDTH, 1024), narrow),
            vmem((20, 32, 128), wide),
            vmem((8, 32, 128), wide),
            vmem((8, 80, 128), wide),
            sems((4, 32)),
            sems((4, 2, 8)),
            sems((4,)),
            sems((4,)),
            sems((4,)),
            sems((4,)),
            sems((2,)),
            sems((2,)),
            sems((7,)),
        ],
        compiler_params=pltpu.CompilerParams(
            collective_id=1, has_side_effects=True, vmem_limit_bytes=59 * 2**20
        ),
        name="gather_weights",
    )(*flat, tokens, depths, spans, natural_places())


REDUCE_STEPS = (
    ("make", 0, 3),
    ("make", 1, 3),
    ("w", 0, 3),
    ("make", 0, 2),
    ("make", 1, 1),
    ("z_early", 0, 3, 1),
    ("w", 1, 3),
    ("w", 0, 2),
    ("make", 2, 3),
    ("z_early", 0, 3, 0),
    ("make", 0, 0),
    ("w", 1, 1),
    ("make", 1, 0),
    ("make", 3, 3),
    ("w", 1, 0),
    ("w", 2, 3),
    ("make", 0, 1),
    ("z_early", 0, 2, 1),
    ("make", 1, 2),
    ("w", 0, 1),
    ("make", 2, 0),
    ("z_early", 0, 2, 0),
    ("z_early", 2, 3, 1),
    ("u", 1, 3),
    ("w", 1, 2),
    ("z_early", 2, 3, 0),
    ("make", 3, 1),
    ("u", 1, 1),
    ("w", 3, 3),
    ("make", 2, 2),
    ("make", 2, 1),
    ("z_early", 0, 1, 0),
    ("w", 2, 2),
    ("z_late", 1, 3),
    ("u", 1, 0),
    ("make", 3, 0),
    ("make", 3, 2),
    ("u", 1, 2),
    ("small", -1),
    ("z_early", 0, 1, 1),
    ("w", 2, 1),
    ("small", 0),
    ("w", 3, 1),
    ("w", 3, 2),
    ("u", 3, 3),
    ("z_early", 2, 2, 0),
    ("w", 2, 0),
    ("w", 0, 0),
    ("z_late", 1, 2),
    ("z_early", 2, 2, 1),
    ("z_early", 2, 1, 0),
    ("z_late", 1, 1),
    ("z_early", 2, 1, 1),
    ("z_early", 2, 0, 0),
    ("small", 1),
    ("u", 3, 1),
    ("u", 3, 2),
    ("z_late", 3, 3),
    ("z_early", 2, 0, 1),
    ("small", 2),
    ("z_early", 0, 0, 1),
    ("z_late", 1, 0),
    ("z_late", 3, 2),
    ("w", 3, 0),
    ("z_early", 0, 0, 0),
    ("u_late", 2),
    ("small", 3),
    ("z_late", 3, 1),
    ("u", 3, 0),
    ("u_late", 0),
    ("small", 4),
    ("z_late", 3, 0),
)


def reduce_kernel(*refs):
    factors_in, small_in, leaving = refs[:9], refs[9], refs[10:11]
    final, small_out, arriving = refs[11:15], refs[15], refs[16:17]
    part, from_core, from_w, from_u, from_z = (refs[17 + 4 * i : 21 + 4 * i] for i in range(5))
    factors, turned = refs[37:46], refs[46]
    small_held, small_got = refs[47:49]
    (
        load_sem,
        core_send,
        core_recv,
        w_send,
        w_recv,
        u_send,
        u_recv,
        z_send,
        z_recv,
        small_send,
        small_recv,
        move_send,
        move_recv,
    ) = refs[49:]
    source, target, moves = move_partners()
    z, u, w, core = place()
    me = block_of(z, u, w, core)
    above, below = device_of(z + 1, u, w, core), device_of(z - 1, u, w, core)
    across_u, across_w = device_of(z, 1 - u, w, core), device_of(z, u, 1 - w, core)
    sibling = device_of(z, w, u, 1 - core)
    near, far_z = z + 1 - 2 * (z % 2), (z + 2) % 4
    partners = (
        sibling,
        across_u,
        across_w,
        device_of(near, u, w, core),
        device_of(far_z, u, w, core),
    )
    middle_z = (z == 1) | (z == 2)

    barrier = pltpu.get_barrier_semaphore()
    for device in partners:
        pl.semaphore_signal(barrier, inc=1, device_id=device, device_id_type=MESH)

    @pl.when(moves == 1)
    def _():
        pl.semaphore_signal(barrier, inc=1, device_id=target, device_id_type=MESH)
        pl.semaphore_signal(barrier, inc=1, device_id=source, device_id_type=MESH)

    @pl.when(middle_z)
    def _():
        pl.semaphore_signal(
            barrier, inc=1, device_id=device_of(3 - z, u, w, core), device_id_type=MESH
        )

    def load(i):
        return pltpu.make_async_copy(factors_in[i], factors[i], load_sem.at[i])

    loaded = set()
    for i in LOAD_ORDER:
        load(i).start()

    pl.semaphore_wait(barrier, 5 + (z + 1) // 2 - z // 3 * 2 + 2 * moves)

    def rows(group, block):
        count = BLOCKS[group][0]
        return part[group].at[pl.ds(pl.multiple_of(block * count, 16), count)]

    def slot_of(far, column, line):
        return (far * 2 + column) * 2 + line

    def small_copy(i):
        return remote(
            small_held.at[i], small_got.at[i], small_send.at[i], small_recv.at[i], partners[i]
        )

    def small_event(i):
        if i < 0:
            small_held[0] = small_in[...]
            small_copy(0).start()
            return
        small_copy(i).wait_recv()
        total = small_held[i] + small_got[i]
        if i < 4:
            small_held[i + 1] = total
            small_copy(i + 1).start()
        else:
            small_out[...] = total

    def product(group, plane, left, right, first, width, chunk):
        count = 8 * BLOCKS[group][0]
        at = pl.multiple_of(plane * count, 128)
        turned[0:count, :] = factors[left][:, pl.ds(at, count)].T

        @pl.loop(0, width // chunk)
        def _(j):
            here = pl.multiple_of(j * chunk, 128)
            there = pl.multiple_of(first + j * chunk, 128)
            part[group][pl.ds(at, count), pl.ds(there, chunk)] = jnp.dot(
                turned[0:count, :],
                factors[right][:, pl.ds(here, chunk)],
                preferred_element_type=jnp.float32,
            ).astype(jnp.bfloat16)

    def make_event(group, step):
        for i in NEEDED[group]:
            if i not in loaded:
                load(i).wait()
                loaded.add(i)

        def action(plane, way):
            for left, right, first, width, chunk in PRODUCTS[group]:
                product(group, plane, left, right, first, width, chunk)
            for column in (0, 1):
                for line in (0, 1):
                    slot = slot_of(plane, column, line)
                    remote(
                        rows(group, block_of(plane, column, line, 1 - core)),
                        from_core[group].at[slot],
                        core_send.at[group],
                        core_recv.at[group, slot],
                        sibling,
                    ).start()

        at_distance(step, action)

    def wait_core(group, slot):
        held = from_core[group].at[slot]
        remote(held, held, core_send.at[group], core_recv.at[group, slot], sibling).wait_recv()

    def accumulate(group, block, terms):
        count = BLOCKS[group][0]
        first = pl.multiple_of(block * count, 16)

        @pl.loop(0, count // 16)
        def _(i):
            at = pl.multiple_of(i * 16, 16)
            total = part[group][pl.ds(first + at, 16), :].astype(jnp.float32)
            for ref, slot in terms:
                total = total + ref[slot, pl.ds(at, 16), :].astype(jnp.float32)
            part[group][pl.ds(first + at, 16), :] = total.astype(jnp.bfloat16)

    def at_distance(step, action):
        if step == 0:
            action(z, 0)
            return

        @pl.when(z + step < N_Z)
        def _():
            action(z + step, 1)

        @pl.when(z - step >= 0)
        def _():
            action(z - step, -1)

    def wait_w(group, slot):
        held = from_w[group].at[slot]
        remote(held, held, w_send.at[group], w_recv.at[group, slot], across_w).wait_recv()

    def w_event(group, step):
        def action(far, way, column):
            block, slot = block_of(far, column, 1 - w, core), slot_of(far, column, 1 - w)
            wait_core(group, slot)
            accumulate(group, block, [(from_core[group], slot)])
            remote(
                rows(group, block),
                from_w[group].at[far * 2 + column],
                w_send.at[group],
                w_recv.at[group, far * 2 + column],
                across_w,
            ).start()

        for column in (1 - u, u):
            at_distance(step, lambda far, way: action(far, way, column))

    def gathered(group, far, column):
        slot = slot_of(far, column, w)
        wait_core(group, slot)
        wait_w(group, far * 2 + column)
        return [(from_core[group], slot), (from_w[group], far * 2 + column)]

    def u_copy(group, src, slot):
        return remote(
            src, from_u[group].at[slot], u_send.at[group], u_recv.at[group, slot], across_u
        )

    def u_event(group, step):
        def action(far, way):
            block = block_of(far, 1 - u, w, core)
            accumulate(group, block, gathered(group, far, 1 - u))
            u_copy(group, rows(group, block), far).start()

        at_distance(step, action)

    def z_copy(group, block, way, slot):
        return remote(
            rows(group, block),
            from_z[group].at[slot],
            z_send.at[group, way, slot],
            z_recv.at[group, slot],
            below if way else above,
        )

    def z_take(group, block, way, slot):
        z_copy(group, block, way, slot).wait_recv()
        accumulate(group, block, [(from_z[group], slot)])

    def z_step(group, step, column, z_slot, terms_of):
        def action(far, way):
            block = block_of(far, column, w, core)
            accumulate(group, block, terms_of(far))
            if way >= 0:

                @pl.when(z > 0)
                def _():
                    z_take(group, block, 0, z_slot(far))

            if way <= 0:

                @pl.when(z < N_Z - 1)
                def _():
                    z_take(group, block, 1, z_slot(far if way else 4))

            if way:
                slot = z_slot(4 if way < 0 and step == 1 else far)
                z_copy(group, block, 0 if way > 0 else 1, slot).start()

        at_distance(step, action)

    def finish(group):
        count = BLOCKS[group][0]
        final[group][...] = part[group][
            pl.ds(pl.multiple_of(me * count, 16), count), :
        ].astype(jnp.float32)

    def z_late_event(group, step):
        def terms_of(far):
            terms = gathered(group, far, u)
            u_copy(group, from_u[group].at[far], far).wait_recv()
            return terms + [(from_u[group], far)]

        z_step(group, step, u, lambda far: far, terms_of)
        if step == 0:
            finish(group)

    def z_early_event(group, step, other):
        column = 1 - u if other else u
        z_step(
            group,
            step,
            column,
            lambda far: far * 2 + column,
            lambda far: gathered(group, far, column),
        )
        if step == 0 and other:
            u_copy(group, rows(group, block_of(z, 1 - u, w, core)), 0).start()

    def u_late_event(group):
        u_copy(group, from_u[group].at[0], 0).wait_recv()
        accumulate(group, me, [(from_u[group], 0)])
        finish(group)

    actions = {
        "small": small_event,
        "make": make_event,
        "w": w_event,
        "u": u_event,
        "z_early": z_early_event,
        "z_late": z_late_event,
        "u_late": u_late_event,
    }
    for event in REDUCE_STEPS:
        actions[event[0]](*event[1:])
        if event == REDUCE_STEPS[20]:
            start_moves(leaving, arriving, move_send, move_recv, target, moves)
    wait_moves(leaving, arriving, move_send, move_recv, target, moves)

    for group in range(4):
        z_first = REDUCE_ORDERS[group] == "zuw"
        count = BLOCKS[group][0]
        for sem, sends in ((core_send, 16), (w_send, 8), (u_send, 4 if z_first else 1)):
            rows_sent = part[group].at[pl.ds(0, sends * count)]
            remote(
                rows_sent, rows_sent, sem.at[group], core_recv.at[group, 0], sibling
            ).wait_send()
        for far in range(N_Z):
            for column in (0,) if z_first else (0, 1):
                slot = far if z_first else far * 2 + column

                @pl.when(z < far)
                def _():
                    z_copy(group, me, 0, slot).wait_send()

                @pl.when(z > far + 1)
                def _():
                    z_copy(group, me, 1, slot).wait_send()

        for column in (0,) if z_first else (0, 1):

            @pl.when(z > 0)
            def _():
                z_copy(group, me, 1, 4 if z_first else 8 + column).wait_send()

    for i in range(5):
        small_copy(i).wait_send()


LOAD_ORDER = (0, 1, 2, 3, 4, 5, 6, 7, 8)
NEEDED = ((0, 1, 2, 3), (4, 5), (4, 6), (7, 8))
PRODUCTS = (
    ((0, 1, 0, 1792, 256), (2, 3, 1792, 1024, 512)),
    ((4, 5, 0, 2560, 512),),
    ((4, 6, 0, 2560, 512),),
    ((7, 8, 0, 1024, 512),),
)


def reduce_gradients(factors, small, leaving):
    narrow, sems, vmem = jnp.bfloat16, pltpu.SemaphoreType.DMA, pltpu.VMEM
    z_first = [order == "zuw" for order in REDUCE_ORDERS]
    scratch = [vmem((32 * rows, columns), narrow) for rows, columns in BLOCKS]
    scratch += [vmem((16, rows, columns), narrow) for rows, columns in BLOCKS]
    scratch += [vmem((8, rows, columns), narrow) for rows, columns in BLOCKS]
    scratch += [
        vmem((4 if first else 1, rows, columns), narrow)
        for (rows, columns), first in zip(BLOCKS, z_first)
    ]
    scratch += [
        vmem((5 if first else 10, rows, columns), narrow)
        for (rows, columns), first in zip(BLOCKS, z_first)
    ]
    scratch += [vmem(x.shape, narrow) for x in factors]
    scratch += [vmem((640, RECUR * 128), narrow)]
    scratch += [vmem((5, 8, 1024), jnp.float32)] * 2
    scratch += [
        sems((9,)),
        sems((4,)),
        sems((4, 16)),
        sems((4,)),
        sems((4, 8)),
        sems((4,)),
        sems((4, 4)),
        sems((4, 2, 10)),
        sems((4, 10)),
        sems((5,)),
        sems((5,)),
        sems((1,)),
        sems((1,)),
    ]
    anywhere, here = pl.BlockSpec(memory_space=pl.ANY), pl.BlockSpec(memory_space=vmem)
    return pl.pallas_call(
        reduce_kernel,
        out_shape=[jax.ShapeDtypeStruct(shape, jnp.float32) for shape in BLOCKS]
        + [jax.ShapeDtypeStruct((8, 1024), jnp.float32)]
        + [jax.ShapeDtypeStruct(x.shape, x.dtype) for x in leaving],
        in_specs=[anywhere] * 9 + [here, anywhere],
        out_specs=[here] * 5 + [anywhere],
        scratch_shapes=scratch,
        compiler_params=pltpu.CompilerParams(
            collective_id=2, has_side_effects=True, vmem_limit_bytes=60 * 2**20
        ),
        name="reduce_gradients",
    )(*factors, small, *leaving)


Q_TILES = 9
O_AT, KV_AT, KV_WIDTH = 1792, 1152, 640
CHUNK = 512
SUB = 64


def dot_nn(left, right):
    return jnp.dot(left, right, preferred_element_type=jnp.float32)


def dot_nt(left, right):
    return lax.dot_general(
        left, right, (((1,), (1,)), ((), ())), preferred_element_type=jnp.float32
    )


def span_of_device():
    seq = lax.axis_index("seq")
    rep = lax.axis_index("rep")
    z, x, y, core = seq // 2, seq % 2, rep // 2, rep % 2
    return z, (2 * x + y + x * (1 - 2 * y)) * 2 + core


def device_of_span(group, span):
    chip = span // 2
    x, y = chip // 2, (chip + 1) // 2 % 2
    return (group * 2 + x, y * 2 + span % 2)


def lanes(shape):
    return lax.broadcasted_iota(jnp.int32, shape, 1)


def rotated(value, cosine, sine):
    first = lanes(value.shape) % 64 < 32
    partner = jnp.where(first, pltpu.roll(value, 96, 1), pltpu.roll(value, 32, 1))
    return value * cosine + partner * sine


def block_kernel(*refs):
    (tokens, cotangent, meta, rope, turn, gain_a, gain_f, routers, wa_in, wg_in, wu_in, wd_in) = refs[:12]
    (output, input_grad, small, a_all, gqkv_all, o_all, gt_all, b_all, gg_all, gu_all, hidden_all, gf_all) = refs[12:24]
    (
        wa, wg, wu, wd, gains, natural_at, padded_at, cotangent_at, leaving, h_all, z_all, tf_all, gate_all, up_all, q_all, window,
        got, sending, depth_win, depth_at, bias_at, cos_at, sin_at, stats, dkv, grad, acc, gg_at, gu_at,
        keys_at, s_at, gp_at, p_at, gs_at, qs_at, us_at, move_send, move_recv,
        load_sem, out_sem, kv_send, kv_recv, back_send, back_recv, depth_send, depth_recv,
    ) = refs[24:]
    narrow, wide = jnp.bfloat16, jnp.float32
    group, span = span_of_device()
    core = span % 2
    target, source, moves = move_partners()

    barrier = pltpu.get_barrier_semaphore()
    for away in (1, 2, 3):

        @pl.when(span + away < 8)
        def _():
            pl.semaphore_signal(
                barrier, inc=1, device_id=device_of_span(group, span + away), device_id_type=MESH
            )

        @pl.when(span - away >= 0)
        def _():
            pl.semaphore_signal(
                barrier, inc=1, device_id=device_of_span(group, span - away), device_id_type=MESH
            )

    @pl.when(moves == 1)
    def _():
        pl.semaphore_signal(barrier, inc=1, device_id=target, device_id_type=MESH)
        pl.semaphore_signal(barrier, inc=1, device_id=source, device_id_type=MESH)

    loads = [
        pltpu.make_async_copy(src, dst, load_sem.at[i])
        for i, (src, dst) in enumerate(((wa_in, wa), (wg_in, wg), (wu_in, wu), (wd_in, wd)))
    ]
    for load in loads:
        load.start()

    depth_win[3] = jnp.broadcast_to(meta[0:1, :], (8, 128))
    for away in (1, 2, 3):

        @pl.when(span - away < 0)
        def _():
            depth_win[3 - away] = jnp.zeros((8, 128), wide)
            for recursion in range(RECUR):
                window[recursion, 3 - away] = jnp.zeros((128, KV_WIDTH), narrow)

    pl.semaphore_wait(barrier, 3 + span + span // 4 * (7 - 2 * span) + 2 * moves)
    start_moves((cotangent,), (cotangent_at,), move_send.at[pl.ds(0, 1)], move_recv.at[pl.ds(0, 1)], target, moves)

    def depth_copy(away, device):
        return remote(
            depth_win.at[3],
            depth_win.at[3 - away],
            depth_send.at[away - 1],
            depth_recv.at[away - 1],
            device,
        )

    def kv_copy(recursion, slot, to_slot, sent, device):
        return remote(
            window.at[recursion, slot],
            window.at[recursion, to_slot],
            kv_send.at[recursion, sent],
            kv_recv.at[recursion, to_slot],
            device,
        )

    def back_copy(recursion, slot, device):
        return remote(
            sending.at[slot],
            got.at[recursion, slot],
            back_send.at[recursion, slot],
            back_recv.at[recursion, slot],
            device,
        )

    def stage_copies(recursion):
        return [
            pltpu.make_async_copy(gg_at, gg_all.at[recursion], out_sem.at[0]),
            pltpu.make_async_copy(gu_at, gu_all.at[recursion], out_sem.at[1]),
        ]

    def neighbour(away):
        return device_of_span(group, span + away)

    sibling = neighbour(1 - 2 * core)

    def when(condition, action):
        @pl.when(condition)
        def _():
            action()

    def send_keys(recursion):
        when(span + 2 < 8, lambda: kv_copy(recursion, 3, 1, 0, neighbour(2)).start())
        when(core == 0, lambda: kv_copy(recursion, 3, 2, 1, sibling).start())
        when(
            (core == 1) & (span + 3 < 8),
            lambda: kv_copy(recursion, 3, 0, 1, neighbour(3)).start(),
        )

    def pass_keys_on(recursion):
        @pl.when(span >= 2)
        def _():
            kv_copy(recursion, 3, 1, 0, sibling).wait_recv()
            kv_copy(recursion, 1, 2 * core, 2, sibling).start()

    def wait_keys(recursion):
        when(span >= 1, lambda: kv_copy(recursion, 3, 2, 1, sibling).wait_recv())
        when(span >= 3, lambda: kv_copy(recursion, 3, 0, 1, sibling).wait_recv())

    def wait_keys_sent(recursion):
        when(span + 2 < 8, lambda: kv_copy(recursion, 3, 1, 0, sibling).wait_send())
        when(core == 0, lambda: kv_copy(recursion, 3, 2, 1, sibling).wait_send())
        when(
            (core == 1) & (span + 3 < 8),
            lambda: kv_copy(recursion, 3, 0, 1, sibling).wait_send(),
        )
        when(span >= 2, lambda: kv_copy(recursion, 1, 2, 2, sibling).wait_send())

    def send_back(recursion):
        @pl.when(span >= 2)
        def _():
            sending[0] = dkv[pl.ds(pl.multiple_of(256 * (1 - core), 128), 128), :].astype(narrow)
            back_copy(recursion, 0, sibling).start()

        sending[2] = dkv[pl.ds(pl.multiple_of(256 * core, 128), 128), :].astype(narrow)
        when(core == 1, lambda: back_copy(recursion, 2, sibling).start())
        when(
            (core == 0) & (span >= 3),
            lambda: back_copy(recursion, 2, neighbour(-3)).start(),
        )

    def pass_back_on(recursion):
        @pl.when(span >= 2)
        def _():
            back_copy(recursion, 0, sibling).wait_recv()
            sending[1] = (dkv[128:256, :] + got[recursion, 0].astype(wide)).astype(narrow)
            back_copy(recursion, 1, neighbour(-2)).start()

    def take_back(recursion):
        @pl.when((core == 0) | (span + 3 < 8))
        def _():
            back_copy(recursion, 2, sibling).wait_recv()
            dkv[384:512, :] += got[recursion, 2].astype(wide)

        @pl.when(span + 2 < 8)
        def _():
            back_copy(recursion, 1, sibling).wait_recv()
            dkv[384:512, :] += got[recursion, 1].astype(wide)

    def wait_back_sent(recursion):
        when(span >= 2, lambda: back_copy(recursion, 0, sibling).wait_send())
        when(span >= 2, lambda: back_copy(recursion, 1, sibling).wait_send())
        when((core == 1) | (span >= 3), lambda: back_copy(recursion, 2, sibling).wait_send())

    def add_pads():
        for block in range(32):
            padded_at[block * PADDED_ROWS : block * PADDED_ROWS + OWN_ROWS, :] = natural_at[
                block * OWN_ROWS : block * OWN_ROWS + OWN_ROWS, :
            ]

    def drop_pads():
        for block in range(32):
            natural_at[block * OWN_ROWS : block * OWN_ROWS + OWN_ROWS, :] = padded_at[
                block * PADDED_ROWS : block * PADDED_ROWS + OWN_ROWS, :
            ]

    here = device_of_span(group, span)
    for away in (1, 2, 3):
        when(span + away < 8, lambda: depth_copy(away, neighbour(away)).start())

    span_lane = meta[1:2, :]
    turn_cos = jnp.zeros((1, 128), wide)
    turn_sin = jnp.zeros((1, 128), wide)
    for k in range(4):
        turn_cos = turn_cos + jnp.where(span_lane == k, turn[k : k + 1, :], 0.0)
        turn_sin = turn_sin + jnp.where(span_lane == k, turn[8 + k : 9 + k, :], 0.0)
    cos_at[...] = turn_cos * rope[0] - turn_sin * rope[1]
    sign = jnp.where(lanes((128, 128)) % 64 < 32, -1.0, 1.0)
    sin_at[...] = sign * (turn_sin * rope[0] + turn_cos * rope[1])

    padded_at[...] = jnp.zeros((1024, 128), wide)
    vectors = jnp.concatenate(
        [gain_a[...], gain_f[...], routers[...], jnp.zeros((123, MODEL_WIDTH), wide)], axis=0
    )
    natural_at[...] = vectors.T
    add_pads()
    gains[...] = padded_at[...].T[0:8, :]
    natural_at[...] = tokens[...].astype(wide)
    add_pads()
    h_all[0] = padded_at[...].T
    small[...] = jnp.zeros((8, 1024), wide)

    for away in (1, 2, 3):
        when(span - away >= 0, lambda: depth_copy(away, here).wait_recv())
    row = lax.broadcasted_iota(jnp.int32, (128, 128), 0)
    column = lanes((128, 128))
    ones = jnp.ones((128, 128), wide)
    for block in range(4):
        held = depth_win[block]
        depth_at[pl.ds(block * 128, 128), :] = dot_nn(
            jnp.where(row == column, jnp.broadcast_to(held[0:1, :], (128, 128)), 0.0), ones
        ).astype(narrow)

    def set_bias(recursion):
        level = recursion.astype(wide)
        for block in range(4):
            active = depth_at[pl.ds(block * 128, 128), :].astype(wide) > level
            if block == 3:
                allowed = (row == column) | (active & (row <= column))
            else:
                allowed = active & (span_lane >= 3 - block)
            bias_at[pl.ds(block * 128, 128), :] = jnp.where(allowed, 0.0, masked_score).astype(narrow)

    def inverse_rms(value):
        return lax.rsqrt(
            jnp.sum(value * value, axis=-1, keepdims=True) / MODEL_WIDTH + epsilon
        )

    def active_column(recursion):
        own = depth_at[384:512, :].astype(wide)[:, 0:1]
        return jnp.where(own > recursion.astype(wide), 1.0, 0.0)

    def mixing_gate(recursion):
        logits = jnp.sum(
            h_all[recursion] * gains[pl.ds(2 + recursion, 1), :], axis=-1, keepdims=True
        )
        return jax.nn.sigmoid(logits)

    def halves(tile, pair):
        low = lanes(tile.shape) < 64
        zero = jnp.zeros_like(tile)
        if pair == 2:
            return jnp.where(low, tile, zero)
        return jnp.concatenate([jnp.where(low, tile, zero), jnp.where(low, zero, tile)], axis=0)

    def set_keys(recursion, pair):
        for block in range(4):
            at = pl.ds(block * 128, 128)
            keys_at[at, 0:128] = window[recursion, block, :, pair * 128 : pair * 128 + 128]
            keys_at[at, 128:256] = bias_at[at, :]

    def value_tile(recursion, pair):
        at = 256 if pair == 2 else 384 + pair * 128
        parts = [window[recursion, b, :, at : at + 128] for b in range(4)]
        return jnp.concatenate(parts, axis=0)

    def set_scores(recursion, pair, part, buffer):
        at = (pair * 3 + part) * 128
        queries = halves(q_all[recursion, :, at : at + 128], pair)
        width = queries.shape[0]
        same = jnp.where(row == column, 1.0, 0.0).astype(narrow)
        same = same if width == 128 else jnp.concatenate([same, same], axis=0)
        both = jnp.concatenate([queries, same], axis=1)
        s_at[buffer, :, 0:width] = dot_nt(keys_at[...], both)
        return queries, width

    def rows_of_eight(value, join):
        return join(value.reshape(value.shape[0] // 8, 8, value.shape[1]), axis=0)

    def joined(out, pair):
        if pair == 2:
            return jnp.where(row < 64, out, 0.0).T
        return jnp.where(row < 64, out[:, :128], out[:, 128:]).T

    def attend(recursion):
        for pair in range(3):
            set_keys(recursion, pair)
            values_t = value_tile(recursion, pair).T
            for part in range(3):
                buffer = part % 2
                _, width = set_scores(recursion, pair, part, buffer)
                top = jnp.full((8, width), masked_score, wide)
                for sub in range(0, 512, SUB):
                    scores = s_at[buffer, sub : sub + SUB, 0:width]
                    top = jnp.maximum(top, rows_of_eight(scores, jnp.max))
                top = jnp.max(top, axis=0, keepdims=True)
                total = jnp.zeros((8, width), wide)
                for sub in range(0, 512, SUB):
                    weight = jnp.exp(s_at[buffer, sub : sub + SUB, 0:width] - top)
                    total = total + rows_of_eight(weight, jnp.sum)
                    p_at[sub : sub + SUB, part * 256 : part * 256 + width] = weight.astype(narrow)
                total = jnp.sum(total, axis=0, keepdims=True)
                stats[recursion, pair * 3 + part, 0:1, 0:width] = top + jnp.log(total)
                out = dot_nn(values_t, p_at[:, part * 256 : part * 256 + width]) / total
                if pair == 2:
                    head = (12 + part) * HEAD_SIZE
                    natural_at[head : head + 64, :] = out[64:, :]
                else:
                    head = (6 * pair + part) * HEAD_SIZE
                    natural_at[head : head + 64, :] = out[:64, :128]
                    head = (6 * pair + 3 + part) * HEAD_SIZE
                    natural_at[head : head + 64, :] = out[64:, 128:]

    def upstream_of(pair, part):
        zero = jnp.zeros((64, 128), narrow)

        def head(number):
            return natural_at[number * 64 : number * 64 + 64, :].astype(narrow)

        if pair == 2:
            return jnp.concatenate([zero, head(12 + part)], axis=0)
        low = jnp.concatenate([head(6 * pair + part), zero], axis=1)
        high = jnp.concatenate([zero, head(6 * pair + 3 + part)], axis=1)
        return jnp.concatenate([low, high], axis=0)

    def attend_back(recursion):
        for pair in range(3):
            set_keys(recursion, pair)
            values = value_tile(recursion, pair)
            keys_t = keys_at[:, 0:128].T
            width = 128 if pair == 2 else 256
            for part in range(3):
                buffer = part % 2
                queries, _ = set_scores(recursion, pair, part, buffer)
                upstream = upstream_of(pair, part)
                qs_at[part * width : part * width + width, :] = queries
                us_at[:, part * width : part * width + width] = upstream
                gp_at[buffer, :, 0:width] = dot_nn(values, upstream)
                log_total = stats[recursion, pair * 3 + part, 0:1, 0:width]
                inner = jnp.zeros((8, width), wide)
                where = slice(part * width, part * width + width)
                for sub in range(0, 512, SUB):
                    probs = jnp.exp(s_at[buffer, sub : sub + SUB, 0:width] - log_total)
                    s_at[buffer, sub : sub + SUB, 0:width] = probs
                    p_at[sub : sub + SUB, where] = probs.astype(narrow)
                    inner = inner + rows_of_eight(
                        probs * gp_at[buffer, sub : sub + SUB, 0:width], jnp.sum
                    )
                inner = jnp.sum(inner, axis=0, keepdims=True)
                for sub in range(0, 512, SUB):
                    rows = slice(sub, sub + SUB)
                    gs_at[rows, where] = (
                        s_at[buffer, rows, 0:width] * (gp_at[buffer, rows, 0:width] - inner)
                    ).astype(narrow)
            grad_keys = dot_nn(gs_at[:, 0 : 3 * width], qs_at[0 : 3 * width, :])
            grad_values = dot_nt(p_at[:, 0 : 3 * width], us_at[:, 0 : 3 * width])
            if pair == 2:
                dkv[:, 256:384] = grad_keys + grad_values
            else:
                dkv[:, pair * 128 : pair * 128 + 128] = grad_keys
                dkv[:, 384 + pair * 128 : 512 + pair * 128] = grad_values
            out = dot_nn(keys_t, gs_at[:, 0 : 3 * width])
            for part in range(3):
                at = (pair * 3 + part) * 128
                gqkv_all[recursion, :, at : at + 128] = rotated(
                    joined(out[:, part * width : part * width + width], pair),
                    cos_at[...] * 0.125,
                    sin_at[...] * -0.125,
                ).astype(narrow)

    def rotate_keys(value, sine):
        cosine = cos_at[...]
        low = lanes((128, 128)) < 64
        parts = []
        for tile in range(5):
            part = value[:, tile * 128 : tile * 128 + 128]
            if tile < 2:
                part = rotated(part, cosine, sine)
            elif tile == 2:
                part = jnp.where(low, rotated(part, cosine, sine), part)
            parts.append(part)
        return jnp.concatenate(parts, axis=1)

    @pl.loop(0, RECUR)
    def _(recursion):
        state = h_all[recursion]
        normal = state * inverse_rms(state)
        a_b = (normal * gains[0:1, :]).astype(narrow)
        a_all[recursion] = a_b

        @pl.when(recursion == 0)
        def _():
            loads[0].wait()

        pair_values = dot_nn(a_b, wa[:, KV_AT:O_AT])
        window[recursion, 3] = rotate_keys(pair_values, sin_at[...]).astype(narrow)
        send_keys(recursion)
        cosine, sine = cos_at[...] * 0.125, sin_at[...] * 0.125
        for first, width in ((0, 512), (512, 512), (1024, 128)):
            queries = dot_nn(a_all[recursion], wa[:, first : first + width])
            for at in range(0, width, 128):
                q_all[recursion, :, first + at : first + at + 128] = rotated(
                    queries[:, at : at + 128], cosine, sine
                ).astype(narrow)
        set_bias(recursion)
        pass_keys_on(recursion)
        wait_keys(recursion)
        attend(recursion)
        add_pads()
        o_pad = padded_at[...].T.astype(narrow)
        o_all[recursion] = o_pad
        branch = dot_nn(o_pad, wa[:, O_AT:])
        middle = h_all[recursion] + branch
        z_all[recursion] = middle
        b_b = (middle * inverse_rms(middle) * gains[1:2, :]).astype(narrow)
        b_all[recursion] = b_b
        acc[...] = branch

        @pl.when(recursion == 0)
        def _():
            for load in loads[1:]:
                load.wait()

        @pl.loop(0, FEEDFORWARD_UNITS // CHUNK)
        def _(j):
            at = pl.ds(pl.multiple_of(j * CHUNK, CHUNK), CHUNK)
            gate = dot_nn(b_all[recursion], wg[:, at])
            up = dot_nn(b_all[recursion], wu[:, at])
            gate_all[recursion, :, at] = gate
            up_all[recursion, :, at] = up
            hidden = (gate * jax.nn.sigmoid(gate) * up).astype(narrow)
            hidden_all[recursion, :, at] = hidden
            acc[...] += dot_nn(hidden, wd[at, :])

        tf_all[recursion] = acc[...]
        mixing = active_column(recursion) * mixing_gate(recursion)
        following = h_all[recursion] + mixing * acc[...]

        @pl.when(recursion < RECUR - 1)
        def _():
            h_all[recursion + 1] = following

        @pl.when(recursion == RECUR - 1)
        def _():
            padded_at[...] = following.astype(narrow).astype(wide).T
            drop_pads()
            leaving[...] = natural_at[...].astype(narrow)

    start_moves((leaving,), (output,), move_send.at[pl.ds(1, 1)], move_recv.at[pl.ds(1, 1)], source, moves)
    wait_moves((cotangent,), (cotangent_at,), move_send.at[pl.ds(0, 1)], move_recv.at[pl.ds(0, 1)], target, moves)
    natural_at[...] = cotangent_at[...].astype(wide)
    add_pads()
    grad[...] = padded_at[...].T

    @pl.loop(0, RECUR)
    def _(i):
        recursion = RECUR - 1 - i
        router_row = gains[pl.ds(2 + recursion, 1), :]
        active, gate_value = active_column(recursion), mixing_gate(recursion)
        upstream = grad[...]
        grad_mix = jnp.sum(upstream * tf_all[recursion], axis=-1, keepdims=True)
        grad_logit = active * grad_mix * gate_value * (1.0 - gate_value)
        small[pl.ds(2 + recursion, 1), :] = jnp.sum(
            grad_logit * h_all[recursion], axis=0, keepdims=True
        )
        delta = (active * gate_value) * upstream
        gf_all[recursion] = delta.astype(narrow)
        grad[...] = upstream + grad_logit * router_row
        tf_all[recursion] = delta
        acc[...] = jnp.zeros((128, 1024), wide)

        @pl.when(recursion < RECUR - 1)
        def _():
            for copy in stage_copies(recursion + 1):
                copy.wait()

        @pl.loop(0, FEEDFORWARD_UNITS // CHUNK)
        def _(j):
            at = pl.ds(pl.multiple_of(j * CHUNK, CHUNK), CHUNK)
            grad_hidden = dot_nt(gf_all[recursion], wd[at, :])
            gate, up = gate_all[recursion, :, at], up_all[recursion, :, at]
            sigmoid = jax.nn.sigmoid(gate)
            grad_gate = (grad_hidden * up * sigmoid * (1.0 + gate * (1.0 - sigmoid))).astype(narrow)
            grad_up = (grad_hidden * gate * sigmoid).astype(narrow)
            gg_at[:, at] = grad_gate
            gu_at[:, at] = grad_up
            acc[...] += dot_nt(grad_gate, wg[:, at]) + dot_nt(grad_up, wu[:, at])

        for copy in stage_copies(recursion):
            copy.start()
        middle = z_all[recursion]
        inverse = inverse_rms(middle)
        normal = middle * inverse
        small[1:2, :] += jnp.sum(acc[...] * normal, axis=0, keepdims=True)
        scaled = acc[...] * gains[1:2, :]
        inner = jnp.sum(scaled * normal, axis=-1, keepdims=True) / MODEL_WIDTH
        grad_middle = inverse * (scaled - normal * inner)
        gt_b = (tf_all[recursion] + grad_middle).astype(narrow)
        gt_all[recursion] = gt_b
        grad[...] += grad_middle
        padded_at[...] = dot_nt(gt_b, wa[:, O_AT:]).T
        drop_pads()
        set_bias(recursion)
        attend_back(recursion)

        @pl.when(recursion < RECUR - 1)
        def _():
            wait_back_sent(recursion + 1)

        send_back(recursion)
        pass_back_on(recursion)
        acc[...] = dot_nt(gqkv_all[recursion, :, :KV_AT], wa[:, :KV_AT])

        take_back(recursion)
        gqkv_all[recursion, :, KV_AT:] = rotate_keys(dkv[384:512, :], -sin_at[...]).astype(narrow)
        grad_normed = acc[...] + dot_nt(gqkv_all[recursion, :, KV_AT:], wa[:, KV_AT:O_AT])
        state = h_all[recursion]
        inverse = inverse_rms(state)
        normal = state * inverse
        small[0:1, :] += jnp.sum(grad_normed * normal, axis=0, keepdims=True)
        scaled = grad_normed * gains[0:1, :]
        inner = jnp.sum(scaled * normal, axis=-1, keepdims=True) / MODEL_WIDTH
        grad[...] += inverse * (scaled - normal * inner)

    for copy in stage_copies(0):
        copy.wait()
    padded_at[...] = grad[...].T
    drop_pads()
    input_grad[...] = natural_at[...].astype(narrow)

    wait_moves((leaving,), (output,), move_send.at[pl.ds(1, 1)], move_recv.at[pl.ds(1, 1)], source, moves)
    for away in (1, 2, 3):
        when(span + away < 8, lambda: depth_copy(away, here).wait_send())
    for recursion in range(RECUR):
        wait_keys_sent(recursion)
    wait_back_sent(0)


def run_block(tokens, cotangent, meta, gains, weights):
    narrow, wide, vmem, sems = jnp.bfloat16, jnp.float32, pltpu.VMEM, pltpu.SemaphoreType.DMA
    half = HEAD_SIZE // 2
    lane = np.arange(128) % half
    frequency = 10000.0 ** (-lane / half)
    angle = np.arange(128)[:, None] * frequency[None, :]
    rope = np.stack([np.cos(angle), np.sin(angle)]).astype(np.float32)
    jump = np.arange(4)[:, None] * 128.0 * frequency[None, :]
    turn = np.zeros((16, 128), np.float32)
    turn[:4], turn[8:12] = np.cos(jump), np.sin(jump)
    outs = [((MODEL_WIDTH, 128), narrow), ((MODEL_WIDTH, 128), narrow), ((8, 1024), wide)]
    outs += [
        ((RECUR, 128, width), narrow)
        for width in (1024, O_AT, 1024, 1024, 1024, 2560, 2560, 2560, 1024)
    ]
    scratch = [
        vmem((1024, 2816), narrow),
        vmem((1024, 2560), narrow),
        vmem((1024, 2560), narrow),
        vmem((2560, 1024), narrow),
        vmem((8, 1024), wide),
        vmem((MODEL_WIDTH, 128), wide),
        vmem((1024, 128), wide),
        vmem((MODEL_WIDTH, 128), narrow),
        vmem((MODEL_WIDTH, 128), narrow),
        vmem((RECUR, 128, 1024), wide),
        vmem((RECUR, 128, 1024), wide),
        vmem((RECUR, 128, 1024), wide),
        vmem((RECUR, 128, 2560), wide),
        vmem((RECUR, 128, 2560), wide),
        vmem((RECUR, 128, KV_AT), narrow),
        vmem((RECUR, 4, 128, KV_WIDTH), narrow),
        vmem((RECUR, 3, 128, KV_WIDTH), narrow),
        vmem((3, 128, KV_WIDTH), narrow),
        vmem((4, 8, 128), wide),
        vmem((512, 128), narrow),
        vmem((512, 128), narrow),
        vmem((128, 128), wide),
        vmem((128, 128), wide),
        vmem((RECUR, Q_TILES, 2, 256), wide),
        vmem((512, KV_WIDTH), wide),
        vmem((128, 1024), wide),
        vmem((128, 1024), wide),
        vmem((128, 2560), narrow),
        vmem((128, 2560), narrow),
        vmem((512, 256), narrow),
        vmem((2, 512, 256), wide),
        vmem((2, 512, 256), wide),
        vmem((512, 768), narrow),
        vmem((512, 768), narrow),
        vmem((768, 128), narrow),
        vmem((128, 768), narrow),
        sems((2,)),
        sems((2,)),
        sems((4,)),
        sems((2,)),
        sems((RECUR, 3)),
        sems((RECUR, 3)),
        sems((RECUR, 3)),
        sems((RECUR, 3)),
        sems((3,)),
        sems((3,)),
    ]
    here, anywhere = pl.BlockSpec(memory_space=vmem), pl.BlockSpec(memory_space=pl.ANY)
    return pl.pallas_call(
        block_kernel,
        out_shape=[jax.ShapeDtypeStruct(shape, dtype) for shape, dtype in outs],
        in_specs=[here, anywhere] + [here] * 6 + [anywhere] * 4,
        out_specs=[here] * 8 + [anywhere] * 2 + [here] * 2,
        scratch_shapes=scratch,
        compiler_params=pltpu.CompilerParams(
            collective_id=3, has_side_effects=True, vmem_limit_bytes=60 * 2**20
        ),
        name="run_block",
    )(tokens, cotangent, meta, rope, turn, *gains, *weights)


HEAD_TILES = tuple(
    (6 * (tile // 3) + tile % 3, 6 * (tile // 3) + 3 + tile % 3) if tile < 6 else (6 + tile, -1)
    for tile in range(9)
)
NATURAL_TILES = tuple((2 * tile, 2 * tile + 1 if tile < 7 else -1) for tile in range(8))


def fill_spread(spread, places):
    @pl.loop(0, MODEL_WIDTH // 64)
    def _(i):
        at = pl.multiple_of(i * 64, 64)
        rows = lax.broadcasted_iota(jnp.int32, (64, 1024), 0) + at
        spread[pl.ds(at, 64), :] = jnp.where(rows == places[0:1, :], 1.0, 0.0).astype(jnp.bfloat16)


def chunk_rows(flat, units, pairs, parity, unit):
    where = units * parity + unit
    return flat[pl.ds(where // 2, pairs, stride=units), :], where % 2


def placed_half(found, low):
    value, half = found
    return value if half == (0 if low else 1) else pltpu.roll(value, 64, 1)


def pack_tiles(flat, out, first, tiles, units, pairs):
    low = lax.broadcasted_iota(jnp.int32, (pairs, 128), 1) < 64
    zero = jnp.zeros((pairs, 128), jnp.float32)
    for parity in (0, 1):
        for tile, (left, right) in enumerate(tiles):
            one = placed_half(chunk_rows(flat, units, pairs, parity, left), True) if left >= 0 else zero
            two = (
                placed_half(chunk_rows(flat, units, pairs, parity, right), False)
                if right >= 0
                else zero
            )
            out[first + tile, pl.ds(parity, pairs, stride=2), :] = jnp.where(low, one, two)


def pack_own(flat, own, spread, places, tiles, natural, long_rows):
    w_query, w_key, w_value, w_out, w_gate, w_up, w_down = flat
    attention, gate, up, down = own
    narrow = jnp.bfloat16
    tiles[...] = jnp.zeros(tiles.shape, jnp.float32)
    natural[...] = jnp.zeros(natural.shape, jnp.float32)
    pack_tiles(w_query, tiles, 0, HEAD_TILES, 15, 15)
    pack_tiles(w_key, tiles, 9, ((0, 1), (2, 3), (4, -1)), 5, 15)
    pack_tiles(w_value, tiles, 12, ((0, 1), (2, 3), (-1, 4)), 5, 15)
    low = lax.broadcasted_iota(jnp.int32, (32, 128), 1) < 64
    tiles[11] = jnp.where(low, tiles[11], tiles[14])
    for tile in range(14):
        attention[:, tile * 128 : tile * 128 + 128] = tiles[tile].astype(narrow)
    pack_tiles(w_out, natural, 0, NATURAL_TILES, 15, 15)
    for source, out in ((w_gate, gate), (w_up, up)):
        for tile in range(20):
            tiles[tile, 0:OWN_ROWS] = source[pl.ds(tile, OWN_ROWS, stride=20), :]
            tiles[tile, OWN_ROWS:] = jnp.zeros((PADDED_ROWS - OWN_ROWS, 128), jnp.float32)
            out[:, tile * 128 : tile * 128 + 128] = tiles[tile].astype(narrow)
    pack_tiles(w_down, long_rows, 0, NATURAL_TILES, 15, 40)
    both = jnp.concatenate([side_by_side(natural), side_by_side(long_rows)], axis=0)
    both = dot_nn(both.astype(narrow), spread[...]).astype(narrow)
    attention[:, 1792:], down[...] = both[0:32], both[32:112]


def side_by_side(tiles):
    return jnp.concatenate([tiles[tile] for tile in range(8)], axis=1)[:, 0:MODEL_WIDTH]


def natural_places():
    padded = np.arange(1024)
    natural = padded // PADDED_ROWS * OWN_ROWS + padded % PADDED_ROWS
    natural = np.where(padded % PADDED_ROWS < OWN_ROWS, natural, -1)
    return np.broadcast_to(natural[None], (8, 1024)).astype(np.int32)


def unpack_tiles(packed, first, tiles, units, pairs, out):
    spots = {}
    for tile, heads in enumerate(tiles):
        for half, unit in enumerate(heads):
            if unit >= 0:
                spots[unit] = (tile, half)
    low = lax.broadcasted_iota(jnp.int32, (pairs, 128), 1) < 64

    def unit_at(where, is_low):
        parity, unit = where // units, where % units
        tile, half = spots[unit]
        value = packed[first + tile, pl.ds(parity, pairs, stride=2), :]
        return placed_half((value, half), is_low)

    for chunk in range(units):
        out[pl.ds(chunk, pairs, stride=units), :] = jnp.where(
            low, unit_at(2 * chunk, True), unit_at(2 * chunk + 1, False)
        )


def exact_gathered(value, spread):
    first = value.astype(jnp.bfloat16)
    rest = value - first.astype(jnp.float32)
    second = rest.astype(jnp.bfloat16)
    third = (rest - second.astype(jnp.float32)).astype(jnp.bfloat16)
    summed = dot_nt(jnp.concatenate([first, second, third], axis=0), spread[...])
    rows = value.shape[0]
    return summed[0:rows] + summed[rows : 2 * rows] + summed[2 * rows :]


def split_tiles(value, tiles):
    for tile in range(7):
        tiles[tile] = value[:, tile * 128 : tile * 128 + 128]
    tiles[7, :, 0:64] = value[:, 896:960]


def unpack_kernel(*refs):
    inside, places = refs[:7], refs[7]
    d_query, d_key, d_value, d_out, d_gate, d_up, d_down = refs[8:15]
    d_attn, d_ffn, d_router, output, input_grad = refs[15:20]
    held, (spread, tiles, natural, long_rows, sems) = refs[20:26], refs[26:]
    copies = [
        pltpu.make_async_copy(src, dst, sems.at[i])
        for i, (src, dst) in enumerate(zip(inside, held + (output,)))
    ]
    for copy in copies:
        copy.start()
    fill_spread(spread, places)
    for copy in copies[:6]:
        copy.wait()
    attention, gate, up, down, small, moved_grad = held
    input_grad[...] = moved_grad[...].astype(jnp.float32)
    for tile in range(14):
        tiles[tile] = attention[:, tile * 128 : tile * 128 + 128]
    unpack_tiles(tiles, 0, HEAD_TILES, 15, 15, d_query)
    unpack_tiles(tiles, 9, ((0, 1), (2, 3), (4, -1)), 5, 15, d_key)
    unpack_tiles(tiles, 11, ((-1, 4), (0, 1), (2, 3)), 5, 15, d_value)
    for packed, out in ((gate, d_gate), (up, d_up)):
        for tile in range(20):
            out[pl.ds(tile, OWN_ROWS, stride=20), :] = packed[
                0:OWN_ROWS, tile * 128 : tile * 128 + 128
            ]
    gathered = exact_gathered(
        jnp.concatenate([attention[:, 1792:], down[...], small[...]], axis=0), spread
    )
    split_tiles(gathered[0:32], natural)
    unpack_tiles(natural, 0, NATURAL_TILES, 15, 15, d_out)
    split_tiles(gathered[32:112], long_rows)
    unpack_tiles(long_rows, 0, NATURAL_TILES, 15, 40, d_down)
    d_attn[...], d_ffn[...], d_router[...] = gathered[112:113], gathered[113:114], gathered[114:117]
    copies[6].wait()


def unpack_gradients(sums, small, input_grad, output):
    narrow, wide, vmem = jnp.bfloat16, jnp.float32, pltpu.VMEM
    here, anywhere = pl.BlockSpec(memory_space=vmem), pl.BlockSpec(memory_space=pl.ANY)
    flat = (225, 75, 75, 225, 600, 600, 600)
    inside = (*sums, small, input_grad, output)
    return pl.pallas_call(
        unpack_kernel,
        out_shape=[jax.ShapeDtypeStruct((rows, 128), wide) for rows in flat]
        + [
            jax.ShapeDtypeStruct((1, MODEL_WIDTH), wide),
            jax.ShapeDtypeStruct((1, MODEL_WIDTH), wide),
            jax.ShapeDtypeStruct((RECUR, MODEL_WIDTH), wide),
            jax.ShapeDtypeStruct((MODEL_WIDTH, 128), narrow),
            jax.ShapeDtypeStruct((MODEL_WIDTH, 128), wide),
        ],
        in_specs=[anywhere] * 7 + [here],
        out_specs=[here] * 10 + [anywhere, here],
        scratch_shapes=[vmem(x.shape, x.dtype) for x in inside[:6]]
        + [
            vmem((MODEL_WIDTH, 1024), narrow),
            vmem((14, 32, 128), wide),
            vmem((8, 32, 128), wide),
            vmem((8, 80, 128), wide),
            pltpu.SemaphoreType.DMA((7,)),
        ],
        compiler_params=pltpu.CompilerParams(vmem_limit_bytes=59 * 2**20),
        name="unpack_gradients",
    )(*inside, natural_places())


def per_device_fast(
    tokens,
    depths,
    seq_spans,
    cotangent,
    w_query,
    key_weight,
    value_weight,
    w_out,
    w_gate,
    w_up,
    w_down,
    attn_gain,
    ffn_gain,
    router,
):
    *weights, own_tokens, own_meta = gather_weights(
        (w_query, key_weight, value_weight, w_out, w_gate, w_up, w_down),
        tokens[0].T,
        depths,
        seq_spans,
    )
    output, input_grad, small, *factors = run_block(
        own_tokens, cotangent[0].T, own_meta, (attn_gain[None], ffn_gain[None], router), weights
    )
    *sums, small_sum, input_grad = reduce_gradients(
        [x.reshape(RECUR * 128, -1) for x in factors], small, (input_grad,)
    )
    *gradients, d_attn, d_ffn, d_router, output, input_grad = unpack_gradients(
        sums, small_sum, input_grad, output
    )
    return (
        output.T[None],
        input_grad.T[None],
        *[x.reshape(-1) for x in gradients],
        d_attn[0],
        d_ffn[0],
        d_router,
    )


def solution(mesh):
    fits = mesh.shape["seq"] == 8 and mesh.shape["rep"] == 4
    placed = (
        P("rep", "seq", None),
        P("rep", "seq"),
        P("rep", None),
        P("rep", "seq", None),
        P(("seq", "rep")),
        P(("seq", "rep")),
        P(("seq", "rep")),
        P(("seq", "rep")),
        P(("seq", "rep")),
        P(("seq", "rep")),
        P(("seq", "rep")),
        P(),
        P(),
        P(),
    )
    return jax.shard_map(
        per_device_fast if fits else per_device,
        mesh=mesh,
        in_specs=placed,
        out_specs=(
            P("rep", "seq", None),
            P("rep", "seq", None),
            P(("seq", "rep")),
            P(("seq", "rep")),
            P(("seq", "rep")),
            P(("seq", "rep")),
            P(("seq", "rep")),
            P(("seq", "rep")),
            P(("seq", "rep")),
            P(),
            P(),
            P(),
        ),
        check_vma=False,
    )
```

```python
import jax
import jax.numpy as jnp
import numpy as np
from jax import lax
from jax.experimental import pallas as pl
from jax.experimental.pallas import tpu as pltpu
from jax.sharding import PartitionSpec as P

MODEL_WIDTH = 960
QUERY_HEADS = 15
KEY_VALUE_HEADS = 5
HEAD_SIZE = 64
FEEDFORWARD_UNITS = 2560
LOGC = 5
RECUR = 3
OWN_ROWS = 30
PADDED_ROWS = 32
PADDED_WIDTH = 1024


highest = lax.Precision.HIGHEST
epsilon = 1e-06
masked_score = -1e30


def passed_along(value, axis, steps):
    count = lax.axis_size(axis)
    initial, last = (max(0, -steps), min(count, count - steps))
    return lax.ppermute(value, axis, [(source, source + steps) for source in range(initial, last)])


def for_sending(x):

    def short(part):
        return part.astype(jnp.bfloat16) if part.dtype == jnp.float32 else part

    return jax.tree.map(short, x)


def unscaled_product(left, right):
    return jnp.dot(left, right, preferred_element_type=jnp.float32)


def left_product(left, right):
    return lax.dot_general(
        left, right, (((0,), (0,)), ((), ())), preferred_element_type=jnp.float32
    )


def right_product(left, right):
    return lax.dot_general(
        left, right, (((1,), (1,)), ((), ())), preferred_element_type=jnp.float32
    )


def rms_parts(vectors, gain):
    inv_rms = lax.rsqrt(jnp.mean(vectors * vectors, axis=-1, keepdims=True) + epsilon)
    normal_part = vectors * inv_rms
    return (normal_part * gain, normal_part, inv_rms)


def rms_backward(upstream, normal_part, inv_rms, gain):
    gain_grad = jnp.sum(upstream * normal_part, axis=0)
    scaled = upstream * gain
    inner = jnp.mean(scaled * normal_part, axis=-1, keepdims=True)
    return (inv_rms * (scaled - normal_part * inner), gain_grad)


def angle_tables(positions, width):
    half_width = width // 2
    frequency = 10000.0 ** (-jnp.arange(half_width, dtype=jnp.float32) / half_width)
    angle_grid = positions[:, None] * frequency[None, :]
    return (jnp.cos(angle_grid)[:, None, :], jnp.sin(angle_grid)[:, None, :])


def apply_rotation(vectors, cosine_table, sine_table):
    half_width = vectors.shape[-1] // 2
    front_half = vectors[..., :half_width]
    back_half = vectors[..., half_width:]
    return jnp.concatenate(
        [
            front_half * cosine_table - back_half * sine_table,
            back_half * cosine_table + front_half * sine_table,
        ],
        axis=-1,
    )


def masked_scores(query_b, keys_win, allowed):
    scores = (
        jnp.einsum("qgjd,kgd->gjqk", query_b, keys_win, preferred_element_type=jnp.float32) * 0.125
    )
    return jnp.where(allowed[None, None], scores, masked_score)


def per_device(
    tokens,
    depths,
    seq_spans,
    cotangent,
    w_query,
    key_weight,
    value_weight,
    w_out,
    w_gate,
    w_up,
    w_down,
    attn_gain,
    ffn_gain,
    router,
):
    narrow_float_type = jnp.bfloat16
    wide_float_type = jnp.float32
    count_of_rows = tokens.shape[1]
    query_groupings = QUERY_HEADS // KEY_VALUE_HEADS
    chain = lax.axis_size("seq")
    most_spans = min(2**LOGC, chain // 2)
    depth_levels = (most_spans - 1).bit_length()
    extra_rows = ((1 << depth_levels) - most_spans) * count_of_rows
    window = most_spans * count_of_rows
    target_tokens = (
        (MODEL_WIDTH, QUERY_HEADS * HEAD_SIZE),
        (MODEL_WIDTH, KEY_VALUE_HEADS * HEAD_SIZE),
        (MODEL_WIDTH, KEY_VALUE_HEADS * HEAD_SIZE),
        (QUERY_HEADS * HEAD_SIZE, MODEL_WIDTH),
        (MODEL_WIDTH, FEEDFORWARD_UNITS),
        (MODEL_WIDTH, FEEDFORWARD_UNITS),
        (FEEDFORWARD_UNITS, MODEL_WIDTH),
    )
    fetched = (
        lax.all_gather(w_query.astype(narrow_float_type), ("seq", "rep"), axis=0, tiled=True),
        lax.all_gather(key_weight.astype(narrow_float_type), ("seq", "rep"), axis=0, tiled=True),
        lax.all_gather(value_weight.astype(narrow_float_type), ("seq", "rep"), axis=0, tiled=True),
        lax.all_gather(w_out.astype(narrow_float_type), ("seq", "rep"), axis=0, tiled=True),
        lax.all_gather(w_gate.astype(narrow_float_type), ("seq", "rep"), axis=0, tiled=True),
        lax.all_gather(w_up.astype(narrow_float_type), ("seq", "rep"), axis=0, tiled=True),
        lax.all_gather(w_down.astype(narrow_float_type), ("seq", "rep"), axis=0, tiled=True),
    )
    attention_weights = tuple(
        (gathered.reshape(target) for gathered, target in zip(fetched, target_tokens))
    )
    place = lax.axis_index("seq")
    lengths = seq_spans[0]
    seq_ends = jnp.cumsum(lengths)
    span_ids = jnp.arange(chain, dtype=jnp.int32)
    owners = jnp.sum((seq_ends[None, :] <= span_ids[:, None]).astype(jnp.int32), axis=1)
    seq_starts = seq_ends - lengths
    numbers = jnp.arange(lengths.shape[0], dtype=jnp.int32)
    first_span = jnp.sum(
        jnp.where(numbers[None, :] == owners[:, None], seq_starts[None, :], 0), axis=1
    )
    index_of_span = jnp.sum(jnp.where(span_ids == place, span_ids - first_span, 0))
    positions = (index_of_span * count_of_rows + jnp.arange(count_of_rows, dtype=jnp.int32)).astype(
        wide_float_type
    )
    cosine_table, sine_table = angle_tables(positions, HEAD_SIZE)
    row_ids = jnp.arange(count_of_rows, dtype=jnp.int32)
    col_ids = jnp.arange(window, dtype=jnp.int32)
    offsets = most_spans - 1 - col_ids // count_of_rows
    local_col = col_ids - (most_spans - 1) * count_of_rows
    causal = jnp.where(offsets[None, :] == 0, local_col[None, :] <= row_ids[:, None], True)
    diagonal = (offsets[None, :] == 0) & (local_col[None, :] == row_ids[:, None])
    span_ok = (index_of_span >= offsets)[None, :]
    active_all = (depths[0][None, :] > jnp.arange(RECUR, dtype=jnp.int32)[:, None]).astype(
        wide_float_type
    )
    hidden_state = tokens[0].astype(wide_float_type)
    saved = []
    for recursion in range(RECUR):
        current_active = active_all[recursion]
        normalized_input, normal_a, inv_a = rms_parts(hidden_state, attn_gain)
        normalized_input_copy = normalized_input.astype(narrow_float_type)
        raw_query = unscaled_product(normalized_input_copy, attention_weights[0]).reshape(
            count_of_rows, QUERY_HEADS, HEAD_SIZE
        )
        query_b = (
            apply_rotation(raw_query, cosine_table, sine_table)
            .astype(narrow_float_type)
            .reshape(count_of_rows, KEY_VALUE_HEADS, query_groupings, HEAD_SIZE)
        )
        unrotated_key = unscaled_product(normalized_input_copy, attention_weights[1]).reshape(
            count_of_rows, KEY_VALUE_HEADS, HEAD_SIZE
        )
        key_b = apply_rotation(unrotated_key, cosine_table, sine_table).astype(narrow_float_type)
        value_copy = (
            unscaled_product(normalized_input_copy, attention_weights[2])
            .astype(narrow_float_type)
            .reshape(count_of_rows, KEY_VALUE_HEADS, HEAD_SIZE)
        )
        active_b = current_active.astype(narrow_float_type)
        keys_win = key_b
        values_win = value_copy
        active_win = active_b
        for level in range(depth_levels):
            far_key, far_value, far_active = passed_along(
                (keys_win, values_win, active_win), "seq", 1 << level
            )
            keys_win = jnp.concatenate([far_key, keys_win], axis=0)
            values_win = jnp.concatenate([far_value, values_win], axis=0)
            active_win = jnp.concatenate([far_active, active_win], axis=0)
        allowed = span_ok & causal & ((active_win > 0)[None, :] | diagonal)
        scores = masked_scores(query_b, keys_win, allowed)
        row_max = jnp.max(scores, axis=-1, keepdims=True)
        expon = jnp.exp(scores - row_max)
        row_total = jnp.sum(expon, axis=-1, keepdims=True)
        probs_b = (expon / row_total).astype(narrow_float_type)
        log_total = row_max + jnp.log(row_total)
        attended_b = (
            jnp.einsum(
                "gjqk,kgd->qgjd", probs_b, values_win, preferred_element_type=wide_float_type
            )
            .astype(narrow_float_type)
            .reshape(count_of_rows, QUERY_HEADS * HEAD_SIZE)
        )
        branch = unscaled_product(attended_b, attention_weights[3])
        middle = hidden_state + branch
        second, normal_z, inv_z = rms_parts(middle, ffn_gain)
        second_b = second.astype(narrow_float_type)
        gate_value = unscaled_product(second_b, attention_weights[4])
        up_value = unscaled_product(second_b, attention_weights[5])
        hidden_b = (jax.nn.silu(gate_value) * up_value).astype(narrow_float_type)
        ffn_out = unscaled_product(hidden_b, attention_weights[6])
        weight_gate = jax.nn.sigmoid(jnp.dot(hidden_state, router[recursion], precision=highest))
        saved.append(
            (
                hidden_state,
                normalized_input_copy,
                normal_a,
                inv_a,
                query_b,
                keys_win,
                values_win,
                allowed,
                log_total,
                attended_b,
                branch,
                normal_z,
                inv_z,
                second_b,
                gate_value,
                up_value,
                hidden_b,
                ffn_out,
                weight_gate,
                current_active,
            )
        )
        hidden_state = hidden_state + (current_active * weight_gate)[:, None] * (branch + ffn_out)
    output = hidden_state.astype(narrow_float_type)
    refetched = (
        lax.all_gather(w_query.astype(narrow_float_type), ("seq", "rep"), axis=0, tiled=True),
        lax.all_gather(key_weight.astype(narrow_float_type), ("seq", "rep"), axis=0, tiled=True),
        lax.all_gather(value_weight.astype(narrow_float_type), ("seq", "rep"), axis=0, tiled=True),
        lax.all_gather(w_out.astype(narrow_float_type), ("seq", "rep"), axis=0, tiled=True),
        lax.all_gather(w_gate.astype(narrow_float_type), ("seq", "rep"), axis=0, tiled=True),
        lax.all_gather(w_up.astype(narrow_float_type), ("seq", "rep"), axis=0, tiled=True),
        lax.all_gather(w_down.astype(narrow_float_type), ("seq", "rep"), axis=0, tiled=True),
    )
    back_weights = tuple(
        (gathered.reshape(target) for gathered, target in zip(refetched, target_tokens))
    )
    master_shapes = (w_query, key_weight, value_weight, w_out, w_gate, w_up, w_down)
    shares = tuple((jnp.zeros_like(master) for master in master_shapes))
    gain_a_total = jnp.zeros((MODEL_WIDTH,), wide_float_type)
    gain_f_total = jnp.zeros((MODEL_WIDTH,), wide_float_type)
    router_rows = [None] * RECUR
    grad_state = cotangent[0].astype(wide_float_type)
    for recursion in reversed(range(RECUR)):
        (
            state_in,
            normalized_input_copy,
            normal_a,
            inv_a,
            query_b,
            keys_win,
            values_win,
            allowed,
            log_total,
            attended_b,
            branch,
            normal_z,
            inv_z,
            second_b,
            gate_value,
            up_value,
            hidden_b,
            ffn_out,
            weight_gate,
            current_active,
        ) = saved[recursion]
        mixing = current_active * weight_gate
        grad_delta = mixing[:, None] * grad_state
        grad_mix = jnp.sum(grad_state * (branch + ffn_out), axis=-1)
        grad_logit = current_active * grad_mix * weight_gate * (1.0 - weight_gate)
        router_rows[recursion] = jnp.dot(grad_logit, state_in, precision=highest)
        grad_next = grad_state + grad_logit[:, None] * router[recursion][None, :]
        ffn_grad_b = grad_delta.astype(narrow_float_type)
        grad_hidden = right_product(ffn_grad_b, back_weights[6])
        d_down = left_product(hidden_b, ffn_grad_b)
        sigmoid_gate = jax.nn.sigmoid(gate_value)
        grad_gate_b = (
            grad_hidden * up_value * sigmoid_gate * (1.0 + gate_value * (1.0 - sigmoid_gate))
        ).astype(narrow_float_type)
        grad_up_b = (grad_hidden * gate_value * sigmoid_gate).astype(narrow_float_type)
        grad_second = right_product(grad_gate_b, back_weights[4]) + right_product(
            grad_up_b, back_weights[5]
        )
        d_gate = left_product(second_b, grad_gate_b)
        d_up = left_product(second_b, grad_up_b)
        grad_middle, gain_f_part = rms_backward(grad_second, normal_z, inv_z, ffn_gain)
        gain_f_total = gain_f_total + gain_f_part
        grad_branch_b = (grad_delta + grad_middle).astype(narrow_float_type)
        grad_attended_b = (
            right_product(grad_branch_b, back_weights[3])
            .astype(narrow_float_type)
            .reshape(count_of_rows, KEY_VALUE_HEADS, query_groupings, HEAD_SIZE)
        )
        d_out = left_product(attended_b, grad_branch_b)
        grad_next = grad_next + grad_middle
        scores = masked_scores(query_b, keys_win, allowed)
        probs = jnp.exp(scores - log_total)
        probs_b = probs.astype(narrow_float_type)
        grad_probs = jnp.einsum(
            "qgjd,kgd->gjqk", grad_attended_b, values_win, preferred_element_type=wide_float_type
        )
        row_dot = jnp.sum(probs * grad_probs, axis=-1, keepdims=True)
        grad_scores_b = (probs * (grad_probs - row_dot)).astype(narrow_float_type)
        grad_queries = (
            jnp.einsum(
                "gjqk,kgd->qgjd", grad_scores_b, keys_win, preferred_element_type=wide_float_type
            )
            * 0.125
        )
        grad_keys = (
            jnp.einsum(
                "gjqk,qgjd->kgd", grad_scores_b, query_b, preferred_element_type=wide_float_type
            )
            * 0.125
        )
        grad_values = jnp.einsum(
            "gjqk,qgjd->kgd", probs_b, grad_attended_b, preferred_element_type=wide_float_type
        )
        extra_zero_rows = jnp.zeros((extra_rows, KEY_VALUE_HEADS, HEAD_SIZE), wide_float_type)
        local_span_keys = jnp.concatenate([extra_zero_rows, grad_keys], axis=0)
        local_span_values = jnp.concatenate([extra_zero_rows, grad_values], axis=0)
        for level in reversed(range(depth_levels)):
            older_rows = (1 << level) * count_of_rows
            back_keys, back_values = passed_along(
                (
                    for_sending(local_span_keys[:older_rows]),
                    for_sending(local_span_values[:older_rows]),
                ),
                "seq",
                -(1 << level),
            )
            local_span_keys = local_span_keys[older_rows:] + back_keys
            local_span_values = local_span_values[older_rows:] + back_values
        grad_query_b = (
            apply_rotation(
                grad_queries.reshape(count_of_rows, QUERY_HEADS, HEAD_SIZE),
                cosine_table,
                -sine_table,
            )
            .astype(narrow_float_type)
            .reshape(count_of_rows, QUERY_HEADS * HEAD_SIZE)
        )
        grad_key_b = (
            apply_rotation(local_span_keys, cosine_table, -sine_table)
            .astype(narrow_float_type)
            .reshape(count_of_rows, KEY_VALUE_HEADS * HEAD_SIZE)
        )
        value_gradient_copy = local_span_values.astype(narrow_float_type).reshape(
            count_of_rows, KEY_VALUE_HEADS * HEAD_SIZE
        )
        grad_normed = (
            right_product(grad_query_b, back_weights[0])
            + right_product(grad_key_b, back_weights[1])
            + right_product(value_gradient_copy, back_weights[2])
        )
        d_query = left_product(normalized_input_copy, grad_query_b)
        d_key = left_product(normalized_input_copy, grad_key_b)
        d_value = left_product(normalized_input_copy, value_gradient_copy)
        grad_input, gain_a_part = rms_backward(grad_normed, normal_a, inv_a, attn_gain)
        gain_a_total = gain_a_total + gain_a_part
        grad_state = grad_next + grad_input
        local_grads = (
            d_query.reshape(-1),
            d_key.reshape(-1),
            d_value.reshape(-1),
            d_out.reshape(-1),
            d_gate.reshape(-1),
            d_up.reshape(-1),
            d_down.reshape(-1),
        )
        summed = (
            lax.psum_scatter(local_grads[0], ("seq", "rep"), scatter_dimension=0, tiled=True),
            lax.psum_scatter(local_grads[1], ("seq", "rep"), scatter_dimension=0, tiled=True),
            lax.psum_scatter(local_grads[2], ("seq", "rep"), scatter_dimension=0, tiled=True),
            lax.psum_scatter(local_grads[3], ("seq", "rep"), scatter_dimension=0, tiled=True),
            lax.psum_scatter(local_grads[4], ("seq", "rep"), scatter_dimension=0, tiled=True),
            lax.psum_scatter(local_grads[5], ("seq", "rep"), scatter_dimension=0, tiled=True),
            lax.psum_scatter(local_grads[6], ("seq", "rep"), scatter_dimension=0, tiled=True),
        )
        shares = tuple((old_share + new_share for old_share, new_share in zip(shares, summed)))
    router_grad = jnp.stack(router_rows, axis=0)
    gain_a_sum, gain_f_sum, router_sum = lax.psum(
        (gain_a_total, gain_f_total, router_grad), ("seq", "rep")
    )
    return (
        output[None],
        grad_state[None],
        shares[0],
        shares[1],
        shares[2],
        shares[3],
        shares[4],
        shares[5],
        shares[6],
        gain_a_sum,
        gain_f_sum,
        router_sum,
    )


MESH = pl.DeviceIdType.MESH
N_Z = 4
BLOCKS = ((32, 2816), (32, 2560), (32, 2560), (80, 1024))
GATHER_ORDERS = ("uzw", "zuw", "uzw", "zuw")
REDUCE_ORDERS = ("uzw", "uzw", "zuw", "zuw")


def place():
    seq = lax.axis_index("seq")
    rep = lax.axis_index("rep")
    z, x, y, core = seq // 2, seq % 2, rep // 2, rep % 2
    return z, x + core * (y - x), y + core * (x - y), core


def device_of(z, u, w, core):
    x, y = u + core * (w - u), w + core * (u - w)
    return (z * 2 + x, y * 2 + core)


def block_of(z, u, w, core):
    seq, rep = device_of(z, u, w, core)
    return seq * 4 + rep


def remote(src, dst, send_sem, recv_sem, device):
    return pltpu.make_async_remote_copy(
        src_ref=src,
        dst_ref=dst,
        send_sem=send_sem,
        recv_sem=recv_sem,
        device_id=device,
        device_id_type=MESH,
    )


def gather_events():
    events = [("own", group) for group in (1, 2, 0, 3)]
    for step in range(6):
        for group in range(4):
            if GATHER_ORDERS[group] == "zuw":
                if 1 <= step <= 3:
                    events.append(("z", group, step, 0))
                if 1 <= step <= 4:
                    events.append(("u", group, step - 1))
                    events.append(("w", group, step - 1, 0))
                if 2 <= step <= 5:
                    events.append(("w", group, step - 2, 1))
            else:
                if step == 1:
                    events.append(("first", group))
                if 1 <= step <= 3:
                    events.append(("z", group, step, 0))
                if 2 <= step <= 4:
                    events.append(("z", group, step - 1, 1))
                if 1 <= step <= 4:
                    events.append(("w", group, step - 1, 0))
                if 2 <= step <= 5:
                    events.append(("w", group, step - 2, 1))
    return events


def move_partners():
    seq, rep = lax.axis_index("seq"), lax.axis_index("rep")
    apart = (seq * 4 + rep) * (seq * 4 + rep - 13)
    return device_of_span(rep, seq), span_of_device()[::-1], (apart * apart + 999999) // 1000000


def start_moves(leaving, arriving, send_sem, recv_sem, target, moves):
    for i, (src, dst) in enumerate(zip(leaving, arriving)):

        @pl.when(moves == 1)
        def _():
            remote(src, dst, send_sem.at[i], recv_sem.at[i], target).start()

        @pl.when(moves == 0)
        def _():
            pltpu.make_async_copy(src, dst, recv_sem.at[i]).start()


def wait_moves(leaving, arriving, send_sem, recv_sem, target, moves):
    for i, (src, dst) in enumerate(zip(leaving, arriving)):

        @pl.when(moves == 1)
        def _():
            remote(src, dst, send_sem.at[i], recv_sem.at[i], target).wait()

        @pl.when(moves == 0)
        def _():
            pltpu.make_async_copy(src, dst, recv_sem.at[i]).wait()


def set_meta(meta, depths, spans):
    own = lax.axis_index("seq")
    first, end = 0, 0
    for sequence in range(spans.shape[1]):
        end = end + spans[0, sequence]
        first = jnp.where(end <= own, end, first)
    row = lax.broadcasted_iota(jnp.int32, (8, 128), 0)
    values = jnp.where(row == 0, depths[...], jnp.where(row == 1, own - first, 0))
    meta[...] = values.astype(jnp.float32)


def gather_kernel(*refs):
    flat_in, tokens, depths, spans, places = refs[:7], refs[7], refs[8], refs[9], refs[10]
    full, arriving = refs[11:15], refs[15:17]
    flat, own, meta = refs[17:24], refs[24:28], refs[28]
    spread, tiles, natural, long_rows = refs[29:33]
    recv_sem, z_sem, u_sem, w_sem, core_sem, local_sem, move_send, move_recv, flat_sem = refs[33:]
    leaving = (tokens, meta)
    z, u, w, core = place()
    me = block_of(z, u, w, core)
    target, source, moves = move_partners()
    above, below = device_of(z + 1, u, w, core), device_of(z - 1, u, w, core)
    across_u, across_w = device_of(z, 1 - u, w, core), device_of(z, u, 1 - w, core)
    sibling = device_of(z, w, u, 1 - core)

    loads = [
        pltpu.make_async_copy(src, dst, flat_sem.at[i])
        for i, (src, dst) in enumerate(zip(flat_in, flat))
    ]
    for copy in loads:
        copy.start()
    barrier = pltpu.get_barrier_semaphore()
    for device in (across_u, across_w, sibling):
        pl.semaphore_signal(barrier, inc=1, device_id=device, device_id_type=MESH)

    @pl.when(moves == 1)
    def _():
        pl.semaphore_signal(barrier, inc=1, device_id=target, device_id_type=MESH)
        pl.semaphore_signal(barrier, inc=1, device_id=source, device_id_type=MESH)

    @pl.when(z < N_Z - 1)
    def _():
        pl.semaphore_signal(barrier, inc=1, device_id=above, device_id_type=MESH)

    @pl.when(z > 0)
    def _():
        pl.semaphore_signal(barrier, inc=1, device_id=below, device_id_type=MESH)

    set_meta(meta, depths, spans)
    for copy in loads:
        copy.wait()
    pack_wide(flat, own, tiles)
    pl.semaphore_wait(barrier, 4 + (z + 1) // 2 - z // 3 * 2 + 2 * moves)

    def rows(group, block):
        count = BLOCKS[group][0]
        return full[group].at[pl.ds(pl.multiple_of(block * count, 16), count)]

    def copy(group, block, src, send_sem, device):
        return remote(src, rows(group, block), send_sem, recv_sem.at[group, block], device)

    def send(group, block, src, ways, slot=0):
        if "z" in ways:

            @pl.when(z < N_Z - 1)
            def _():
                copy(group, block, src, z_sem.at[group, 0, slot], above).start()

            @pl.when(z > 0)
            def _():
                copy(group, block, src, z_sem.at[group, 1, slot], below).start()

        if "+" in ways:

            @pl.when(z < N_Z - 1)
            def _():
                copy(group, block, src, z_sem.at[group, 0, slot], above).start()

        if "-" in ways:

            @pl.when(z > 0)
            def _():
                copy(group, block, src, z_sem.at[group, 1, slot], below).start()

        if "u" in ways:
            copy(group, block, src, u_sem.at[group], across_u).start()
        if "w" in ways:
            copy(group, block, src, w_sem.at[group], across_w).start()
        if "c" in ways:
            copy(group, block, src, core_sem.at[group], sibling).start()

    def passed_on(group, block, ways, slot=0):
        copy(group, block, rows(group, block), core_sem.at[group], sibling).wait_recv()
        send(group, block, rows(group, block), ways, slot)

    def at_distance(step, action):
        if step == 0:
            action(z, "")
            return

        @pl.when(z - step >= 0)
        def _():
            action(z - step, "+")

        @pl.when(z + step < N_Z)
        def _():
            action(z + step, "-")

    def own_event(group):
        send(group, me, own[group], "zuwc")
        pltpu.make_async_copy(own[group], rows(group, me), local_sem.at[group]).start()

    def first_event(group):
        passed_on(group, block_of(z, 1 - u, w, core), "zwc", 1)

    def z_event(group, step, other):
        z_first = GATHER_ORDERS[group] == "zuw"
        column = 1 - u if other else u
        slot = step if z_first else 2 * step + other
        at_distance(
            step,
            lambda far, way: passed_on(
                group,
                block_of(far, column, w, core),
                way + ("uwc" if z_first else "wc"),
                slot,
            ),
        )

    def u_event(group, step):
        at_distance(
            step, lambda far, way: passed_on(group, block_of(far, 1 - u, w, core), "wc")
        )

    def w_event(group, step, other):
        column = 1 - u if other else u
        at_distance(
            step, lambda far, way: passed_on(group, block_of(far, column, 1 - w, core), "c")
        )

    actions = {"own": own_event, "first": first_event, "z": z_event, "u": u_event, "w": w_event}
    for event in gather_events():
        if event == ("own", 0):
            fill_spread(spread, places)
            pack_rest(flat, own, spread, tiles, natural, long_rows)
        if event == ("z", 0, 1, 0):
            start_moves(leaving, arriving, move_send, move_recv, target, moves)
        actions[event[0]](*event[1:])
    wait_moves(leaving, arriving, move_send, move_recv, target, moves)

    for group in range(4):
        z_first = GATHER_ORDERS[group] == "zuw"
        count = BLOCKS[group][0]
        pltpu.make_async_copy(own[group], rows(group, me), local_sem.at[group]).wait()

        @pl.loop(0, 16)
        def _(i):
            block = i * 2 + (1 - core)
            copy(group, block, rows(group, block), core_sem.at[group], sibling).wait_recv()

        for sem, sends in ((u_sem, 4 if z_first else 1), (w_sem, 8), (core_sem, 16)):
            part = full[group].at[pl.ds(0, sends * count)]
            remote(part, part, sem.at[group], recv_sem.at[group, 0], sibling).wait_send()
        for step in range(N_Z):
            for other in (0,) if z_first else (0, 1):
                slot = step if z_first else 2 * step + other

                @pl.when((z - step >= 0) & (z < N_Z - 1))
                def _():
                    copy(group, me, own[group], z_sem.at[group, 0, slot], above).wait_send()

                @pl.when((z + step < N_Z) & (z > 0))
                def _():
                    copy(group, me, own[group], z_sem.at[group, 1, slot], below).wait_send()


def gather_weights(flat, tokens, depths, spans):
    narrow, wide, vmem, sems = jnp.bfloat16, jnp.float32, pltpu.VMEM, pltpu.SemaphoreType.DMA
    anywhere, here = pl.BlockSpec(memory_space=pl.ANY), pl.BlockSpec(memory_space=vmem)
    flat = [x.reshape(-1, 128) for x in flat]
    return pl.pallas_call(
        gather_kernel,
        out_shape=[jax.ShapeDtypeStruct((32 * rows, columns), narrow) for rows, columns in BLOCKS]
        + [jax.ShapeDtypeStruct(tokens.shape, narrow), jax.ShapeDtypeStruct((8, 128), wide)],
        in_specs=[anywhere] * 8 + [here, pl.BlockSpec(memory_space=pltpu.SMEM), here],
        out_specs=[anywhere] * 6,
        scratch_shapes=[vmem(x.shape, wide) for x in flat]
        + [vmem(shape, narrow) for shape in BLOCKS]
        + [
            vmem((8, 128), wide),
            vmem((MODEL_WIDTH, 1024), narrow),
            vmem((20, 32, 128), wide),
            vmem((8, 32, 128), wide),
            vmem((8, 80, 128), wide),
            sems((4, 32)),
            sems((4, 2, 8)),
            sems((4,)),
            sems((4,)),
            sems((4,)),
            sems((4,)),
            sems((2,)),
            sems((2,)),
            sems((7,)),
        ],
        compiler_params=pltpu.CompilerParams(
            collective_id=1, has_side_effects=True, vmem_limit_bytes=59 * 2**20
        ),
        name="gather_weights",
    )(*flat, tokens, depths, spans, natural_places())


REDUCE_STEPS = (
    ("make", 2, 2),
    ("make", 2, 1),
    ("small", -1),
    ("w", 2, 2),
    ("make", 0, 3),
    ("w", 0, 3),
    ("make", 1, 3),
    ("make", 2, 3),
    ("w", 1, 3),
    ("u", 2, 2),
    ("make", 0, 2),
    ("w", 2, 1),
    ("z_early", 1, 3, 1),
    ("make", 3, 3),
    ("w", 0, 2),
    ("z_early", 1, 3, 0),
    ("w", 3, 3),
    ("w", 2, 3),
    ("z_early", 0, 3, 1),
    ("make", 0, 1),
    ("make", 1, 1),
    ("z_early", 0, 3, 0),
    ("make", 3, 1),
    ("small", 0),
    ("w", 0, 1),
    ("w", 1, 1),
    ("z_early", 0, 2, 0),
    ("make", 1, 2),
    ("z_early", 0, 2, 1),
    ("make", 3, 2),
    ("u", 2, 1),
    ("u", 2, 3),
    ("z_early", 0, 1, 0),
    ("w", 1, 2),
    ("z_early", 0, 1, 1),
    ("small", 1),
    ("w", 3, 1),
    ("z_early", 1, 2, 1),
    ("z_late", 2, 3),
    ("u", 3, 3),
    ("w", 3, 2),
    ("make", 2, 0),
    ("u", 3, 1),
    ("make", 1, 0),
    ("z_late", 2, 2),
    ("z_early", 1, 1, 1),
    ("w", 2, 0),
    ("make", 0, 0),
    ("w", 1, 0),
    ("make", 3, 0),
    ("z_early", 1, 2, 0),
    ("w", 0, 0),
    ("z_late", 2, 1),
    ("small", 2),
    ("z_early", 1, 1, 0),
    ("u", 3, 2),
    ("z_early", 0, 0, 1),
    ("z_late", 3, 3),
    ("small", 3),
    ("z_early", 0, 0, 0),
    ("z_early", 1, 0, 1),
    ("z_early", 1, 0, 0),
    ("w", 3, 0),
    ("u", 2, 0),
    ("z_late", 3, 2),
    ("u_late", 1),
    ("u", 3, 0),
    ("z_late", 3, 1),
    ("small", 4),
    ("u_late", 0),
    ("z_late", 2, 0),
    ("z_late", 3, 0),
)


def reduce_kernel(*refs):
    factors_in, small_in, leaving = refs[:9], refs[9], refs[10:11]
    final, small_out, arriving = refs[11:15], refs[15], refs[16:17]
    part, from_core, from_w, from_u, from_z = (refs[17 + 4 * i : 21 + 4 * i] for i in range(5))
    factors, turned = refs[37:46], refs[46]
    small_held, small_got = refs[47:49]
    (
        load_sem,
        core_send,
        core_recv,
        w_send,
        w_recv,
        u_send,
        u_recv,
        z_send,
        z_recv,
        small_send,
        small_recv,
        move_send,
        move_recv,
    ) = refs[49:]
    source, target, moves = move_partners()
    z, u, w, core = place()
    me = block_of(z, u, w, core)
    above, below = device_of(z + 1, u, w, core), device_of(z - 1, u, w, core)
    across_u, across_w = device_of(z, 1 - u, w, core), device_of(z, u, 1 - w, core)
    sibling = device_of(z, w, u, 1 - core)
    near, far_z = z + 1 - 2 * (z % 2), (z + 2) % 4
    partners = (
        sibling,
        across_u,
        across_w,
        device_of(near, u, w, core),
        device_of(far_z, u, w, core),
    )
    middle_z = (z == 1) | (z == 2)

    barrier = pltpu.get_barrier_semaphore()
    for device in partners:
        pl.semaphore_signal(barrier, inc=1, device_id=device, device_id_type=MESH)

    @pl.when(moves == 1)
    def _():
        pl.semaphore_signal(barrier, inc=1, device_id=target, device_id_type=MESH)
        pl.semaphore_signal(barrier, inc=1, device_id=source, device_id_type=MESH)

    @pl.when(middle_z)
    def _():
        pl.semaphore_signal(
            barrier, inc=1, device_id=device_of(3 - z, u, w, core), device_id_type=MESH
        )

    def load(i):
        return pltpu.make_async_copy(factors_in[i], factors[i], load_sem.at[i])

    loaded = set()
    for i in LOAD_ORDER:
        load(i).start()

    pl.semaphore_wait(barrier, 5 + (z + 1) // 2 - z // 3 * 2 + 2 * moves)

    def rows(group, block):
        count = BLOCKS[group][0]
        return part[group].at[pl.ds(pl.multiple_of(block * count, 16), count)]

    def slot_of(far, column, line):
        return (far * 2 + column) * 2 + line

    def small_copy(i):
        return remote(
            small_held.at[i], small_got.at[i], small_send.at[i], small_recv.at[i], partners[i]
        )

    def small_event(i):
        if i < 0:
            small_held[0] = small_in[...]
            small_copy(0).start()
            return
        small_copy(i).wait_recv()
        total = small_held[i] + small_got[i]
        if i < 4:
            small_held[i + 1] = total
            small_copy(i + 1).start()
        else:
            small_out[...] = total

    def product(group, plane, left, right, first, width, chunk):
        count = 8 * BLOCKS[group][0]
        at = pl.multiple_of(plane * count, 128)
        turned[0:count, :] = factors[left][:, pl.ds(at, count)].T

        @pl.loop(0, width // chunk)
        def _(j):
            here = pl.multiple_of(j * chunk, 128)
            there = pl.multiple_of(first + j * chunk, 128)
            part[group][pl.ds(at, count), pl.ds(there, chunk)] = jnp.dot(
                turned[0:count, :],
                factors[right][:, pl.ds(here, chunk)],
                preferred_element_type=jnp.float32,
            ).astype(jnp.bfloat16)

    def make_event(group, step):
        for i in NEEDED[group]:
            if i not in loaded:
                load(i).wait()
                loaded.add(i)

        plane = (z, z + 1 - 2 * (z % 2), (z + 2) % 4, 3 - z)[step]
        for left, right, first, width, chunk in PRODUCTS[group]:
            product(group, plane, left, right, first, width, chunk)
        for column in (0, 1):
            for line in (0, 1):
                slot = slot_of(plane, column, line)
                remote(
                    rows(group, block_of(plane, column, line, 1 - core)),
                    from_core[group].at[slot],
                    core_send.at[group],
                    core_recv.at[group, slot],
                    sibling,
                ).start()

    def wait_core(group, slot):
        held = from_core[group].at[slot]
        remote(held, held, core_send.at[group], core_recv.at[group, slot], sibling).wait_recv()

    def accumulate(group, block, terms):
        count = BLOCKS[group][0]
        first = pl.multiple_of(block * count, 16)

        @pl.loop(0, count // 16)
        def _(i):
            at = pl.multiple_of(i * 16, 16)
            total = part[group][pl.ds(first + at, 16), :].astype(jnp.float32)
            for ref, slot in terms:
                total = total + ref[slot, pl.ds(at, 16), :].astype(jnp.float32)
            part[group][pl.ds(first + at, 16), :] = total.astype(jnp.bfloat16)

    def at_distance(step, action):
        if step == 0:
            action(z, 0)
            return

        @pl.when(z + step < N_Z)
        def _():
            action(z + step, 1)

        @pl.when(z - step >= 0)
        def _():
            action(z - step, -1)

    def wait_w(group, slot):
        held = from_w[group].at[slot]
        remote(held, held, w_send.at[group], w_recv.at[group, slot], across_w).wait_recv()

    def w_event(group, step):
        def action(far, way, column):
            block, slot = block_of(far, column, 1 - w, core), slot_of(far, column, 1 - w)
            wait_core(group, slot)
            accumulate(group, block, [(from_core[group], slot)])
            remote(
                rows(group, block),
                from_w[group].at[far * 2 + column],
                w_send.at[group],
                w_recv.at[group, far * 2 + column],
                across_w,
            ).start()

        for column in (1 - u, u):
            at_distance(step, lambda far, way: action(far, way, column))

    def gathered(group, far, column):
        slot = slot_of(far, column, w)
        wait_core(group, slot)
        wait_w(group, far * 2 + column)
        return [(from_core[group], slot), (from_w[group], far * 2 + column)]

    def u_copy(group, src, slot):
        return remote(
            src, from_u[group].at[slot], u_send.at[group], u_recv.at[group, slot], across_u
        )

    def u_event(group, step):
        def action(far, way):
            block = block_of(far, 1 - u, w, core)
            accumulate(group, block, gathered(group, far, 1 - u))
            u_copy(group, rows(group, block), far).start()

        at_distance(step, action)

    def z_copy(group, block, way, slot):
        return remote(
            rows(group, block),
            from_z[group].at[slot],
            z_send.at[group, way, slot],
            z_recv.at[group, slot],
            below if way else above,
        )

    def z_take(group, block, way, slot):
        z_copy(group, block, way, slot).wait_recv()
        accumulate(group, block, [(from_z[group], slot)])

    def z_step(group, step, column, z_slot, terms_of):
        def action(far, way):
            block = block_of(far, column, w, core)
            accumulate(group, block, terms_of(far))
            if way >= 0:

                @pl.when(z > 0)
                def _():
                    z_take(group, block, 0, z_slot(far))

            if way <= 0:

                @pl.when(z < N_Z - 1)
                def _():
                    z_take(group, block, 1, z_slot(far if way else 4))

            if way:
                slot = z_slot(4 if way < 0 and step == 1 else far)
                z_copy(group, block, 0 if way > 0 else 1, slot).start()

        at_distance(step, action)

    def finish(group):
        count = BLOCKS[group][0]
        final[group][...] = part[group][
            pl.ds(pl.multiple_of(me * count, 16), count), :
        ].astype(jnp.float32)

    def z_late_event(group, step):
        def terms_of(far):
            terms = gathered(group, far, u)
            u_copy(group, from_u[group].at[far], far).wait_recv()
            return terms + [(from_u[group], far)]

        z_step(group, step, u, lambda far: far, terms_of)
        if step == 0:
            finish(group)

    def z_early_event(group, step, other):
        column = 1 - u if other else u
        z_step(
            group,
            step,
            column,
            lambda far: far * 2 + column,
            lambda far: gathered(group, far, column),
        )
        if step == 0 and other:
            u_copy(group, rows(group, block_of(z, 1 - u, w, core)), 0).start()

    def u_late_event(group):
        u_copy(group, from_u[group].at[0], 0).wait_recv()
        accumulate(group, me, [(from_u[group], 0)])
        finish(group)

    actions = {
        "small": small_event,
        "make": make_event,
        "w": w_event,
        "u": u_event,
        "z_early": z_early_event,
        "z_late": z_late_event,
        "u_late": u_late_event,
    }
    for event in REDUCE_STEPS:
        actions[event[0]](*event[1:])
        if event == REDUCE_STEPS[20]:
            start_moves(leaving, arriving, move_send, move_recv, target, moves)
    wait_moves(leaving, arriving, move_send, move_recv, target, moves)

    for group in range(4):
        z_first = REDUCE_ORDERS[group] == "zuw"
        count = BLOCKS[group][0]
        for sem, sends in ((core_send, 16), (w_send, 8), (u_send, 4 if z_first else 1)):
            rows_sent = part[group].at[pl.ds(0, sends * count)]
            remote(
                rows_sent, rows_sent, sem.at[group], core_recv.at[group, 0], sibling
            ).wait_send()
        for far in range(N_Z):
            for column in (0,) if z_first else (0, 1):
                slot = far if z_first else far * 2 + column

                @pl.when(z < far)
                def _():
                    z_copy(group, me, 0, slot).wait_send()

                @pl.when(z > far + 1)
                def _():
                    z_copy(group, me, 1, slot).wait_send()

        for column in (0,) if z_first else (0, 1):

            @pl.when(z > 0)
            def _():
                z_copy(group, me, 1, 4 if z_first else 8 + column).wait_send()

    for i in range(5):
        small_copy(i).wait_send()


LOAD_ORDER = (4, 6, 0, 1, 2, 3, 5, 7, 8)
NEEDED = ((0, 1, 2, 3), (4, 5), (4, 6), (7, 8))
PRODUCTS = (
    ((0, 1, 0, 1792, 256), (2, 3, 1792, 1024, 512)),
    ((4, 5, 0, 2560, 512),),
    ((4, 6, 0, 2560, 512),),
    ((7, 8, 0, 1024, 512),),
)


def reduce_gradients(factors, small, leaving):
    narrow, sems, vmem = jnp.bfloat16, pltpu.SemaphoreType.DMA, pltpu.VMEM
    z_first = [order == "zuw" for order in REDUCE_ORDERS]
    scratch = [vmem((32 * rows, columns), narrow) for rows, columns in BLOCKS]
    scratch += [vmem((16, rows, columns), narrow) for rows, columns in BLOCKS]
    scratch += [vmem((8, rows, columns), narrow) for rows, columns in BLOCKS]
    scratch += [
        vmem((4 if first else 1, rows, columns), narrow)
        for (rows, columns), first in zip(BLOCKS, z_first)
    ]
    scratch += [
        vmem((5 if first else 10, rows, columns), narrow)
        for (rows, columns), first in zip(BLOCKS, z_first)
    ]
    scratch += [vmem(x.shape, narrow) for x in factors]
    scratch += [vmem((640, RECUR * 128), narrow)]
    scratch += [vmem((5, 8, 1024), jnp.float32)] * 2
    scratch += [
        sems((9,)),
        sems((4,)),
        sems((4, 16)),
        sems((4,)),
        sems((4, 8)),
        sems((4,)),
        sems((4, 4)),
        sems((4, 2, 10)),
        sems((4, 10)),
        sems((5,)),
        sems((5,)),
        sems((1,)),
        sems((1,)),
    ]
    anywhere, here = pl.BlockSpec(memory_space=pl.ANY), pl.BlockSpec(memory_space=vmem)
    return pl.pallas_call(
        reduce_kernel,
        out_shape=[jax.ShapeDtypeStruct(shape, jnp.float32) for shape in BLOCKS]
        + [jax.ShapeDtypeStruct((8, 1024), jnp.float32)]
        + [jax.ShapeDtypeStruct(x.shape, x.dtype) for x in leaving],
        in_specs=[anywhere] * 9 + [here, anywhere],
        out_specs=[here] * 5 + [anywhere],
        scratch_shapes=scratch,
        compiler_params=pltpu.CompilerParams(
            collective_id=2, has_side_effects=True, vmem_limit_bytes=60 * 2**20
        ),
        name="reduce_gradients",
    )(*factors, small, *leaving)


Q_TILES = 9
O_AT, KV_AT, KV_WIDTH = 1792, 1152, 640
CHUNK = 1280
SUB = 64


def dot_nn(left, right):
    return jnp.dot(left, right, preferred_element_type=jnp.float32)


def dot_nt(left, right):
    return lax.dot_general(
        left, right, (((1,), (1,)), ((), ())), preferred_element_type=jnp.float32
    )


def span_of_device():
    seq = lax.axis_index("seq")
    rep = lax.axis_index("rep")
    z, x, y, core = seq // 2, seq % 2, rep // 2, rep % 2
    return z, (2 * y + x + y * (1 - 2 * x)) * 2 + core


def device_of_span(group, span):
    chip = span // 2
    x, y = (chip + 1) // 2 % 2, chip // 2
    return (group * 2 + x, y * 2 + span % 2)


def lanes(shape):
    return lax.broadcasted_iota(jnp.int32, shape, 1)


def rotated(value, cosine, sine):
    first = lanes(value.shape) % 64 < 32
    partner = jnp.where(first, pltpu.roll(value, 96, 1), pltpu.roll(value, 32, 1))
    return value * cosine + partner * sine


def block_kernel(*refs):
    (tokens, cotangent, meta, rope, turn, gain_a, gain_f, routers, wa_in, wg_in, wu_in, wd_in) = refs[:12]
    (output, input_grad, small) = refs[12:15]
    a_out, gqkv_out, o_out, gt_out, b_out, gg_all, gu_all, hidden_out, gf_out = refs[15:24]
    (
        wa, wg, wu, wd, gains, natural_at, padded_at, cotangent_at, leaving, h_all, z_all, tf_all, gate_all, up_all, q_all, window_two, window_one,
        got_two, got_one, sending_two, sending_one, depth_win, depth_at, bias_at, cos_at, sin_at, stats, dkv, grad, acc, gg_at, gu_at,
        keys_at, s_at, gp_at, p_at, gs_at, qs_at, us_at, move_send, move_recv, a_all, gqkv_all, o_all, gt_all, b_all, hidden_all, gf_all, factor_sem,
        load_sem, out_sem, kv_send, kv_recv, back_send, back_recv, depth_send, depth_recv,
    ) = refs[24:]
    narrow, wide = jnp.bfloat16, jnp.float32
    group, span = span_of_device()
    core = span % 2
    target, source, moves = move_partners()

    barrier = pltpu.get_barrier_semaphore()
    for away in (1, 2, 3):

        @pl.when(span + away < 8)
        def _():
            pl.semaphore_signal(
                barrier, inc=1, device_id=device_of_span(group, span + away), device_id_type=MESH
            )

        @pl.when(span - away >= 0)
        def _():
            pl.semaphore_signal(
                barrier, inc=1, device_id=device_of_span(group, span - away), device_id_type=MESH
            )

    @pl.when(moves == 1)
    def _():
        pl.semaphore_signal(barrier, inc=1, device_id=target, device_id_type=MESH)
        pl.semaphore_signal(barrier, inc=1, device_id=source, device_id_type=MESH)

    loads = [
        pltpu.make_async_copy(src, dst, load_sem.at[i])
        for i, (src, dst) in enumerate(((wa_in, wa), (wg_in, wg), (wu_in, wu), (wd_in, wd)))
    ]
    for load in loads:
        load.start()

    depth_win[3] = jnp.broadcast_to(meta[0:1, :], (8, 128))
    for away in (1, 2, 3):

        @pl.when(span - away < 0)
        def _():
            depth_win[3 - away] = jnp.zeros((8, 128), wide)
            for recursion in range(RECUR):
                window_two[recursion, 3 - away] = jnp.zeros((2, 128, 256), narrow)
                window_one[recursion, 3 - away] = jnp.zeros((128, 128), narrow)


    def depth_copy(away, device):
        return remote(
            depth_win.at[3],
            depth_win.at[3 - away],
            depth_send.at[away - 1],
            depth_recv.at[away - 1],
            device,
        )

    def window(recursion, slot, pair):
        if pair == 2:
            return window_one.at[recursion, slot]
        return window_two.at[recursion, slot, pair]

    def kv_copy(recursion, pair, slot, to_slot, sent, device):
        return remote(
            window(recursion, slot, pair),
            window(recursion, to_slot, pair),
            kv_send.at[recursion, pair, sent],
            kv_recv.at[recursion, pair, to_slot],
            device,
        )

    def sending(slot, pair):
        return sending_one.at[slot] if pair == 2 else sending_two.at[slot, pair]

    def got(recursion, slot, pair):
        return got_one.at[recursion, slot] if pair == 2 else got_two.at[recursion, slot, pair]

    def back_copy(recursion, pair, slot, device):
        return remote(
            sending(slot, pair),
            got(recursion, slot, pair),
            back_send.at[recursion, pair, slot],
            back_recv.at[recursion, pair, slot],
            device,
        )

    def pair_lanes(pair):
        return slice(512, 640) if pair == 2 else slice(pair * 256, pair * 256 + 256)

    def factor_copies(recursion, which):
        pairs = (
            (a_all, a_out),
            (o_all, o_out),
            (b_all, b_out),
            (hidden_all, hidden_out),
            (gf_all, gf_out),
            (gt_all, gt_out),
            (gqkv_all, gqkv_out),
        )
        return [
            pltpu.make_async_copy(
                pairs[i][0].at[recursion], pairs[i][1].at[recursion], factor_sem.at[i, recursion]
            )
            for i in which
        ]

    def stage_copies(recursion):
        return [
            pltpu.make_async_copy(gg_at, gg_all.at[recursion], out_sem.at[0]),
            pltpu.make_async_copy(gu_at, gu_all.at[recursion], out_sem.at[1]),
        ]

    def neighbour(away):
        return device_of_span(group, span + away)

    sibling = neighbour(1 - 2 * core)

    def when(condition, action):
        @pl.when(condition)
        def _():
            action()

    def send_keys(recursion, pair):
        when(span + 2 < 8, lambda: kv_copy(recursion, pair, 3, 1, 0, neighbour(2)).start())
        when(core == 0, lambda: kv_copy(recursion, pair, 3, 2, 1, sibling).start())
        when(
            (core == 1) & (span + 3 < 8),
            lambda: kv_copy(recursion, pair, 3, 0, 1, neighbour(3)).start(),
        )

    def pass_keys_on(recursion, pair):
        @pl.when(span >= 2)
        def _():
            kv_copy(recursion, pair, 3, 1, 0, sibling).wait_recv()
            kv_copy(recursion, pair, 1, 2 * core, 2, sibling).start()

    def wait_keys(recursion, pair):
        when(span >= 1, lambda: kv_copy(recursion, pair, 3, 2, 1, sibling).wait_recv())
        when(span >= 3, lambda: kv_copy(recursion, pair, 3, 0, 1, sibling).wait_recv())

    def wait_keys_sent(recursion, pair):
        when(span + 2 < 8, lambda: kv_copy(recursion, pair, 3, 1, 0, sibling).wait_send())
        when(core == 0, lambda: kv_copy(recursion, pair, 3, 2, 1, sibling).wait_send())
        when(
            (core == 1) & (span + 3 < 8),
            lambda: kv_copy(recursion, pair, 3, 0, 1, sibling).wait_send(),
        )
        when(span >= 2, lambda: kv_copy(recursion, pair, 1, 2, 2, sibling).wait_send())

    def send_back(recursion, pair):
        at = pair_lanes(pair)

        @pl.when(span >= 2)
        def _():
            first = pl.multiple_of(256 * (1 - core), 128)
            sending(0, pair)[...] = dkv[pl.ds(first, 128), at].astype(narrow)
            back_copy(recursion, pair, 0, sibling).start()

        sending(2, pair)[...] = dkv[
            pl.ds(pl.multiple_of(256 * core, 128), 128), at
        ].astype(narrow)
        when(core == 1, lambda: back_copy(recursion, pair, 2, sibling).start())
        when(
            (core == 0) & (span >= 3),
            lambda: back_copy(recursion, pair, 2, neighbour(-3)).start(),
        )

    def pass_back_on(recursion, pair):
        @pl.when(span >= 2)
        def _():
            back_copy(recursion, pair, 0, sibling).wait_recv()
            sending(1, pair)[...] = (
                dkv[128:256, pair_lanes(pair)] + got(recursion, 0, pair)[...].astype(wide)
            ).astype(narrow)
            back_copy(recursion, pair, 1, neighbour(-2)).start()

    def take_back(recursion, pair):
        at = pair_lanes(pair)

        @pl.when((core == 0) | (span + 3 < 8))
        def _():
            back_copy(recursion, pair, 2, sibling).wait_recv()
            dkv[384:512, at] += got(recursion, 2, pair)[...].astype(wide)

        @pl.when(span + 2 < 8)
        def _():
            back_copy(recursion, pair, 1, sibling).wait_recv()
            dkv[384:512, at] += got(recursion, 1, pair)[...].astype(wide)

    def wait_back_sent(recursion, pair):
        when(span >= 2, lambda: back_copy(recursion, pair, 0, sibling).wait_send())
        when(span >= 2, lambda: back_copy(recursion, pair, 1, sibling).wait_send())
        when((core == 1) | (span >= 3), lambda: back_copy(recursion, pair, 2, sibling).wait_send())

    def add_pads():
        for block in range(32):
            padded_at[block * PADDED_ROWS : block * PADDED_ROWS + OWN_ROWS, :] = natural_at[
                block * OWN_ROWS : block * OWN_ROWS + OWN_ROWS, :
            ]

    def drop_pads():
        for block in range(32):
            natural_at[block * OWN_ROWS : block * OWN_ROWS + OWN_ROWS, :] = padded_at[
                block * PADDED_ROWS : block * PADDED_ROWS + OWN_ROWS, :
            ]

    here = device_of_span(group, span)

    span_lane = meta[1:2, :]
    turn_cos = jnp.zeros((1, 128), wide)
    turn_sin = jnp.zeros((1, 128), wide)
    for k in range(4):
        turn_cos = turn_cos + jnp.where(span_lane == k, turn[k : k + 1, :], 0.0)
        turn_sin = turn_sin + jnp.where(span_lane == k, turn[8 + k : 9 + k, :], 0.0)
    cos_at[...] = turn_cos * rope[0] - turn_sin * rope[1]
    sign = jnp.where(lanes((128, 128)) % 64 < 32, -1.0, 1.0)
    sin_at[...] = sign * (turn_sin * rope[0] + turn_cos * rope[1])

    padded_at[...] = jnp.zeros((1024, 128), wide)
    vectors = jnp.concatenate(
        [gain_a[...], gain_f[...], routers[...], jnp.zeros((123, MODEL_WIDTH), wide)], axis=0
    )
    natural_at[...] = vectors.T
    add_pads()
    gains[...] = padded_at[...].T[0:8, :]
    natural_at[...] = tokens[...].astype(wide)
    add_pads()
    h_all[0] = padded_at[...].T
    pl.semaphore_wait(barrier, 3 + span + span // 4 * (7 - 2 * span) + 2 * moves)
    for away in (1, 2, 3):
        when(span + away < 8, lambda: depth_copy(away, neighbour(away)).start())
    small[...] = jnp.zeros((8, 1024), wide)

    row = lax.broadcasted_iota(jnp.int32, (128, 128), 0)
    column = lanes((128, 128))
    ones = jnp.ones((128, 128), wide)
    def set_depths():
        for away in (1, 2, 3):
            when(span - away >= 0, lambda: depth_copy(away, here).wait_recv())
        for block in range(4):
            held = depth_win[block]
            depth_at[pl.ds(block * 128, 128), :] = dot_nn(
                jnp.where(row == column, jnp.broadcast_to(held[0:1, :], (128, 128)), 0.0), ones
            ).astype(narrow)

    def set_bias(recursion):
        level = recursion.astype(wide)
        for block in range(4):
            active = depth_at[pl.ds(block * 128, 128), :].astype(wide) > level
            if block == 3:
                allowed = (row == column) | (active & (row <= column))
            else:
                allowed = active & (span_lane >= 3 - block)
            bias_at[pl.ds(block * 128, 128), :] = jnp.where(allowed, 0.0, masked_score).astype(narrow)

    def inverse_rms(value):
        return lax.rsqrt(
            jnp.sum(value * value, axis=-1, keepdims=True) / MODEL_WIDTH + epsilon
        )

    def active_column(recursion):
        own = depth_at[384:512, :].astype(wide)[:, 0:1]
        return jnp.where(own > recursion.astype(wide), 1.0, 0.0)

    def mixing_gate(recursion):
        logits = jnp.sum(
            h_all[recursion] * gains[pl.ds(2 + recursion, 1), :], axis=-1, keepdims=True
        )
        return jax.nn.sigmoid(logits)

    def halves(tile, pair):
        low = lanes(tile.shape) < 64
        zero = jnp.zeros_like(tile)
        if pair == 2:
            return jnp.where(low, tile, zero)
        return jnp.concatenate([jnp.where(low, tile, zero), jnp.where(low, zero, tile)], axis=0)

    def set_keys(recursion, pair):
        for block in range(4):
            at = pl.ds(block * 128, 128)
            keys_at[at, 0:128] = window(recursion, block, pair)[:, 0:128]
            keys_at[at, 128:256] = bias_at[at, :]

    def value_tile(recursion, pair):
        at = 0 if pair == 2 else 128
        parts = [window(recursion, b, pair)[:, at : at + 128] for b in range(4)]
        return jnp.concatenate(parts, axis=0)

    def set_scores(recursion, pair, part, buffer):
        at = (pair * 3 + part) * 128
        queries = halves(q_all[recursion, :, at : at + 128], pair)
        width = queries.shape[0]
        same = jnp.where(row == column, 1.0, 0.0).astype(narrow)
        same = same if width == 128 else jnp.concatenate([same, same], axis=0)
        both = jnp.concatenate([queries, same], axis=1)
        s_at[buffer, :, 0:width] = dot_nt(keys_at[...], both)
        return queries, width

    def rows_of_eight(value, join):
        return join(value.reshape(value.shape[0] // 8, 8, value.shape[1]), axis=0)

    def joined(out, pair):
        if pair == 2:
            return jnp.where(row < 64, out, 0.0).T
        return jnp.where(row < 64, out[:, :128], out[:, 128:]).T

    def attend(recursion):
        pass_keys_on(recursion, 0)
        pass_keys_on(recursion, 1)
        for pair in range(3):
            wait_keys(recursion, pair)
            set_keys(recursion, pair)
            values_t = value_tile(recursion, pair).T
            for part in range(3):
                buffer = part % 2
                _, width = set_scores(recursion, pair, part, buffer)
                top = jnp.full((8, width), masked_score, wide)
                for sub in range(0, 512, SUB):
                    scores = s_at[buffer, sub : sub + SUB, 0:width]
                    top = jnp.maximum(top, rows_of_eight(scores, jnp.max))
                top = jnp.max(top, axis=0, keepdims=True)
                total = jnp.zeros((8, width), wide)
                for sub in range(0, 512, SUB):
                    weight = jnp.exp(s_at[buffer, sub : sub + SUB, 0:width] - top)
                    total = total + rows_of_eight(weight, jnp.sum)
                    p_at[sub : sub + SUB, part * 256 : part * 256 + width] = weight.astype(narrow)
                total = jnp.sum(total, axis=0, keepdims=True)
                stats[recursion, pair * 3 + part, 0:1, 0:width] = top + jnp.log(total)
                out = dot_nn(values_t, p_at[:, part * 256 : part * 256 + width]) / total
                if pair == 2:
                    head = (12 + part) * HEAD_SIZE
                    natural_at[head : head + 64, :] = out[64:, :]
                else:
                    head = (6 * pair + part) * HEAD_SIZE
                    natural_at[head : head + 64, :] = out[:64, :128]
                    head = (6 * pair + 3 + part) * HEAD_SIZE
                    natural_at[head : head + 64, :] = out[64:, 128:]
            if pair == 0:
                pass_keys_on(recursion, 2)

    def upstream_of(pair, part):
        zero = jnp.zeros((64, 128), narrow)

        def head(number):
            return natural_at[number * 64 : number * 64 + 64, :].astype(narrow)

        if pair == 2:
            return jnp.concatenate([zero, head(12 + part)], axis=0)
        low = jnp.concatenate([head(6 * pair + part), zero], axis=1)
        high = jnp.concatenate([zero, head(6 * pair + 3 + part)], axis=1)
        return jnp.concatenate([low, high], axis=0)

    def attend_back(recursion):
        for pair in range(3):
            set_keys(recursion, pair)
            values = value_tile(recursion, pair)
            keys_t = keys_at[:, 0:128].T
            width = 128 if pair == 2 else 256
            for part in range(3):
                buffer = part % 2
                queries, _ = set_scores(recursion, pair, part, buffer)
                upstream = upstream_of(pair, part)
                qs_at[part * width : part * width + width, :] = queries
                us_at[:, part * width : part * width + width] = upstream
                gp_at[buffer, :, 0:width] = dot_nn(values, upstream)
                log_total = stats[recursion, pair * 3 + part, 0:1, 0:width]
                inner = jnp.zeros((8, width), wide)
                where = slice(part * width, part * width + width)
                for sub in range(0, 512, SUB):
                    probs = jnp.exp(s_at[buffer, sub : sub + SUB, 0:width] - log_total)
                    s_at[buffer, sub : sub + SUB, 0:width] = probs
                    p_at[sub : sub + SUB, where] = probs.astype(narrow)
                    inner = inner + rows_of_eight(
                        probs * gp_at[buffer, sub : sub + SUB, 0:width], jnp.sum
                    )
                inner = jnp.sum(inner, axis=0, keepdims=True)
                for sub in range(0, 512, SUB):
                    rows = slice(sub, sub + SUB)
                    gs_at[rows, where] = (
                        s_at[buffer, rows, 0:width] * (gp_at[buffer, rows, 0:width] - inner)
                    ).astype(narrow)
            grad_keys = dot_nn(gs_at[:, 0 : 3 * width], qs_at[0 : 3 * width, :])
            grad_values = dot_nt(p_at[:, 0 : 3 * width], us_at[:, 0 : 3 * width])
            if pair == 2:
                dkv[:, 512:640] = grad_keys + grad_values
            else:
                dkv[:, pair * 256 : pair * 256 + 128] = grad_keys
                dkv[:, pair * 256 + 128 : pair * 256 + 256] = grad_values
            send_back(recursion, pair)
            out = dot_nn(keys_t, gs_at[:, 0 : 3 * width])
            for part in range(3):
                at = (pair * 3 + part) * 128
                gqkv_all[recursion, :, at : at + 128] = rotated(
                    joined(out[:, part * width : part * width + width], pair),
                    cos_at[...] * 0.125,
                    sin_at[...] * -0.125,
                ).astype(narrow)
            if pair > 0:
                pass_back_on(recursion, pair - 1)

    def rotate_keys(value, sine):
        cosine = cos_at[...]
        low = lanes((128, 128)) < 64
        parts = []
        for tile in range(5):
            part = value[:, tile * 128 : tile * 128 + 128]
            if tile in (0, 2):
                part = rotated(part, cosine, sine)
            elif tile == 4:
                part = jnp.where(low, rotated(part, cosine, sine), part)
            parts.append(part)
        return jnp.concatenate(parts, axis=1)

    @pl.loop(0, RECUR)
    def _(recursion):
        state = h_all[recursion]
        normal = state * inverse_rms(state)
        a_b = (normal * gains[0:1, :]).astype(narrow)
        a_all[recursion] = a_b

        @pl.when(recursion == 0)
        def _():
            loads[0].wait()

        pair_values = dot_nn(a_b, wa[:, KV_AT:O_AT])
        pair_values = rotate_keys(pair_values, sin_at[...]).astype(narrow)
        for pair in range(3):
            window(recursion, 3, pair)[...] = pair_values[:, pair_lanes(pair)]
            send_keys(recursion, pair)
        cosine, sine = cos_at[...] * 0.125, sin_at[...] * 0.125
        for first, width in ((0, 512), (512, 512), (1024, 128)):
            queries = dot_nn(a_all[recursion], wa[:, first : first + width])
            for at in range(0, width, 128):
                q_all[recursion, :, first + at : first + at + 128] = rotated(
                    queries[:, at : at + 128], cosine, sine
                ).astype(narrow)

        @pl.when(recursion == 0)
        def _():
            set_depths()

        set_bias(recursion)
        attend(recursion)

        @pl.when(recursion == 0)
        def _():
            start_moves(
                (cotangent,),
                (cotangent_at,),
                move_send.at[pl.ds(0, 1)],
                move_recv.at[pl.ds(0, 1)],
                target,
                moves,
            )

        add_pads()
        o_pad = padded_at[...].T.astype(narrow)
        o_all[recursion] = o_pad
        branch = dot_nn(o_pad, wa[:, O_AT:])
        middle = h_all[recursion] + branch
        z_all[recursion] = middle
        b_b = (middle * inverse_rms(middle) * gains[1:2, :]).astype(narrow)
        b_all[recursion] = b_b
        acc[...] = branch

        @pl.when(recursion == 0)
        def _():
            for load in loads[1:]:
                load.wait()

        for j in range(FEEDFORWARD_UNITS // CHUNK):
            at = slice(j * CHUNK, j * CHUNK + CHUNK)
            gate = dot_nn(b_all[recursion], wg[:, at])
            up = dot_nn(b_all[recursion], wu[:, at])
            gate_all[recursion, :, at] = gate
            up_all[recursion, :, at] = up
            hidden = (gate * jax.nn.sigmoid(gate) * up).astype(narrow)
            hidden_all[recursion, :, at] = hidden
            acc[...] += dot_nn(hidden, wd[at, :])

        for copy in factor_copies(recursion, (0, 1, 2, 3)):
            copy.start()
        tf_all[recursion] = acc[...]
        mixing = active_column(recursion) * mixing_gate(recursion)
        following = h_all[recursion] + mixing * acc[...]

        @pl.when(recursion < RECUR - 1)
        def _():
            h_all[recursion + 1] = following

        @pl.when(recursion == RECUR - 1)
        def _():
            padded_at[...] = following.astype(narrow).astype(wide).T
            drop_pads()
            leaving[...] = natural_at[...].astype(narrow)

    wait_moves((cotangent,), (cotangent_at,), move_send.at[pl.ds(0, 1)], move_recv.at[pl.ds(0, 1)], target, moves)
    natural_at[...] = cotangent_at[...].astype(wide)
    add_pads()
    grad[...] = padded_at[...].T

    @pl.loop(0, RECUR)
    def _(i):
        recursion = RECUR - 1 - i

        @pl.when(i == 1)
        def _():
            start_moves(
                (leaving,),
                (output,),
                move_send.at[pl.ds(1, 1)],
                move_recv.at[pl.ds(1, 1)],
                source,
                moves,
            )

        router_row = gains[pl.ds(2 + recursion, 1), :]
        active, gate_value = active_column(recursion), mixing_gate(recursion)
        upstream = grad[...]
        grad_mix = jnp.sum(upstream * tf_all[recursion], axis=-1, keepdims=True)
        grad_logit = active * grad_mix * gate_value * (1.0 - gate_value)
        small[pl.ds(2 + recursion, 1), :] = jnp.sum(
            grad_logit * h_all[recursion], axis=0, keepdims=True
        )
        delta = (active * gate_value) * upstream
        gf_all[recursion] = delta.astype(narrow)
        grad[...] = upstream + grad_logit * router_row
        tf_all[recursion] = delta
        acc[...] = jnp.zeros((128, 1024), wide)

        @pl.when(recursion < RECUR - 1)
        def _():
            for copy in stage_copies(recursion + 1):
                copy.wait()

        for j in range(FEEDFORWARD_UNITS // CHUNK):
            at = slice(j * CHUNK, j * CHUNK + CHUNK)
            grad_hidden = dot_nt(gf_all[recursion], wd[at, :])
            gate, up = gate_all[recursion, :, at], up_all[recursion, :, at]
            sigmoid = jax.nn.sigmoid(gate)
            grad_gate = (grad_hidden * up * sigmoid * (1.0 + gate * (1.0 - sigmoid))).astype(narrow)
            grad_up = (grad_hidden * gate * sigmoid).astype(narrow)
            gg_at[:, at] = grad_gate
            gu_at[:, at] = grad_up
            acc[...] += dot_nt(grad_gate, wg[:, at]) + dot_nt(grad_up, wu[:, at])

        for copy in stage_copies(recursion) + factor_copies(recursion, (4,)):
            copy.start()
        middle = z_all[recursion]
        inverse = inverse_rms(middle)
        normal = middle * inverse
        small[1:2, :] += jnp.sum(acc[...] * normal, axis=0, keepdims=True)
        scaled = acc[...] * gains[1:2, :]
        inner = jnp.sum(scaled * normal, axis=-1, keepdims=True) / MODEL_WIDTH
        grad_middle = inverse * (scaled - normal * inner)
        gt_b = (tf_all[recursion] + grad_middle).astype(narrow)
        gt_all[recursion] = gt_b
        for copy in factor_copies(recursion, (5,)):
            copy.start()
        grad[...] += grad_middle
        padded_at[...] = dot_nt(gt_b, wa[:, O_AT:]).T
        drop_pads()
        set_bias(recursion)

        @pl.when(recursion < RECUR - 1)
        def _():
            for pair in range(3):
                wait_back_sent(recursion + 1, pair)

        attend_back(recursion)
        acc[...] = dot_nt(gqkv_all[recursion, :, :KV_AT], wa[:, :KV_AT])

        pass_back_on(recursion, 2)
        for pair in range(3):
            take_back(recursion, pair)
        gqkv_all[recursion, :, KV_AT:] = rotate_keys(dkv[384:512, :], -sin_at[...]).astype(narrow)
        for copy in factor_copies(recursion, (6,)):
            copy.start()
        grad_normed = acc[...] + dot_nt(gqkv_all[recursion, :, KV_AT:], wa[:, KV_AT:O_AT])
        state = h_all[recursion]
        inverse = inverse_rms(state)
        normal = state * inverse
        small[0:1, :] += jnp.sum(grad_normed * normal, axis=0, keepdims=True)
        scaled = grad_normed * gains[0:1, :]
        inner = jnp.sum(scaled * normal, axis=-1, keepdims=True) / MODEL_WIDTH
        grad[...] += inverse * (scaled - normal * inner)

    for copy in stage_copies(0):
        copy.wait()
    for recursion in range(RECUR):
        for copy in factor_copies(recursion, range(7)):
            copy.wait()
    padded_at[...] = grad[...].T
    drop_pads()
    input_grad[...] = natural_at[...].astype(narrow)

    wait_moves((leaving,), (output,), move_send.at[pl.ds(1, 1)], move_recv.at[pl.ds(1, 1)], source, moves)
    for away in (1, 2, 3):
        when(span + away < 8, lambda: depth_copy(away, here).wait_send())
    for recursion in range(RECUR):
        for pair in range(3):
            wait_keys_sent(recursion, pair)
    for pair in range(3):
        wait_back_sent(0, pair)


def run_block(tokens, cotangent, meta, gains, weights):
    narrow, wide, vmem, sems = jnp.bfloat16, jnp.float32, pltpu.VMEM, pltpu.SemaphoreType.DMA
    half = HEAD_SIZE // 2
    lane = np.arange(128) % half
    frequency = 10000.0 ** (-lane / half)
    angle = np.arange(128)[:, None] * frequency[None, :]
    rope = np.stack([np.cos(angle), np.sin(angle)]).astype(np.float32)
    jump = np.arange(4)[:, None] * 128.0 * frequency[None, :]
    turn = np.zeros((16, 128), np.float32)
    turn[:4], turn[8:12] = np.cos(jump), np.sin(jump)
    outs = [((MODEL_WIDTH, 128), narrow), ((MODEL_WIDTH, 128), narrow), ((8, 1024), wide)]
    outs += [
        ((RECUR, 128, width), narrow)
        for width in (1024, O_AT, 1024, 1024, 1024, 2560, 2560, 2560, 1024)
    ]
    scratch = [
        vmem((1024, 2816), narrow),
        vmem((1024, 2560), narrow),
        vmem((1024, 2560), narrow),
        vmem((2560, 1024), narrow),
        vmem((8, 1024), wide),
        vmem((MODEL_WIDTH, 128), wide),
        vmem((1024, 128), wide),
        vmem((MODEL_WIDTH, 128), narrow),
        vmem((MODEL_WIDTH, 128), narrow),
        vmem((RECUR, 128, 1024), wide),
        vmem((RECUR, 128, 1024), wide),
        vmem((RECUR, 128, 1024), wide),
        vmem((RECUR, 128, 2560), wide),
        vmem((RECUR, 128, 2560), wide),
        vmem((RECUR, 128, KV_AT), narrow),
        vmem((RECUR, 4, 2, 128, 256), narrow),
        vmem((RECUR, 4, 128, 128), narrow),
        vmem((RECUR, 3, 2, 128, 256), narrow),
        vmem((RECUR, 3, 128, 128), narrow),
        vmem((3, 2, 128, 256), narrow),
        vmem((3, 128, 128), narrow),
        vmem((4, 8, 128), wide),
        vmem((512, 128), narrow),
        vmem((512, 128), narrow),
        vmem((128, 128), wide),
        vmem((128, 128), wide),
        vmem((RECUR, Q_TILES, 2, 256), wide),
        vmem((512, KV_WIDTH), wide),
        vmem((128, 1024), wide),
        vmem((128, 1024), wide),
        vmem((128, 2560), narrow),
        vmem((128, 2560), narrow),
        vmem((512, 256), narrow),
        vmem((2, 512, 256), wide),
        vmem((2, 512, 256), wide),
        vmem((512, 768), narrow),
        vmem((512, 768), narrow),
        vmem((768, 128), narrow),
        vmem((128, 768), narrow),
        sems((2,)),
        sems((2,)),
        *[vmem((RECUR, 128, width), narrow) for width in (1024, O_AT, 1024, 1024, 1024, 2560, 1024)],
        sems((7, RECUR)),
        sems((4,)),
        sems((2,)),
        sems((RECUR, 3, 3)),
        sems((RECUR, 3, 3)),
        sems((RECUR, 3, 3)),
        sems((RECUR, 3, 3)),
        sems((3,)),
        sems((3,)),
    ]
    here, anywhere = pl.BlockSpec(memory_space=vmem), pl.BlockSpec(memory_space=pl.ANY)
    return pl.pallas_call(
        block_kernel,
        out_shape=[jax.ShapeDtypeStruct(shape, dtype) for shape, dtype in outs],
        in_specs=[here, anywhere] + [here] * 6 + [anywhere] * 4,
        out_specs=[here] * 3 + [anywhere] * 9,
        scratch_shapes=scratch,
        compiler_params=pltpu.CompilerParams(
            collective_id=3, has_side_effects=True, vmem_limit_bytes=60 * 2**20
        ),
        name="run_block",
    )(tokens, cotangent, meta, rope, turn, *gains, *weights)


HEAD_TILES = tuple(
    (6 * (tile // 3) + tile % 3, 6 * (tile // 3) + 3 + tile % 3) if tile < 6 else (6 + tile, -1)
    for tile in range(9)
)
NATURAL_TILES = tuple((2 * tile, 2 * tile + 1 if tile < 7 else -1) for tile in range(8))


def fill_spread(spread, places):
    @pl.loop(0, MODEL_WIDTH // 64)
    def _(i):
        at = pl.multiple_of(i * 64, 64)
        rows = lax.broadcasted_iota(jnp.int32, (64, 1024), 0) + at
        spread[pl.ds(at, 64), :] = jnp.where(rows == places[0:1, :], 1.0, 0.0).astype(jnp.bfloat16)


def chunk_rows(flat, units, pairs, parity, unit):
    where = units * parity + unit
    return flat[pl.ds(where // 2, pairs, stride=units), :], where % 2


def placed_half(found, low):
    value, half = found
    return value if half == (0 if low else 1) else pltpu.roll(value, 64, 1)


def pack_tiles(flat, out, first, tiles, units, pairs):
    low = lax.broadcasted_iota(jnp.int32, (pairs, 128), 1) < 64
    zero = jnp.zeros((pairs, 128), jnp.float32)
    for parity in (0, 1):
        for tile, (left, right) in enumerate(tiles):
            one = placed_half(chunk_rows(flat, units, pairs, parity, left), True) if left >= 0 else zero
            two = (
                placed_half(chunk_rows(flat, units, pairs, parity, right), False)
                if right >= 0
                else zero
            )
            out[first + tile, pl.ds(parity, pairs, stride=2), :] = jnp.where(low, one, two)


def pack_wide(flat, own, tiles):
    for source, out in zip(flat[4:6], own[1:3]):
        for tile in range(20):
            tiles[tile, 0:OWN_ROWS] = source[pl.ds(tile, OWN_ROWS, stride=20), :]
            tiles[tile, OWN_ROWS:] = jnp.zeros((PADDED_ROWS - OWN_ROWS, 128), jnp.float32)
            out[:, tile * 128 : tile * 128 + 128] = tiles[tile].astype(jnp.bfloat16)


def pack_rest(flat, own, spread, tiles, natural, long_rows):
    w_query, w_key, w_value, w_out = flat[:4]
    attention, down = own[0], own[3]
    narrow = jnp.bfloat16
    tiles[...] = jnp.zeros(tiles.shape, jnp.float32)
    natural[...] = jnp.zeros(natural.shape, jnp.float32)
    pack_tiles(w_query, tiles, 0, HEAD_TILES, 15, 15)
    for tile, heads in ((9, (0, 1)), (11, (2, 3)), (13, (4, -1))):
        pack_tiles(w_key, tiles, tile, (heads,), 5, 15)
    for tile, heads in ((10, (0, 1)), (12, (2, 3)), (14, (-1, 4))):
        pack_tiles(w_value, tiles, tile, (heads,), 5, 15)
    low = lax.broadcasted_iota(jnp.int32, (32, 128), 1) < 64
    tiles[13] = jnp.where(low, tiles[13], tiles[14])
    for tile in range(14):
        attention[:, tile * 128 : tile * 128 + 128] = tiles[tile].astype(narrow)
    pack_tiles(w_out, natural, 0, NATURAL_TILES, 15, 15)
    pack_tiles(flat[6], long_rows, 0, NATURAL_TILES, 15, 40)
    both = jnp.concatenate([side_by_side(natural), side_by_side(long_rows)], axis=0)
    both = dot_nn(both.astype(narrow), spread[...]).astype(narrow)
    attention[:, 1792:], down[...] = both[0:32], both[32:112]


def side_by_side(tiles):
    return jnp.concatenate([tiles[tile] for tile in range(8)], axis=1)[:, 0:MODEL_WIDTH]


def natural_places():
    padded = np.arange(1024)
    natural = padded // PADDED_ROWS * OWN_ROWS + padded % PADDED_ROWS
    natural = np.where(padded % PADDED_ROWS < OWN_ROWS, natural, -1)
    return np.broadcast_to(natural[None], (8, 1024)).astype(np.int32)


def unpack_tiles(packed, first, tiles, units, pairs, out):
    spots = {}
    for tile, heads in enumerate(tiles):
        for half, unit in enumerate(heads):
            if unit >= 0:
                spots[unit] = (tile, half)
    low = lax.broadcasted_iota(jnp.int32, (pairs, 128), 1) < 64

    def unit_at(where, is_low):
        parity, unit = where // units, where % units
        tile, half = spots[unit]
        value = packed[first + tile, pl.ds(parity, pairs, stride=2), :]
        return placed_half((value, half), is_low)

    for chunk in range(units):
        out[pl.ds(chunk, pairs, stride=units), :] = jnp.where(
            low, unit_at(2 * chunk, True), unit_at(2 * chunk + 1, False)
        )


def exact_gathered(value, spread):
    first = value.astype(jnp.bfloat16)
    rest = value - first.astype(jnp.float32)
    second = rest.astype(jnp.bfloat16)
    third = (rest - second.astype(jnp.float32)).astype(jnp.bfloat16)
    summed = dot_nt(jnp.concatenate([first, second, third], axis=0), spread[...])
    rows = value.shape[0]
    return summed[0:rows] + summed[rows : 2 * rows] + summed[2 * rows :]


def split_tiles(value, tiles):
    for tile in range(7):
        tiles[tile] = value[:, tile * 128 : tile * 128 + 128]
    tiles[7, :, 0:64] = value[:, 896:960]


def unpack_kernel(*refs):
    inside, places = refs[:7], refs[7]
    d_query, d_key, d_value, d_out, d_gate, d_up, d_down = refs[8:15]
    d_attn, d_ffn, d_router, output, input_grad = refs[15:20]
    held, (spread, tiles, natural, long_rows, sems) = refs[20:27], refs[27:]
    copies = [
        pltpu.make_async_copy(src, dst, sems.at[i])
        for i, (src, dst) in enumerate(zip(inside, held))
    ]
    for copy in copies:
        copy.start()
    fill_spread(spread, places)
    for copy in copies:
        copy.wait()
    attention, gate, up, down, small, moved_grad, moved_output = held
    output[...] = moved_output[...]
    input_grad[...] = moved_grad[...].astype(jnp.float32)
    for tile in range(14):
        tiles[tile] = attention[:, tile * 128 : tile * 128 + 128]
    unpack_tiles(tiles, 0, HEAD_TILES, 15, 15, d_query)
    none = (-1, -1)
    unpack_tiles(tiles, 9, ((0, 1), none, (2, 3), none, (4, -1)), 5, 15, d_key)
    unpack_tiles(tiles, 9, (none, (0, 1), none, (2, 3), (-1, 4)), 5, 15, d_value)
    for packed, out in ((gate, d_gate), (up, d_up)):
        for tile in range(20):
            out[pl.ds(tile, OWN_ROWS, stride=20), :] = packed[
                0:OWN_ROWS, tile * 128 : tile * 128 + 128
            ]
    gathered = exact_gathered(
        jnp.concatenate([attention[:, 1792:], down[...], small[...]], axis=0), spread
    )
    split_tiles(gathered[0:32], natural)
    unpack_tiles(natural, 0, NATURAL_TILES, 15, 15, d_out)
    split_tiles(gathered[32:112], long_rows)
    unpack_tiles(long_rows, 0, NATURAL_TILES, 15, 40, d_down)
    d_attn[...], d_ffn[...], d_router[...] = gathered[112:113], gathered[113:114], gathered[114:117]


def unpack_gradients(sums, small, input_grad, output):
    narrow, wide, vmem = jnp.bfloat16, jnp.float32, pltpu.VMEM
    here, anywhere = pl.BlockSpec(memory_space=vmem), pl.BlockSpec(memory_space=pl.ANY)
    flat = (225, 75, 75, 225, 600, 600, 600)
    inside = (*sums, small, input_grad, output)
    return pl.pallas_call(
        unpack_kernel,
        out_shape=[jax.ShapeDtypeStruct((rows, 128), wide) for rows in flat]
        + [
            jax.ShapeDtypeStruct((1, MODEL_WIDTH), wide),
            jax.ShapeDtypeStruct((1, MODEL_WIDTH), wide),
            jax.ShapeDtypeStruct((RECUR, MODEL_WIDTH), wide),
            jax.ShapeDtypeStruct((MODEL_WIDTH, 128), narrow),
            jax.ShapeDtypeStruct((MODEL_WIDTH, 128), wide),
        ],
        in_specs=[anywhere] * 7 + [here],
        out_specs=[here] * 12,
        scratch_shapes=[vmem(x.shape, x.dtype) for x in inside]
        + [
            vmem((MODEL_WIDTH, 1024), narrow),
            vmem((14, 32, 128), wide),
            vmem((8, 32, 128), wide),
            vmem((8, 80, 128), wide),
            pltpu.SemaphoreType.DMA((7,)),
        ],
        compiler_params=pltpu.CompilerParams(vmem_limit_bytes=59 * 2**20),
        name="unpack_gradients",
    )(*inside, natural_places())


def per_device_fast(
    tokens,
    depths,
    seq_spans,
    cotangent,
    w_query,
    key_weight,
    value_weight,
    w_out,
    w_gate,
    w_up,
    w_down,
    attn_gain,
    ffn_gain,
    router,
):
    *weights, own_tokens, own_meta = gather_weights(
        (w_query, key_weight, value_weight, w_out, w_gate, w_up, w_down),
        tokens[0].T,
        depths,
        seq_spans,
    )
    output, input_grad, small, *factors = run_block(
        own_tokens, cotangent[0].T, own_meta, (attn_gain[None], ffn_gain[None], router), weights
    )
    *sums, small_sum, input_grad = reduce_gradients(
        [x.reshape(RECUR * 128, -1) for x in factors], small, (input_grad,)
    )
    *gradients, d_attn, d_ffn, d_router, output, input_grad = unpack_gradients(
        sums, small_sum, input_grad, output
    )
    return (
        output.T[None],
        input_grad.T[None],
        *[x.reshape(-1) for x in gradients],
        d_attn[0],
        d_ffn[0],
        d_router,
    )


def solution(mesh):
    fits = mesh.shape["seq"] == 8 and mesh.shape["rep"] == 4
    placed = (
        P("rep", "seq", None),
        P("rep", "seq"),
        P("rep", None),
        P("rep", "seq", None),
        P(("seq", "rep")),
        P(("seq", "rep")),
        P(("seq", "rep")),
        P(("seq", "rep")),
        P(("seq", "rep")),
        P(("seq", "rep")),
        P(("seq", "rep")),
        P(),
        P(),
        P(),
    )
    return jax.shard_map(
        per_device_fast if fits else per_device,
        mesh=mesh,
        in_specs=placed,
        out_specs=(
            P("rep", "seq", None),
            P("rep", "seq", None),
            P(("seq", "rep")),
            P(("seq", "rep")),
            P(("seq", "rep")),
            P(("seq", "rep")),
            P(("seq", "rep")),
            P(("seq", "rep")),
            P(("seq", "rep")),
            P(),
            P(),
            P(),
        ),
        check_vma=False,
    )
```

```python
import jax
import jax.numpy as jnp
import numpy as np
from jax import lax
from jax.experimental import pallas as pl
from jax.experimental.pallas import tpu as pltpu
from jax.sharding import PartitionSpec as P

MODEL_WIDTH = 960
QUERY_HEADS = 15
KEY_VALUE_HEADS = 5
HEAD_SIZE = 64
FEEDFORWARD_UNITS = 2560
LOGC = 5
RECUR = 3
OWN_ROWS = 30
PADDED_ROWS = 32
PADDED_WIDTH = 1024


highest = lax.Precision.HIGHEST
epsilon = 1e-06
masked_score = -1e30


def passed_along(value, axis, steps):
    count = lax.axis_size(axis)
    initial, last = (max(0, -steps), min(count, count - steps))
    return lax.ppermute(value, axis, [(source, source + steps) for source in range(initial, last)])


def for_sending(x):

    def short(part):
        return part.astype(jnp.bfloat16) if part.dtype == jnp.float32 else part

    return jax.tree.map(short, x)


def unscaled_product(left, right):
    return jnp.dot(left, right, preferred_element_type=jnp.float32)


def left_product(left, right):
    return lax.dot_general(
        left, right, (((0,), (0,)), ((), ())), preferred_element_type=jnp.float32
    )


def right_product(left, right):
    return lax.dot_general(
        left, right, (((1,), (1,)), ((), ())), preferred_element_type=jnp.float32
    )


def rms_parts(vectors, gain):
    inv_rms = lax.rsqrt(jnp.mean(vectors * vectors, axis=-1, keepdims=True) + epsilon)
    normal_part = vectors * inv_rms
    return (normal_part * gain, normal_part, inv_rms)


def rms_backward(upstream, normal_part, inv_rms, gain):
    gain_grad = jnp.sum(upstream * normal_part, axis=0)
    scaled = upstream * gain
    inner = jnp.mean(scaled * normal_part, axis=-1, keepdims=True)
    return (inv_rms * (scaled - normal_part * inner), gain_grad)


def angle_tables(positions, width):
    half_width = width // 2
    frequency = 10000.0 ** (-jnp.arange(half_width, dtype=jnp.float32) / half_width)
    angle_grid = positions[:, None] * frequency[None, :]
    return (jnp.cos(angle_grid)[:, None, :], jnp.sin(angle_grid)[:, None, :])


def apply_rotation(vectors, cosine_table, sine_table):
    half_width = vectors.shape[-1] // 2
    front_half = vectors[..., :half_width]
    back_half = vectors[..., half_width:]
    return jnp.concatenate(
        [
            front_half * cosine_table - back_half * sine_table,
            back_half * cosine_table + front_half * sine_table,
        ],
        axis=-1,
    )


def masked_scores(query_b, keys_win, allowed):
    scores = (
        jnp.einsum("qgjd,kgd->gjqk", query_b, keys_win, preferred_element_type=jnp.float32) * 0.125
    )
    return jnp.where(allowed[None, None], scores, masked_score)


def per_device(
    tokens,
    depths,
    seq_spans,
    cotangent,
    w_query,
    key_weight,
    value_weight,
    w_out,
    w_gate,
    w_up,
    w_down,
    attn_gain,
    ffn_gain,
    router,
):
    narrow_float_type = jnp.bfloat16
    wide_float_type = jnp.float32
    count_of_rows = tokens.shape[1]
    query_groupings = QUERY_HEADS // KEY_VALUE_HEADS
    chain = lax.axis_size("seq")
    most_spans = min(2**LOGC, chain // 2)
    depth_levels = (most_spans - 1).bit_length()
    extra_rows = ((1 << depth_levels) - most_spans) * count_of_rows
    window = most_spans * count_of_rows
    target_tokens = (
        (MODEL_WIDTH, QUERY_HEADS * HEAD_SIZE),
        (MODEL_WIDTH, KEY_VALUE_HEADS * HEAD_SIZE),
        (MODEL_WIDTH, KEY_VALUE_HEADS * HEAD_SIZE),
        (QUERY_HEADS * HEAD_SIZE, MODEL_WIDTH),
        (MODEL_WIDTH, FEEDFORWARD_UNITS),
        (MODEL_WIDTH, FEEDFORWARD_UNITS),
        (FEEDFORWARD_UNITS, MODEL_WIDTH),
    )
    fetched = (
        lax.all_gather(w_query.astype(narrow_float_type), ("seq", "rep"), axis=0, tiled=True),
        lax.all_gather(key_weight.astype(narrow_float_type), ("seq", "rep"), axis=0, tiled=True),
        lax.all_gather(value_weight.astype(narrow_float_type), ("seq", "rep"), axis=0, tiled=True),
        lax.all_gather(w_out.astype(narrow_float_type), ("seq", "rep"), axis=0, tiled=True),
        lax.all_gather(w_gate.astype(narrow_float_type), ("seq", "rep"), axis=0, tiled=True),
        lax.all_gather(w_up.astype(narrow_float_type), ("seq", "rep"), axis=0, tiled=True),
        lax.all_gather(w_down.astype(narrow_float_type), ("seq", "rep"), axis=0, tiled=True),
    )
    attention_weights = tuple(
        (gathered.reshape(target) for gathered, target in zip(fetched, target_tokens))
    )
    place = lax.axis_index("seq")
    lengths = seq_spans[0]
    seq_ends = jnp.cumsum(lengths)
    span_ids = jnp.arange(chain, dtype=jnp.int32)
    owners = jnp.sum((seq_ends[None, :] <= span_ids[:, None]).astype(jnp.int32), axis=1)
    seq_starts = seq_ends - lengths
    numbers = jnp.arange(lengths.shape[0], dtype=jnp.int32)
    first_span = jnp.sum(
        jnp.where(numbers[None, :] == owners[:, None], seq_starts[None, :], 0), axis=1
    )
    index_of_span = jnp.sum(jnp.where(span_ids == place, span_ids - first_span, 0))
    positions = (index_of_span * count_of_rows + jnp.arange(count_of_rows, dtype=jnp.int32)).astype(
        wide_float_type
    )
    cosine_table, sine_table = angle_tables(positions, HEAD_SIZE)
    row_ids = jnp.arange(count_of_rows, dtype=jnp.int32)
    col_ids = jnp.arange(window, dtype=jnp.int32)
    offsets = most_spans - 1 - col_ids // count_of_rows
    local_col = col_ids - (most_spans - 1) * count_of_rows
    causal = jnp.where(offsets[None, :] == 0, local_col[None, :] <= row_ids[:, None], True)
    diagonal = (offsets[None, :] == 0) & (local_col[None, :] == row_ids[:, None])
    span_ok = (index_of_span >= offsets)[None, :]
    active_all = (depths[0][None, :] > jnp.arange(RECUR, dtype=jnp.int32)[:, None]).astype(
        wide_float_type
    )
    hidden_state = tokens[0].astype(wide_float_type)
    saved = []
    for recursion in range(RECUR):
        current_active = active_all[recursion]
        normalized_input, normal_a, inv_a = rms_parts(hidden_state, attn_gain)
        normalized_input_copy = normalized_input.astype(narrow_float_type)
        raw_query = unscaled_product(normalized_input_copy, attention_weights[0]).reshape(
            count_of_rows, QUERY_HEADS, HEAD_SIZE
        )
        query_b = (
            apply_rotation(raw_query, cosine_table, sine_table)
            .astype(narrow_float_type)
            .reshape(count_of_rows, KEY_VALUE_HEADS, query_groupings, HEAD_SIZE)
        )
        unrotated_key = unscaled_product(normalized_input_copy, attention_weights[1]).reshape(
            count_of_rows, KEY_VALUE_HEADS, HEAD_SIZE
        )
        key_b = apply_rotation(unrotated_key, cosine_table, sine_table).astype(narrow_float_type)
        value_copy = (
            unscaled_product(normalized_input_copy, attention_weights[2])
            .astype(narrow_float_type)
            .reshape(count_of_rows, KEY_VALUE_HEADS, HEAD_SIZE)
        )
        active_b = current_active.astype(narrow_float_type)
        keys_win = key_b
        values_win = value_copy
        active_win = active_b
        for level in range(depth_levels):
            far_key, far_value, far_active = passed_along(
                (keys_win, values_win, active_win), "seq", 1 << level
            )
            keys_win = jnp.concatenate([far_key, keys_win], axis=0)
            values_win = jnp.concatenate([far_value, values_win], axis=0)
            active_win = jnp.concatenate([far_active, active_win], axis=0)
        allowed = span_ok & causal & ((active_win > 0)[None, :] | diagonal)
        scores = masked_scores(query_b, keys_win, allowed)
        row_max = jnp.max(scores, axis=-1, keepdims=True)
        expon = jnp.exp(scores - row_max)
        row_total = jnp.sum(expon, axis=-1, keepdims=True)
        probs_b = (expon / row_total).astype(narrow_float_type)
        log_total = row_max + jnp.log(row_total)
        attended_b = (
            jnp.einsum(
                "gjqk,kgd->qgjd", probs_b, values_win, preferred_element_type=wide_float_type
            )
            .astype(narrow_float_type)
            .reshape(count_of_rows, QUERY_HEADS * HEAD_SIZE)
        )
        branch = unscaled_product(attended_b, attention_weights[3])
        middle = hidden_state + branch
        second, normal_z, inv_z = rms_parts(middle, ffn_gain)
        second_b = second.astype(narrow_float_type)
        gate_value = unscaled_product(second_b, attention_weights[4])
        up_value = unscaled_product(second_b, attention_weights[5])
        hidden_b = (jax.nn.silu(gate_value) * up_value).astype(narrow_float_type)
        ffn_out = unscaled_product(hidden_b, attention_weights[6])
        weight_gate = jax.nn.sigmoid(jnp.dot(hidden_state, router[recursion], precision=highest))
        saved.append(
            (
                hidden_state,
                normalized_input_copy,
                normal_a,
                inv_a,
                query_b,
                keys_win,
                values_win,
                allowed,
                log_total,
                attended_b,
                branch,
                normal_z,
                inv_z,
                second_b,
                gate_value,
                up_value,
                hidden_b,
                ffn_out,
                weight_gate,
                current_active,
            )
        )
        hidden_state = hidden_state + (current_active * weight_gate)[:, None] * (branch + ffn_out)
    output = hidden_state.astype(narrow_float_type)
    refetched = (
        lax.all_gather(w_query.astype(narrow_float_type), ("seq", "rep"), axis=0, tiled=True),
        lax.all_gather(key_weight.astype(narrow_float_type), ("seq", "rep"), axis=0, tiled=True),
        lax.all_gather(value_weight.astype(narrow_float_type), ("seq", "rep"), axis=0, tiled=True),
        lax.all_gather(w_out.astype(narrow_float_type), ("seq", "rep"), axis=0, tiled=True),
        lax.all_gather(w_gate.astype(narrow_float_type), ("seq", "rep"), axis=0, tiled=True),
        lax.all_gather(w_up.astype(narrow_float_type), ("seq", "rep"), axis=0, tiled=True),
        lax.all_gather(w_down.astype(narrow_float_type), ("seq", "rep"), axis=0, tiled=True),
    )
    back_weights = tuple(
        (gathered.reshape(target) for gathered, target in zip(refetched, target_tokens))
    )
    master_shapes = (w_query, key_weight, value_weight, w_out, w_gate, w_up, w_down)
    shares = tuple((jnp.zeros_like(master) for master in master_shapes))
    gain_a_total = jnp.zeros((MODEL_WIDTH,), wide_float_type)
    gain_f_total = jnp.zeros((MODEL_WIDTH,), wide_float_type)
    router_rows = [None] * RECUR
    grad_state = cotangent[0].astype(wide_float_type)
    for recursion in reversed(range(RECUR)):
        (
            state_in,
            normalized_input_copy,
            normal_a,
            inv_a,
            query_b,
            keys_win,
            values_win,
            allowed,
            log_total,
            attended_b,
            branch,
            normal_z,
            inv_z,
            second_b,
            gate_value,
            up_value,
            hidden_b,
            ffn_out,
            weight_gate,
            current_active,
        ) = saved[recursion]
        mixing = current_active * weight_gate
        grad_delta = mixing[:, None] * grad_state
        grad_mix = jnp.sum(grad_state * (branch + ffn_out), axis=-1)
        grad_logit = current_active * grad_mix * weight_gate * (1.0 - weight_gate)
        router_rows[recursion] = jnp.dot(grad_logit, state_in, precision=highest)
        grad_next = grad_state + grad_logit[:, None] * router[recursion][None, :]
        ffn_grad_b = grad_delta.astype(narrow_float_type)
        grad_hidden = right_product(ffn_grad_b, back_weights[6])
        d_down = left_product(hidden_b, ffn_grad_b)
        sigmoid_gate = jax.nn.sigmoid(gate_value)
        grad_gate_b = (
            grad_hidden * up_value * sigmoid_gate * (1.0 + gate_value * (1.0 - sigmoid_gate))
        ).astype(narrow_float_type)
        grad_up_b = (grad_hidden * gate_value * sigmoid_gate).astype(narrow_float_type)
        grad_second = right_product(grad_gate_b, back_weights[4]) + right_product(
            grad_up_b, back_weights[5]
        )
        d_gate = left_product(second_b, grad_gate_b)
        d_up = left_product(second_b, grad_up_b)
        grad_middle, gain_f_part = rms_backward(grad_second, normal_z, inv_z, ffn_gain)
        gain_f_total = gain_f_total + gain_f_part
        grad_branch_b = (grad_delta + grad_middle).astype(narrow_float_type)
        grad_attended_b = (
            right_product(grad_branch_b, back_weights[3])
            .astype(narrow_float_type)
            .reshape(count_of_rows, KEY_VALUE_HEADS, query_groupings, HEAD_SIZE)
        )
        d_out = left_product(attended_b, grad_branch_b)
        grad_next = grad_next + grad_middle
        scores = masked_scores(query_b, keys_win, allowed)
        probs = jnp.exp(scores - log_total)
        probs_b = probs.astype(narrow_float_type)
        grad_probs = jnp.einsum(
            "qgjd,kgd->gjqk", grad_attended_b, values_win, preferred_element_type=wide_float_type
        )
        row_dot = jnp.sum(probs * grad_probs, axis=-1, keepdims=True)
        grad_scores_b = (probs * (grad_probs - row_dot)).astype(narrow_float_type)
        grad_queries = (
            jnp.einsum(
                "gjqk,kgd->qgjd", grad_scores_b, keys_win, preferred_element_type=wide_float_type
            )
            * 0.125
        )
        grad_keys = (
            jnp.einsum(
                "gjqk,qgjd->kgd", grad_scores_b, query_b, preferred_element_type=wide_float_type
            )
            * 0.125
        )
        grad_values = jnp.einsum(
            "gjqk,qgjd->kgd", probs_b, grad_attended_b, preferred_element_type=wide_float_type
        )
        extra_zero_rows = jnp.zeros((extra_rows, KEY_VALUE_HEADS, HEAD_SIZE), wide_float_type)
        local_span_keys = jnp.concatenate([extra_zero_rows, grad_keys], axis=0)
        local_span_values = jnp.concatenate([extra_zero_rows, grad_values], axis=0)
        for level in reversed(range(depth_levels)):
            older_rows = (1 << level) * count_of_rows
            back_keys, back_values = passed_along(
                (
                    for_sending(local_span_keys[:older_rows]),
                    for_sending(local_span_values[:older_rows]),
                ),
                "seq",
                -(1 << level),
            )
            local_span_keys = local_span_keys[older_rows:] + back_keys
            local_span_values = local_span_values[older_rows:] + back_values
        grad_query_b = (
            apply_rotation(
                grad_queries.reshape(count_of_rows, QUERY_HEADS, HEAD_SIZE),
                cosine_table,
                -sine_table,
            )
            .astype(narrow_float_type)
            .reshape(count_of_rows, QUERY_HEADS * HEAD_SIZE)
        )
        grad_key_b = (
            apply_rotation(local_span_keys, cosine_table, -sine_table)
            .astype(narrow_float_type)
            .reshape(count_of_rows, KEY_VALUE_HEADS * HEAD_SIZE)
        )
        value_gradient_copy = local_span_values.astype(narrow_float_type).reshape(
            count_of_rows, KEY_VALUE_HEADS * HEAD_SIZE
        )
        grad_normed = (
            right_product(grad_query_b, back_weights[0])
            + right_product(grad_key_b, back_weights[1])
            + right_product(value_gradient_copy, back_weights[2])
        )
        d_query = left_product(normalized_input_copy, grad_query_b)
        d_key = left_product(normalized_input_copy, grad_key_b)
        d_value = left_product(normalized_input_copy, value_gradient_copy)
        grad_input, gain_a_part = rms_backward(grad_normed, normal_a, inv_a, attn_gain)
        gain_a_total = gain_a_total + gain_a_part
        grad_state = grad_next + grad_input
        local_grads = (
            d_query.reshape(-1),
            d_key.reshape(-1),
            d_value.reshape(-1),
            d_out.reshape(-1),
            d_gate.reshape(-1),
            d_up.reshape(-1),
            d_down.reshape(-1),
        )
        summed = (
            lax.psum_scatter(local_grads[0], ("seq", "rep"), scatter_dimension=0, tiled=True),
            lax.psum_scatter(local_grads[1], ("seq", "rep"), scatter_dimension=0, tiled=True),
            lax.psum_scatter(local_grads[2], ("seq", "rep"), scatter_dimension=0, tiled=True),
            lax.psum_scatter(local_grads[3], ("seq", "rep"), scatter_dimension=0, tiled=True),
            lax.psum_scatter(local_grads[4], ("seq", "rep"), scatter_dimension=0, tiled=True),
            lax.psum_scatter(local_grads[5], ("seq", "rep"), scatter_dimension=0, tiled=True),
            lax.psum_scatter(local_grads[6], ("seq", "rep"), scatter_dimension=0, tiled=True),
        )
        shares = tuple((old_share + new_share for old_share, new_share in zip(shares, summed)))
    router_grad = jnp.stack(router_rows, axis=0)
    gain_a_sum, gain_f_sum, router_sum = lax.psum(
        (gain_a_total, gain_f_total, router_grad), ("seq", "rep")
    )
    return (
        output[None],
        grad_state[None],
        shares[0],
        shares[1],
        shares[2],
        shares[3],
        shares[4],
        shares[5],
        shares[6],
        gain_a_sum,
        gain_f_sum,
        router_sum,
    )


MESH = pl.DeviceIdType.MESH
N_Z = 4
BLOCKS = ((32, 2816), (32, 2560), (32, 2560), (80, 1024))
GATHER_ORDERS = ("uzw", "zuw", "uzw", "zuw")
REDUCE_ORDERS = ("uzw", "uzw", "zuw", "zuw")


def place():
    seq = lax.axis_index("seq")
    rep = lax.axis_index("rep")
    z, x, y, core = seq // 2, seq % 2, rep // 2, rep % 2
    return z, x + core * (y - x), y + core * (x - y), core


def device_of(z, u, w, core):
    x, y = u + core * (w - u), w + core * (u - w)
    return (z * 2 + x, y * 2 + core)


def block_of(z, u, w, core):
    seq, rep = device_of(z, u, w, core)
    return seq * 4 + rep


def remote(src, dst, send_sem, recv_sem, device):
    return pltpu.make_async_remote_copy(
        src_ref=src,
        dst_ref=dst,
        send_sem=send_sem,
        recv_sem=recv_sem,
        device_id=device,
        device_id_type=MESH,
    )


def gather_events():
    events = [("own", group) for group in (1, 2, 0, 3)]
    for step in range(6):
        for group in range(4):
            if GATHER_ORDERS[group] == "zuw":
                if 1 <= step <= 3:
                    events.append(("z", group, step, 0))
                if 1 <= step <= 4:
                    events.append(("u", group, step - 1))
                    events.append(("w", group, step - 1, 0))
                if 2 <= step <= 5:
                    events.append(("w", group, step - 2, 1))
            else:
                if step == 1:
                    events.append(("first", group))
                if 1 <= step <= 3:
                    events.append(("z", group, step, 0))
                if 2 <= step <= 4:
                    events.append(("z", group, step - 1, 1))
                if 1 <= step <= 4:
                    events.append(("w", group, step - 1, 0))
                if 2 <= step <= 5:
                    events.append(("w", group, step - 2, 1))
    return events


def move_partners():
    seq, rep = lax.axis_index("seq"), lax.axis_index("rep")
    apart = (seq * 4 + rep) * (seq * 4 + rep - 13)
    return device_of_span(rep, seq), span_of_device()[::-1], (apart * apart + 999999) // 1000000


def start_moves(leaving, arriving, send_sem, recv_sem, target, moves):
    for i, (src, dst) in enumerate(zip(leaving, arriving)):

        @pl.when(moves == 1)
        def _():
            remote(src, dst, send_sem.at[i], recv_sem.at[i], target).start()

        @pl.when(moves == 0)
        def _():
            pltpu.make_async_copy(src, dst, recv_sem.at[i]).start()


def wait_moves(leaving, arriving, send_sem, recv_sem, target, moves):
    for i, (src, dst) in enumerate(zip(leaving, arriving)):

        @pl.when(moves == 1)
        def _():
            remote(src, dst, send_sem.at[i], recv_sem.at[i], target).wait()

        @pl.when(moves == 0)
        def _():
            pltpu.make_async_copy(src, dst, recv_sem.at[i]).wait()


def set_meta(meta, depths, spans):
    own = lax.axis_index("seq")
    first, end = 0, 0
    for sequence in range(spans.shape[1]):
        end = end + spans[0, sequence]
        first = jnp.where(end <= own, end, first)
    row = lax.broadcasted_iota(jnp.int32, (8, 128), 0)
    values = jnp.where(row == 0, depths[...], jnp.where(row == 1, own - first, 0))
    meta[...] = values.astype(jnp.float32)


def gather_kernel(*refs):
    flat_in, tokens, depths, spans, places = refs[:7], refs[7], refs[8], refs[9], refs[10]
    full, arriving = refs[11:15], refs[15:17]
    flat, own, meta = refs[17:24], refs[24:28], refs[28]
    spread, tiles, natural, long_rows = refs[29:33]
    recv_sem, z_sem, u_sem, w_sem, core_sem, local_sem, move_send, move_recv, flat_sem = refs[33:]
    leaving = (tokens, meta)
    z, u, w, core = place()
    me = block_of(z, u, w, core)
    target, source, moves = move_partners()
    above, below = device_of(z + 1, u, w, core), device_of(z - 1, u, w, core)
    across_u, across_w = device_of(z, 1 - u, w, core), device_of(z, u, 1 - w, core)
    sibling = device_of(z, w, u, 1 - core)

    loads = [
        pltpu.make_async_copy(src, dst, flat_sem.at[i])
        for i, (src, dst) in enumerate(zip(flat_in, flat))
    ]
    for copy in loads:
        copy.start()
    barrier = pltpu.get_barrier_semaphore()
    for device in (across_u, across_w, sibling):
        pl.semaphore_signal(barrier, inc=1, device_id=device, device_id_type=MESH)

    @pl.when(moves == 1)
    def _():
        pl.semaphore_signal(barrier, inc=1, device_id=target, device_id_type=MESH)
        pl.semaphore_signal(barrier, inc=1, device_id=source, device_id_type=MESH)

    @pl.when(z < N_Z - 1)
    def _():
        pl.semaphore_signal(barrier, inc=1, device_id=above, device_id_type=MESH)

    @pl.when(z > 0)
    def _():
        pl.semaphore_signal(barrier, inc=1, device_id=below, device_id_type=MESH)

    set_meta(meta, depths, spans)
    for copy in loads:
        copy.wait()
    pack_wide(flat, own, tiles)
    pl.semaphore_wait(barrier, 4 + (z + 1) // 2 - z // 3 * 2 + 2 * moves)

    def rows(group, block):
        count = BLOCKS[group][0]
        return full[group].at[pl.ds(pl.multiple_of(block * count, 16), count)]

    def copy(group, block, src, send_sem, device):
        return remote(src, rows(group, block), send_sem, recv_sem.at[group, block], device)

    def send(group, block, src, ways, slot=0):
        if "z" in ways:

            @pl.when(z < N_Z - 1)
            def _():
                copy(group, block, src, z_sem.at[group, 0, slot], above).start()

            @pl.when(z > 0)
            def _():
                copy(group, block, src, z_sem.at[group, 1, slot], below).start()

        if "+" in ways:

            @pl.when(z < N_Z - 1)
            def _():
                copy(group, block, src, z_sem.at[group, 0, slot], above).start()

        if "-" in ways:

            @pl.when(z > 0)
            def _():
                copy(group, block, src, z_sem.at[group, 1, slot], below).start()

        if "u" in ways:
            copy(group, block, src, u_sem.at[group], across_u).start()
        if "w" in ways:
            copy(group, block, src, w_sem.at[group], across_w).start()
        if "c" in ways:
            copy(group, block, src, core_sem.at[group], sibling).start()

    def passed_on(group, block, ways, slot=0):
        copy(group, block, rows(group, block), core_sem.at[group], sibling).wait_recv()
        send(group, block, rows(group, block), ways, slot)

    def at_distance(step, action):
        if step == 0:
            action(z, "")
            return

        @pl.when(z - step >= 0)
        def _():
            action(z - step, "+")

        @pl.when(z + step < N_Z)
        def _():
            action(z + step, "-")

    def own_event(group):
        send(group, me, own[group], "zuwc")
        pltpu.make_async_copy(own[group], rows(group, me), local_sem.at[group]).start()

    def first_event(group):
        passed_on(group, block_of(z, 1 - u, w, core), "zwc", 1)

    def z_event(group, step, other):
        z_first = GATHER_ORDERS[group] == "zuw"
        column = 1 - u if other else u
        slot = step if z_first else 2 * step + other
        at_distance(
            step,
            lambda far, way: passed_on(
                group,
                block_of(far, column, w, core),
                way + ("uwc" if z_first else "wc"),
                slot,
            ),
        )

    def u_event(group, step):
        at_distance(
            step, lambda far, way: passed_on(group, block_of(far, 1 - u, w, core), "wc")
        )

    def w_event(group, step, other):
        column = 1 - u if other else u
        at_distance(
            step, lambda far, way: passed_on(group, block_of(far, column, 1 - w, core), "c")
        )

    actions = {"own": own_event, "first": first_event, "z": z_event, "u": u_event, "w": w_event}
    for event in gather_events():
        if event == ("own", 0):
            fill_spread(spread, places)
            pack_rest(flat, own, spread, tiles, natural, long_rows)
        if event == ("z", 0, 1, 0):
            start_moves(leaving, arriving, move_send, move_recv, target, moves)
        actions[event[0]](*event[1:])
    wait_moves(leaving, arriving, move_send, move_recv, target, moves)

    for group in range(4):
        z_first = GATHER_ORDERS[group] == "zuw"
        count = BLOCKS[group][0]
        pltpu.make_async_copy(own[group], rows(group, me), local_sem.at[group]).wait()

        @pl.loop(0, 16)
        def _(i):
            block = i * 2 + (1 - core)
            copy(group, block, rows(group, block), core_sem.at[group], sibling).wait_recv()

        for sem, sends in ((u_sem, 4 if z_first else 1), (w_sem, 8), (core_sem, 16)):
            part = full[group].at[pl.ds(0, sends * count)]
            remote(part, part, sem.at[group], recv_sem.at[group, 0], sibling).wait_send()
        for step in range(N_Z):
            for other in (0,) if z_first else (0, 1):
                slot = step if z_first else 2 * step + other

                @pl.when((z - step >= 0) & (z < N_Z - 1))
                def _():
                    copy(group, me, own[group], z_sem.at[group, 0, slot], above).wait_send()

                @pl.when((z + step < N_Z) & (z > 0))
                def _():
                    copy(group, me, own[group], z_sem.at[group, 1, slot], below).wait_send()


def gather_weights(flat, tokens, depths, spans):
    narrow, wide, vmem, sems = jnp.bfloat16, jnp.float32, pltpu.VMEM, pltpu.SemaphoreType.DMA
    anywhere, here = pl.BlockSpec(memory_space=pl.ANY), pl.BlockSpec(memory_space=vmem)
    flat = [x.reshape(-1, 128) for x in flat]
    return pl.pallas_call(
        gather_kernel,
        out_shape=[jax.ShapeDtypeStruct((32 * rows, columns), narrow) for rows, columns in BLOCKS]
        + [jax.ShapeDtypeStruct(tokens.shape, narrow), jax.ShapeDtypeStruct((8, 128), wide)],
        in_specs=[anywhere] * 8 + [here, pl.BlockSpec(memory_space=pltpu.SMEM), here],
        out_specs=[anywhere] * 6,
        scratch_shapes=[vmem(x.shape, wide) for x in flat]
        + [vmem(shape, narrow) for shape in BLOCKS]
        + [
            vmem((8, 128), wide),
            vmem((MODEL_WIDTH, 1024), narrow),
            vmem((20, 32, 128), wide),
            vmem((8, 32, 128), wide),
            vmem((8, 80, 128), wide),
            sems((4, 32)),
            sems((4, 2, 8)),
            sems((4,)),
            sems((4,)),
            sems((4,)),
            sems((4,)),
            sems((2,)),
            sems((2,)),
            sems((7,)),
        ],
        compiler_params=pltpu.CompilerParams(
            collective_id=1, has_side_effects=True, vmem_limit_bytes=59 * 2**20
        ),
        name="gather_weights",
    )(*flat, tokens, depths, spans, natural_places())


REDUCE_STEPS = (
    ("make", 2, 2),
    ("make", 2, 1),
    ("small", -1),
    ("w", 2, 2),
    ("make", 0, 3),
    ("w", 0, 3),
    ("make", 1, 3),
    ("make", 2, 3),
    ("w", 1, 3),
    ("u", 2, 2),
    ("make", 0, 2),
    ("w", 2, 1),
    ("z_early", 1, 3, 1),
    ("make", 3, 3),
    ("w", 0, 2),
    ("z_early", 1, 3, 0),
    ("w", 3, 3),
    ("w", 2, 3),
    ("z_early", 0, 3, 1),
    ("make", 0, 1),
    ("make", 1, 1),
    ("z_early", 0, 3, 0),
    ("make", 3, 1),
    ("small", 0),
    ("w", 0, 1),
    ("w", 1, 1),
    ("z_early", 0, 2, 0),
    ("make", 1, 2),
    ("z_early", 0, 2, 1),
    ("make", 3, 2),
    ("u", 2, 1),
    ("u", 2, 3),
    ("z_early", 0, 1, 0),
    ("w", 1, 2),
    ("z_early", 0, 1, 1),
    ("small", 1),
    ("w", 3, 1),
    ("z_early", 1, 2, 1),
    ("z_late", 2, 3),
    ("u", 3, 3),
    ("w", 3, 2),
    ("make", 2, 0),
    ("u", 3, 1),
    ("make", 1, 0),
    ("z_late", 2, 2),
    ("z_early", 1, 1, 1),
    ("w", 2, 0),
    ("make", 0, 0),
    ("w", 1, 0),
    ("make", 3, 0),
    ("z_early", 1, 2, 0),
    ("w", 0, 0),
    ("z_late", 2, 1),
    ("small", 2),
    ("z_early", 1, 1, 0),
    ("u", 3, 2),
    ("z_early", 0, 0, 1),
    ("z_late", 3, 3),
    ("small", 3),
    ("z_early", 0, 0, 0),
    ("z_early", 1, 0, 1),
    ("z_early", 1, 0, 0),
    ("w", 3, 0),
    ("u", 2, 0),
    ("z_late", 3, 2),
    ("u_late", 1),
    ("u", 3, 0),
    ("z_late", 3, 1),
    ("small", 4),
    ("u_late", 0),
    ("z_late", 2, 0),
    ("z_late", 3, 0),
)


def reduce_kernel(*refs):
    factors_in, small_in, leaving = refs[:9], refs[9], refs[10:11]
    final, small_out, arriving = refs[11:15], refs[15], refs[16:17]
    part, from_core, from_w, from_u, from_z = (refs[17 + 4 * i : 21 + 4 * i] for i in range(5))
    factors, turned = refs[37:46], refs[46]
    small_held, small_got = refs[47:49]
    (
        load_sem,
        core_send,
        core_recv,
        w_send,
        w_recv,
        u_send,
        u_recv,
        z_send,
        z_recv,
        small_send,
        small_recv,
        move_send,
        move_recv,
    ) = refs[49:]
    source, target, moves = move_partners()
    z, u, w, core = place()
    me = block_of(z, u, w, core)
    above, below = device_of(z + 1, u, w, core), device_of(z - 1, u, w, core)
    across_u, across_w = device_of(z, 1 - u, w, core), device_of(z, u, 1 - w, core)
    sibling = device_of(z, w, u, 1 - core)
    near, far_z = z + 1 - 2 * (z % 2), (z + 2) % 4
    partners = (
        sibling,
        across_u,
        across_w,
        device_of(near, u, w, core),
        device_of(far_z, u, w, core),
    )
    middle_z = (z == 1) | (z == 2)

    barrier = pltpu.get_barrier_semaphore()
    for device in partners:
        pl.semaphore_signal(barrier, inc=1, device_id=device, device_id_type=MESH)

    @pl.when(moves == 1)
    def _():
        pl.semaphore_signal(barrier, inc=1, device_id=target, device_id_type=MESH)
        pl.semaphore_signal(barrier, inc=1, device_id=source, device_id_type=MESH)

    @pl.when(middle_z)
    def _():
        pl.semaphore_signal(
            barrier, inc=1, device_id=device_of(3 - z, u, w, core), device_id_type=MESH
        )

    def load(i):
        return pltpu.make_async_copy(factors_in[i], factors[i], load_sem.at[i])

    loaded = set()
    for i in LOAD_ORDER:
        load(i).start()

    pl.semaphore_wait(barrier, 5 + (z + 1) // 2 - z // 3 * 2 + 2 * moves)

    def rows(group, block):
        count = BLOCKS[group][0]
        return part[group].at[pl.ds(pl.multiple_of(block * count, 16), count)]

    def slot_of(far, column, line):
        return (far * 2 + column) * 2 + line

    def small_copy(i):
        return remote(
            small_held.at[i], small_got.at[i], small_send.at[i], small_recv.at[i], partners[i]
        )

    def small_event(i):
        if i < 0:
            small_held[0] = small_in[...]
            small_copy(0).start()
            return
        small_copy(i).wait_recv()
        total = small_held[i] + small_got[i]
        if i < 4:
            small_held[i + 1] = total
            small_copy(i + 1).start()
        else:
            small_out[...] = total

    def product(group, plane, left, right, first, width, chunk):
        count = 8 * BLOCKS[group][0]
        at = pl.multiple_of(plane * count, 128)
        turned[0:count, :] = factors[left][:, pl.ds(at, count)].T

        @pl.loop(0, width // chunk)
        def _(j):
            here = pl.multiple_of(j * chunk, 128)
            there = pl.multiple_of(first + j * chunk, 128)
            part[group][pl.ds(at, count), pl.ds(there, chunk)] = jnp.dot(
                turned[0:count, :],
                factors[right][:, pl.ds(here, chunk)],
                preferred_element_type=jnp.float32,
            ).astype(jnp.bfloat16)

    def make_event(group, step):
        for i in NEEDED[group]:
            if i not in loaded:
                load(i).wait()
                loaded.add(i)

        plane = (z, z + 1 - 2 * (z % 2), (z + 2) % 4, 3 - z)[step]
        for left, right, first, width, chunk in PRODUCTS[group]:
            product(group, plane, left, right, first, width, chunk)
        for column in (0, 1):
            for line in (0, 1):
                slot = slot_of(plane, column, line)
                remote(
                    rows(group, block_of(plane, column, line, 1 - core)),
                    from_core[group].at[slot],
                    core_send.at[group],
                    core_recv.at[group, slot],
                    sibling,
                ).start()

    def wait_core(group, slot):
        held = from_core[group].at[slot]
        remote(held, held, core_send.at[group], core_recv.at[group, slot], sibling).wait_recv()

    def accumulate(group, block, terms):
        count = BLOCKS[group][0]
        first = pl.multiple_of(block * count, 16)

        @pl.loop(0, count // 16)
        def _(i):
            at = pl.multiple_of(i * 16, 16)
            total = part[group][pl.ds(first + at, 16), :].astype(jnp.float32)
            for ref, slot in terms:
                total = total + ref[slot, pl.ds(at, 16), :].astype(jnp.float32)
            part[group][pl.ds(first + at, 16), :] = total.astype(jnp.bfloat16)

    def at_distance(step, action):
        if step == 0:
            action(z, 0)
            return

        @pl.when(z + step < N_Z)
        def _():
            action(z + step, 1)

        @pl.when(z - step >= 0)
        def _():
            action(z - step, -1)

    def wait_w(group, slot):
        held = from_w[group].at[slot]
        remote(held, held, w_send.at[group], w_recv.at[group, slot], across_w).wait_recv()

    def w_event(group, step):
        def action(far, way, column):
            block, slot = block_of(far, column, 1 - w, core), slot_of(far, column, 1 - w)
            wait_core(group, slot)
            accumulate(group, block, [(from_core[group], slot)])
            remote(
                rows(group, block),
                from_w[group].at[far * 2 + column],
                w_send.at[group],
                w_recv.at[group, far * 2 + column],
                across_w,
            ).start()

        for column in (1 - u, u):
            at_distance(step, lambda far, way: action(far, way, column))

    def gathered(group, far, column):
        slot = slot_of(far, column, w)
        wait_core(group, slot)
        wait_w(group, far * 2 + column)
        return [(from_core[group], slot), (from_w[group], far * 2 + column)]

    def u_copy(group, src, slot):
        return remote(
            src, from_u[group].at[slot], u_send.at[group], u_recv.at[group, slot], across_u
        )

    def u_event(group, step):
        def action(far, way):
            block = block_of(far, 1 - u, w, core)
            accumulate(group, block, gathered(group, far, 1 - u))
            u_copy(group, rows(group, block), far).start()

        at_distance(step, action)

    def z_copy(group, block, way, slot):
        return remote(
            rows(group, block),
            from_z[group].at[slot],
            z_send.at[group, way, slot],
            z_recv.at[group, slot],
            below if way else above,
        )

    def z_take(group, block, way, slot):
        z_copy(group, block, way, slot).wait_recv()
        accumulate(group, block, [(from_z[group], slot)])

    def z_step(group, step, column, z_slot, terms_of):
        def action(far, way):
            block = block_of(far, column, w, core)
            accumulate(group, block, terms_of(far))
            if way >= 0:

                @pl.when(z > 0)
                def _():
                    z_take(group, block, 0, z_slot(far))

            if way <= 0:

                @pl.when(z < N_Z - 1)
                def _():
                    z_take(group, block, 1, z_slot(far if way else 4))

            if way:
                slot = z_slot(4 if way < 0 and step == 1 else far)
                z_copy(group, block, 0 if way > 0 else 1, slot).start()

        at_distance(step, action)

    def finish(group):
        count = BLOCKS[group][0]
        final[group][...] = part[group][
            pl.ds(pl.multiple_of(me * count, 16), count), :
        ].astype(jnp.float32)

    def z_late_event(group, step):
        def terms_of(far):
            terms = gathered(group, far, u)
            u_copy(group, from_u[group].at[far], far).wait_recv()
            return terms + [(from_u[group], far)]

        z_step(group, step, u, lambda far: far, terms_of)
        if step == 0:
            finish(group)

    def z_early_event(group, step, other):
        column = 1 - u if other else u
        z_step(
            group,
            step,
            column,
            lambda far: far * 2 + column,
            lambda far: gathered(group, far, column),
        )
        if step == 0 and other:
            u_copy(group, rows(group, block_of(z, 1 - u, w, core)), 0).start()

    def u_late_event(group):
        u_copy(group, from_u[group].at[0], 0).wait_recv()
        accumulate(group, me, [(from_u[group], 0)])
        finish(group)

    actions = {
        "small": small_event,
        "make": make_event,
        "w": w_event,
        "u": u_event,
        "z_early": z_early_event,
        "z_late": z_late_event,
        "u_late": u_late_event,
    }
    start_moves(leaving, arriving, move_send, move_recv, target, moves)
    for event in REDUCE_STEPS:
        actions[event[0]](*event[1:])
    wait_moves(leaving, arriving, move_send, move_recv, target, moves)

    for group in range(4):
        z_first = REDUCE_ORDERS[group] == "zuw"
        count = BLOCKS[group][0]
        for sem, sends in ((core_send, 16), (w_send, 8), (u_send, 4 if z_first else 1)):
            rows_sent = part[group].at[pl.ds(0, sends * count)]
            remote(
                rows_sent, rows_sent, sem.at[group], core_recv.at[group, 0], sibling
            ).wait_send()
        for far in range(N_Z):
            for column in (0,) if z_first else (0, 1):
                slot = far if z_first else far * 2 + column

                @pl.when(z < far)
                def _():
                    z_copy(group, me, 0, slot).wait_send()

                @pl.when(z > far + 1)
                def _():
                    z_copy(group, me, 1, slot).wait_send()

        for column in (0,) if z_first else (0, 1):

            @pl.when(z > 0)
            def _():
                z_copy(group, me, 1, 4 if z_first else 8 + column).wait_send()

    for i in range(5):
        small_copy(i).wait_send()


LOAD_ORDER = (4, 6, 0, 1, 2, 3, 5, 7, 8)
NEEDED = ((0, 1, 2, 3), (4, 5), (4, 6), (7, 8))
PRODUCTS = (
    ((0, 1, 0, 1792, 256), (2, 3, 1792, 1024, 512)),
    ((4, 5, 0, 2560, 512),),
    ((4, 6, 0, 2560, 512),),
    ((7, 8, 0, 1024, 512),),
)


def reduce_gradients(factors, small, leaving):
    narrow, sems, vmem = jnp.bfloat16, pltpu.SemaphoreType.DMA, pltpu.VMEM
    z_first = [order == "zuw" for order in REDUCE_ORDERS]
    scratch = [vmem((32 * rows, columns), narrow) for rows, columns in BLOCKS]
    scratch += [vmem((16, rows, columns), narrow) for rows, columns in BLOCKS]
    scratch += [vmem((8, rows, columns), narrow) for rows, columns in BLOCKS]
    scratch += [
        vmem((4 if first else 1, rows, columns), narrow)
        for (rows, columns), first in zip(BLOCKS, z_first)
    ]
    scratch += [
        vmem((5 if first else 10, rows, columns), narrow)
        for (rows, columns), first in zip(BLOCKS, z_first)
    ]
    scratch += [vmem(x.shape, narrow) for x in factors]
    scratch += [vmem((640, RECUR * 128), narrow)]
    scratch += [vmem((5, 8, 1024), jnp.float32)] * 2
    scratch += [
        sems((9,)),
        sems((4,)),
        sems((4, 16)),
        sems((4,)),
        sems((4, 8)),
        sems((4,)),
        sems((4, 4)),
        sems((4, 2, 10)),
        sems((4, 10)),
        sems((5,)),
        sems((5,)),
        sems((1,)),
        sems((1,)),
    ]
    anywhere, here = pl.BlockSpec(memory_space=pl.ANY), pl.BlockSpec(memory_space=vmem)
    return pl.pallas_call(
        reduce_kernel,
        out_shape=[jax.ShapeDtypeStruct(shape, jnp.float32) for shape in BLOCKS]
        + [jax.ShapeDtypeStruct((8, 1024), jnp.float32)]
        + [jax.ShapeDtypeStruct(x.shape, x.dtype) for x in leaving],
        in_specs=[anywhere] * 9 + [here, anywhere],
        out_specs=[here] * 5 + [anywhere],
        scratch_shapes=scratch,
        compiler_params=pltpu.CompilerParams(
            collective_id=2, has_side_effects=True, vmem_limit_bytes=60 * 2**20
        ),
        name="reduce_gradients",
    )(*factors, small, *leaving)


Q_TILES = 9
O_AT, KV_AT, KV_WIDTH = 1792, 1152, 640
CHUNK = 1280
SUB = 64


def dot_nn(left, right):
    return jnp.dot(left, right, preferred_element_type=jnp.float32)


def dot_nt(left, right):
    return lax.dot_general(
        left, right, (((1,), (1,)), ((), ())), preferred_element_type=jnp.float32
    )


def span_of_device():
    seq = lax.axis_index("seq")
    rep = lax.axis_index("rep")
    z, x, y, core = seq // 2, seq % 2, rep // 2, rep % 2
    return z, (2 * y + x + y * (1 - 2 * x)) * 2 + core


def device_of_span(group, span):
    chip = span // 2
    x, y = (chip + 1) // 2 % 2, chip // 2
    return (group * 2 + x, y * 2 + span % 2)


def lanes(shape):
    return lax.broadcasted_iota(jnp.int32, shape, 1)


def rotated(value, cosine, sine):
    first = lanes(value.shape) % 64 < 32
    partner = jnp.where(first, pltpu.roll(value, 96, 1), pltpu.roll(value, 32, 1))
    return value * cosine + partner * sine


def block_kernel(*refs):
    (tokens, cotangent, meta, rope, turn, gain_a, gain_f, routers, wa_in, wg_in, wu_in, wd_in) = refs[:12]
    (output, input_grad, small) = refs[12:15]
    a_out, gqkv_out, o_out, gt_out, b_out, gg_all, gu_all, hidden_out, gf_out = refs[15:24]
    (
        wa, wg, wu, wd, gains, natural_at, padded_at, cotangent_at, leaving, h_all, z_all, tf_all, gate_all, up_all, q_all, window_two, window_one,
        got_two, got_one, sending_two, sending_one, depth_win, depth_at, bias_at, cos_at, sin_at, stats, dkv, grad, acc, gg_at, gu_at,
        keys_at, s_at, gp_at, p_at, gs_at, qs_at, us_at, move_send, move_recv, a_all, gqkv_all, o_all, gt_all, b_all, hidden_all, gf_all, factor_sem,
        load_sem, out_sem, kv_send, kv_recv, back_send, back_recv, depth_send, depth_recv,
    ) = refs[24:]
    narrow, wide = jnp.bfloat16, jnp.float32
    group, span = span_of_device()
    core = span % 2
    target, source, moves = move_partners()

    barrier = pltpu.get_barrier_semaphore()
    for away in (1, 2, 3):

        @pl.when(span + away < 8)
        def _():
            pl.semaphore_signal(
                barrier, inc=1, device_id=device_of_span(group, span + away), device_id_type=MESH
            )

        @pl.when(span - away >= 0)
        def _():
            pl.semaphore_signal(
                barrier, inc=1, device_id=device_of_span(group, span - away), device_id_type=MESH
            )

    @pl.when(moves == 1)
    def _():
        pl.semaphore_signal(barrier, inc=1, device_id=target, device_id_type=MESH)
        pl.semaphore_signal(barrier, inc=1, device_id=source, device_id_type=MESH)

    loads = [
        pltpu.make_async_copy(src, dst, load_sem.at[i])
        for i, (src, dst) in enumerate(((wa_in, wa), (wg_in, wg), (wu_in, wu), (wd_in, wd)))
    ]
    for load in loads:
        load.start()

    depth_win[3] = jnp.broadcast_to(meta[0:1, :], (8, 128))
    for away in (1, 2, 3):

        @pl.when(span - away < 0)
        def _():
            depth_win[3 - away] = jnp.zeros((8, 128), wide)
            for recursion in range(RECUR):
                window_two[recursion, 3 - away] = jnp.zeros((2, 128, 256), narrow)
                window_one[recursion, 3 - away] = jnp.zeros((128, 128), narrow)


    def depth_copy(away, device):
        return remote(
            depth_win.at[3],
            depth_win.at[3 - away],
            depth_send.at[away - 1],
            depth_recv.at[away - 1],
            device,
        )

    def window(recursion, slot, pair):
        if pair == 2:
            return window_one.at[recursion, slot]
        return window_two.at[recursion, slot, pair]

    def kv_copy(recursion, pair, slot, to_slot, sent, device):
        return remote(
            window(recursion, slot, pair),
            window(recursion, to_slot, pair),
            kv_send.at[recursion, pair, sent],
            kv_recv.at[recursion, pair, to_slot],
            device,
        )

    def sending(slot, pair):
        return sending_one.at[slot] if pair == 2 else sending_two.at[slot, pair]

    def got(recursion, slot, pair):
        return got_one.at[recursion, slot] if pair == 2 else got_two.at[recursion, slot, pair]

    def back_copy(recursion, pair, slot, device):
        return remote(
            sending(slot, pair),
            got(recursion, slot, pair),
            back_send.at[recursion, pair, slot],
            back_recv.at[recursion, pair, slot],
            device,
        )

    def pair_lanes(pair):
        return slice(512, 640) if pair == 2 else slice(pair * 256, pair * 256 + 256)

    def factor_copies(recursion, which):
        pairs = (
            (a_all, a_out),
            (o_all, o_out),
            (b_all, b_out),
            (hidden_all, hidden_out),
            (gf_all, gf_out),
            (gt_all, gt_out),
            (gqkv_all, gqkv_out),
        )
        return [
            pltpu.make_async_copy(
                pairs[i][0].at[recursion], pairs[i][1].at[recursion], factor_sem.at[i, recursion]
            )
            for i in which
        ]

    def stage_copies(recursion):
        return [
            pltpu.make_async_copy(gg_at, gg_all.at[recursion], out_sem.at[0]),
            pltpu.make_async_copy(gu_at, gu_all.at[recursion], out_sem.at[1]),
        ]

    def neighbour(away):
        return device_of_span(group, span + away)

    sibling = neighbour(1 - 2 * core)

    def when(condition, action):
        @pl.when(condition)
        def _():
            action()

    def send_keys(recursion, pair):
        when(span + 2 < 8, lambda: kv_copy(recursion, pair, 3, 1, 0, neighbour(2)).start())
        when(core == 0, lambda: kv_copy(recursion, pair, 3, 2, 1, sibling).start())
        when(
            (core == 1) & (span + 3 < 8),
            lambda: kv_copy(recursion, pair, 3, 0, 1, neighbour(3)).start(),
        )

    def pass_keys_on(recursion, pair):
        @pl.when(span >= 2)
        def _():
            kv_copy(recursion, pair, 3, 1, 0, sibling).wait_recv()
            kv_copy(recursion, pair, 1, 2 * core, 2, sibling).start()

    def wait_keys(recursion, pair):
        when(span >= 1, lambda: kv_copy(recursion, pair, 3, 2, 1, sibling).wait_recv())
        when(span >= 3, lambda: kv_copy(recursion, pair, 3, 0, 1, sibling).wait_recv())

    def wait_keys_sent(recursion, pair):
        when(span + 2 < 8, lambda: kv_copy(recursion, pair, 3, 1, 0, sibling).wait_send())
        when(core == 0, lambda: kv_copy(recursion, pair, 3, 2, 1, sibling).wait_send())
        when(
            (core == 1) & (span + 3 < 8),
            lambda: kv_copy(recursion, pair, 3, 0, 1, sibling).wait_send(),
        )
        when(span >= 2, lambda: kv_copy(recursion, pair, 1, 2, 2, sibling).wait_send())

    def send_back(recursion, pair):
        at = pair_lanes(pair)

        @pl.when(span >= 2)
        def _():
            first = pl.multiple_of(256 * (1 - core), 128)
            sending(0, pair)[...] = dkv[pl.ds(first, 128), at].astype(narrow)
            back_copy(recursion, pair, 0, sibling).start()

        sending(2, pair)[...] = dkv[
            pl.ds(pl.multiple_of(256 * core, 128), 128), at
        ].astype(narrow)
        when(core == 1, lambda: back_copy(recursion, pair, 2, sibling).start())
        when(
            (core == 0) & (span >= 3),
            lambda: back_copy(recursion, pair, 2, neighbour(-3)).start(),
        )

    def pass_back_on(recursion, pair):
        @pl.when(span >= 2)
        def _():
            back_copy(recursion, pair, 0, sibling).wait_recv()
            sending(1, pair)[...] = (
                dkv[128:256, pair_lanes(pair)] + got(recursion, 0, pair)[...].astype(wide)
            ).astype(narrow)
            back_copy(recursion, pair, 1, neighbour(-2)).start()

    def take_back(recursion, pair):
        at = pair_lanes(pair)

        @pl.when((core == 0) | (span + 3 < 8))
        def _():
            back_copy(recursion, pair, 2, sibling).wait_recv()
            dkv[384:512, at] += got(recursion, 2, pair)[...].astype(wide)

        @pl.when(span + 2 < 8)
        def _():
            back_copy(recursion, pair, 1, sibling).wait_recv()
            dkv[384:512, at] += got(recursion, 1, pair)[...].astype(wide)

    def wait_back_sent(recursion, pair):
        when(span >= 2, lambda: back_copy(recursion, pair, 0, sibling).wait_send())
        when(span >= 2, lambda: back_copy(recursion, pair, 1, sibling).wait_send())
        when((core == 1) | (span >= 3), lambda: back_copy(recursion, pair, 2, sibling).wait_send())

    def add_pads():
        for block in range(32):
            padded_at[block * PADDED_ROWS : block * PADDED_ROWS + OWN_ROWS, :] = natural_at[
                block * OWN_ROWS : block * OWN_ROWS + OWN_ROWS, :
            ]

    def drop_pads():
        for block in range(32):
            natural_at[block * OWN_ROWS : block * OWN_ROWS + OWN_ROWS, :] = padded_at[
                block * PADDED_ROWS : block * PADDED_ROWS + OWN_ROWS, :
            ]

    here = device_of_span(group, span)

    span_lane = meta[1:2, :]
    turn_cos = jnp.zeros((1, 128), wide)
    turn_sin = jnp.zeros((1, 128), wide)
    for k in range(4):
        turn_cos = turn_cos + jnp.where(span_lane == k, turn[k : k + 1, :], 0.0)
        turn_sin = turn_sin + jnp.where(span_lane == k, turn[8 + k : 9 + k, :], 0.0)
    cos_at[...] = turn_cos * rope[0] - turn_sin * rope[1]
    sign = jnp.where(lanes((128, 128)) % 64 < 32, -1.0, 1.0)
    sin_at[...] = sign * (turn_sin * rope[0] + turn_cos * rope[1])

    padded_at[...] = jnp.zeros((1024, 128), wide)
    vectors = jnp.concatenate(
        [gain_a[...], gain_f[...], routers[...], jnp.zeros((123, MODEL_WIDTH), wide)], axis=0
    )
    natural_at[...] = vectors.T
    add_pads()
    gains[...] = padded_at[...].T[0:8, :]
    natural_at[...] = tokens[...].astype(wide)
    add_pads()
    h_all[0] = padded_at[...].T
    pl.semaphore_wait(barrier, 3 + span + span // 4 * (7 - 2 * span) + 2 * moves)
    for away in (1, 2, 3):
        when(span + away < 8, lambda: depth_copy(away, neighbour(away)).start())
    small[...] = jnp.zeros((8, 1024), wide)

    row = lax.broadcasted_iota(jnp.int32, (128, 128), 0)
    column = lanes((128, 128))
    ones = jnp.ones((128, 128), wide)
    def set_depths():
        for away in (1, 2, 3):
            when(span - away >= 0, lambda: depth_copy(away, here).wait_recv())
        for block in range(4):
            held = depth_win[block]
            depth_at[pl.ds(block * 128, 128), :] = dot_nn(
                jnp.where(row == column, jnp.broadcast_to(held[0:1, :], (128, 128)), 0.0), ones
            ).astype(narrow)

    def set_bias(recursion):
        level = recursion.astype(wide)
        for block in range(4):
            active = depth_at[pl.ds(block * 128, 128), :].astype(wide) > level
            if block == 3:
                allowed = (row == column) | (active & (row <= column))
            else:
                allowed = active & (span_lane >= 3 - block)
            bias_at[pl.ds(block * 128, 128), :] = jnp.where(allowed, 0.0, masked_score).astype(narrow)

    def inverse_rms(value):
        return lax.rsqrt(
            jnp.sum(value * value, axis=-1, keepdims=True) / MODEL_WIDTH + epsilon
        )

    def active_column(recursion):
        own = depth_at[384:512, :].astype(wide)[:, 0:1]
        return jnp.where(own > recursion.astype(wide), 1.0, 0.0)

    def mixing_gate(recursion):
        logits = jnp.sum(
            h_all[recursion] * gains[pl.ds(2 + recursion, 1), :], axis=-1, keepdims=True
        )
        return jax.nn.sigmoid(logits)

    def halves(tile, pair):
        low = lanes(tile.shape) < 64
        zero = jnp.zeros_like(tile)
        if pair == 2:
            return jnp.where(low, tile, zero)
        return jnp.concatenate([jnp.where(low, tile, zero), jnp.where(low, zero, tile)], axis=0)

    def set_keys(recursion, pair):
        for block in range(4):
            at = pl.ds(block * 128, 128)
            keys_at[at, 0:128] = window(recursion, block, pair)[:, 0:128]
            keys_at[at, 128:256] = bias_at[at, :]

    def value_tile(recursion, pair):
        at = 0 if pair == 2 else 128
        parts = [window(recursion, b, pair)[:, at : at + 128] for b in range(4)]
        return jnp.concatenate(parts, axis=0)

    def set_scores(recursion, pair, part, buffer):
        at = (pair * 3 + part) * 128
        queries = halves(q_all[recursion, :, at : at + 128], pair)
        width = queries.shape[0]
        same = jnp.where(row == column, 1.0, 0.0).astype(narrow)
        same = same if width == 128 else jnp.concatenate([same, same], axis=0)
        both = jnp.concatenate([queries, same], axis=1)
        s_at[buffer, :, 0:width] = dot_nt(keys_at[...], both)
        return queries, width

    def rows_of_eight(value, join):
        return join(value.reshape(value.shape[0] // 8, 8, value.shape[1]), axis=0)

    def joined(out, pair):
        if pair == 2:
            return jnp.where(row < 64, out, 0.0).T
        return jnp.where(row < 64, out[:, :128], out[:, 128:]).T

    def attend(recursion):
        pass_keys_on(recursion, 0)
        pass_keys_on(recursion, 1)
        for pair in range(3):
            wait_keys(recursion, pair)
            set_keys(recursion, pair)
            values_t = value_tile(recursion, pair).T
            for part in range(3):
                buffer = part % 2
                _, width = set_scores(recursion, pair, part, buffer)
                top = jnp.full((8, width), masked_score, wide)
                for sub in range(0, 512, SUB):
                    scores = s_at[buffer, sub : sub + SUB, 0:width]
                    top = jnp.maximum(top, rows_of_eight(scores, jnp.max))
                top = jnp.max(top, axis=0, keepdims=True)
                total = jnp.zeros((8, width), wide)
                for sub in range(0, 512, SUB):
                    weight = jnp.exp(s_at[buffer, sub : sub + SUB, 0:width] - top)
                    total = total + rows_of_eight(weight, jnp.sum)
                    p_at[sub : sub + SUB, part * 256 : part * 256 + width] = weight.astype(narrow)
                total = jnp.sum(total, axis=0, keepdims=True)
                stats[recursion, pair * 3 + part, 0:1, 0:width] = top + jnp.log(total)
                out = dot_nn(values_t, p_at[:, part * 256 : part * 256 + width]) / total
                if pair == 2:
                    head = (12 + part) * HEAD_SIZE
                    natural_at[head : head + 64, :] = out[64:, :]
                else:
                    head = (6 * pair + part) * HEAD_SIZE
                    natural_at[head : head + 64, :] = out[:64, :128]
                    head = (6 * pair + 3 + part) * HEAD_SIZE
                    natural_at[head : head + 64, :] = out[64:, 128:]
            if pair == 0:
                pass_keys_on(recursion, 2)

    def upstream_of(pair, part):
        zero = jnp.zeros((64, 128), narrow)

        def head(number):
            return natural_at[number * 64 : number * 64 + 64, :].astype(narrow)

        if pair == 2:
            return jnp.concatenate([zero, head(12 + part)], axis=0)
        low = jnp.concatenate([head(6 * pair + part), zero], axis=1)
        high = jnp.concatenate([zero, head(6 * pair + 3 + part)], axis=1)
        return jnp.concatenate([low, high], axis=0)

    def attend_back(recursion):
        for pair in range(3):
            set_keys(recursion, pair)
            values = value_tile(recursion, pair)
            keys_t = keys_at[:, 0:128].T
            width = 128 if pair == 2 else 256
            for part in range(3):
                buffer = part % 2
                queries, _ = set_scores(recursion, pair, part, buffer)
                upstream = upstream_of(pair, part)
                qs_at[part * width : part * width + width, :] = queries
                us_at[:, part * width : part * width + width] = upstream
                gp_at[buffer, :, 0:width] = dot_nn(values, upstream)
                log_total = stats[recursion, pair * 3 + part, 0:1, 0:width]
                inner = jnp.zeros((8, width), wide)
                where = slice(part * width, part * width + width)
                for sub in range(0, 512, SUB):
                    probs = jnp.exp(s_at[buffer, sub : sub + SUB, 0:width] - log_total)
                    s_at[buffer, sub : sub + SUB, 0:width] = probs
                    p_at[sub : sub + SUB, where] = probs.astype(narrow)
                    inner = inner + rows_of_eight(
                        probs * gp_at[buffer, sub : sub + SUB, 0:width], jnp.sum
                    )
                inner = jnp.sum(inner, axis=0, keepdims=True)
                for sub in range(0, 512, SUB):
                    rows = slice(sub, sub + SUB)
                    gs_at[rows, where] = (
                        s_at[buffer, rows, 0:width] * (gp_at[buffer, rows, 0:width] - inner)
                    ).astype(narrow)
            grad_keys = dot_nn(gs_at[:, 0 : 3 * width], qs_at[0 : 3 * width, :])
            grad_values = dot_nt(p_at[:, 0 : 3 * width], us_at[:, 0 : 3 * width])
            if pair == 2:
                dkv[:, 512:640] = grad_keys + grad_values
            else:
                dkv[:, pair * 256 : pair * 256 + 128] = grad_keys
                dkv[:, pair * 256 + 128 : pair * 256 + 256] = grad_values
            send_back(recursion, pair)
            out = dot_nn(keys_t, gs_at[:, 0 : 3 * width])
            for part in range(3):
                at = (pair * 3 + part) * 128
                gqkv_all[recursion, :, at : at + 128] = rotated(
                    joined(out[:, part * width : part * width + width], pair),
                    cos_at[...] * 0.125,
                    sin_at[...] * -0.125,
                ).astype(narrow)
            if pair > 0:
                pass_back_on(recursion, pair - 1)

    def rotate_keys(value, sine):
        cosine = cos_at[...]
        low = lanes((128, 128)) < 64
        parts = []
        for tile in range(5):
            part = value[:, tile * 128 : tile * 128 + 128]
            if tile in (0, 2):
                part = rotated(part, cosine, sine)
            elif tile == 4:
                part = jnp.where(low, rotated(part, cosine, sine), part)
            parts.append(part)
        return jnp.concatenate(parts, axis=1)

    @pl.loop(0, RECUR)
    def _(recursion):
        state = h_all[recursion]
        normal = state * inverse_rms(state)
        a_b = (normal * gains[0:1, :]).astype(narrow)
        a_all[recursion] = a_b

        @pl.when(recursion == 0)
        def _():
            loads[0].wait()

        pair_values = dot_nn(a_b, wa[:, KV_AT:O_AT])
        pair_values = rotate_keys(pair_values, sin_at[...]).astype(narrow)
        for pair in range(3):
            window(recursion, 3, pair)[...] = pair_values[:, pair_lanes(pair)]
            send_keys(recursion, pair)
        cosine, sine = cos_at[...] * 0.125, sin_at[...] * 0.125
        for first, width in ((0, 512), (512, 512), (1024, 128)):
            queries = dot_nn(a_all[recursion], wa[:, first : first + width])
            for at in range(0, width, 128):
                q_all[recursion, :, first + at : first + at + 128] = rotated(
                    queries[:, at : at + 128], cosine, sine
                ).astype(narrow)

        @pl.when(recursion == 0)
        def _():
            set_depths()

        set_bias(recursion)
        attend(recursion)

        @pl.when(recursion == 0)
        def _():
            start_moves(
                (cotangent,),
                (cotangent_at,),
                move_send.at[pl.ds(0, 1)],
                move_recv.at[pl.ds(0, 1)],
                target,
                moves,
            )

        add_pads()
        o_pad = padded_at[...].T.astype(narrow)
        o_all[recursion] = o_pad
        branch = dot_nn(o_pad, wa[:, O_AT:])
        middle = h_all[recursion] + branch
        z_all[recursion] = middle
        b_b = (middle * inverse_rms(middle) * gains[1:2, :]).astype(narrow)
        b_all[recursion] = b_b
        acc[...] = branch

        @pl.when(recursion == 0)
        def _():
            for load in loads[1:]:
                load.wait()

        for j in range(FEEDFORWARD_UNITS // CHUNK):
            at = slice(j * CHUNK, j * CHUNK + CHUNK)
            gate = dot_nn(b_all[recursion], wg[:, at])
            up = dot_nn(b_all[recursion], wu[:, at])
            gate_all[recursion, :, at] = gate
            up_all[recursion, :, at] = up
            hidden = (gate * jax.nn.sigmoid(gate) * up).astype(narrow)
            hidden_all[recursion, :, at] = hidden
            acc[...] += dot_nn(hidden, wd[at, :])

        for copy in factor_copies(recursion, (0, 1, 2, 3)):
            copy.start()
        tf_all[recursion] = acc[...]
        mixing = active_column(recursion) * mixing_gate(recursion)
        following = h_all[recursion] + mixing * acc[...]

        @pl.when(recursion < RECUR - 1)
        def _():
            h_all[recursion + 1] = following

        @pl.when(recursion == RECUR - 1)
        def _():
            padded_at[...] = following.astype(narrow).astype(wide).T
            drop_pads()
            leaving[...] = natural_at[...].astype(narrow)

    wait_moves((cotangent,), (cotangent_at,), move_send.at[pl.ds(0, 1)], move_recv.at[pl.ds(0, 1)], target, moves)
    natural_at[...] = cotangent_at[...].astype(wide)
    add_pads()
    grad[...] = padded_at[...].T

    @pl.loop(0, RECUR)
    def _(i):
        recursion = RECUR - 1 - i

        @pl.when(i == 1)
        def _():
            start_moves(
                (leaving,),
                (output,),
                move_send.at[pl.ds(1, 1)],
                move_recv.at[pl.ds(1, 1)],
                source,
                moves,
            )

        router_row = gains[pl.ds(2 + recursion, 1), :]
        active, gate_value = active_column(recursion), mixing_gate(recursion)
        upstream = grad[...]
        grad_mix = jnp.sum(upstream * tf_all[recursion], axis=-1, keepdims=True)
        grad_logit = active * grad_mix * gate_value * (1.0 - gate_value)
        small[pl.ds(2 + recursion, 1), :] = jnp.sum(
            grad_logit * h_all[recursion], axis=0, keepdims=True
        )
        delta = (active * gate_value) * upstream
        gf_all[recursion] = delta.astype(narrow)
        grad[...] = upstream + grad_logit * router_row
        tf_all[recursion] = delta
        acc[...] = jnp.zeros((128, 1024), wide)

        @pl.when(recursion < RECUR - 1)
        def _():
            for copy in stage_copies(recursion + 1):
                copy.wait()

        for j in range(FEEDFORWARD_UNITS // CHUNK):
            at = slice(j * CHUNK, j * CHUNK + CHUNK)
            grad_hidden = dot_nt(gf_all[recursion], wd[at, :])
            gate, up = gate_all[recursion, :, at], up_all[recursion, :, at]
            sigmoid = jax.nn.sigmoid(gate)
            grad_gate = (grad_hidden * up * sigmoid * (1.0 + gate * (1.0 - sigmoid))).astype(narrow)
            grad_up = (grad_hidden * gate * sigmoid).astype(narrow)
            gg_at[:, at] = grad_gate
            gu_at[:, at] = grad_up
            acc[...] += dot_nt(grad_gate, wg[:, at]) + dot_nt(grad_up, wu[:, at])

        for copy in stage_copies(recursion) + factor_copies(recursion, (4,)):
            copy.start()
        middle = z_all[recursion]
        inverse = inverse_rms(middle)
        normal = middle * inverse
        small[1:2, :] += jnp.sum(acc[...] * normal, axis=0, keepdims=True)
        scaled = acc[...] * gains[1:2, :]
        inner = jnp.sum(scaled * normal, axis=-1, keepdims=True) / MODEL_WIDTH
        grad_middle = inverse * (scaled - normal * inner)
        gt_b = (tf_all[recursion] + grad_middle).astype(narrow)
        gt_all[recursion] = gt_b
        for copy in factor_copies(recursion, (5,)):
            copy.start()
        grad[...] += grad_middle
        padded_at[...] = dot_nt(gt_b, wa[:, O_AT:]).T
        drop_pads()
        set_bias(recursion)

        @pl.when(recursion < RECUR - 1)
        def _():
            for pair in range(3):
                wait_back_sent(recursion + 1, pair)

        attend_back(recursion)
        acc[...] = dot_nt(gqkv_all[recursion, :, :KV_AT], wa[:, :KV_AT])

        pass_back_on(recursion, 2)
        for pair in range(3):
            take_back(recursion, pair)
        gqkv_all[recursion, :, KV_AT:] = rotate_keys(dkv[384:512, :], -sin_at[...]).astype(narrow)
        for copy in factor_copies(recursion, (6,)):
            copy.start()
        grad_normed = acc[...] + dot_nt(gqkv_all[recursion, :, KV_AT:], wa[:, KV_AT:O_AT])
        state = h_all[recursion]
        inverse = inverse_rms(state)
        normal = state * inverse
        small[0:1, :] += jnp.sum(grad_normed * normal, axis=0, keepdims=True)
        scaled = grad_normed * gains[0:1, :]
        inner = jnp.sum(scaled * normal, axis=-1, keepdims=True) / MODEL_WIDTH
        grad[...] += inverse * (scaled - normal * inner)

    for copy in stage_copies(0):
        copy.wait()
    for recursion in range(RECUR):
        for copy in factor_copies(recursion, range(7)):
            copy.wait()
    padded_at[...] = grad[...].T
    drop_pads()
    input_grad[...] = natural_at[...].astype(narrow)

    wait_moves((leaving,), (output,), move_send.at[pl.ds(1, 1)], move_recv.at[pl.ds(1, 1)], source, moves)
    for away in (1, 2, 3):
        when(span + away < 8, lambda: depth_copy(away, here).wait_send())
    for recursion in range(RECUR):
        for pair in range(3):
            wait_keys_sent(recursion, pair)
    for pair in range(3):
        wait_back_sent(0, pair)


def run_block(tokens, cotangent, meta, gains, weights):
    narrow, wide, vmem, sems = jnp.bfloat16, jnp.float32, pltpu.VMEM, pltpu.SemaphoreType.DMA
    half = HEAD_SIZE // 2
    lane = np.arange(128) % half
    frequency = 10000.0 ** (-lane / half)
    angle = np.arange(128)[:, None] * frequency[None, :]
    rope = np.stack([np.cos(angle), np.sin(angle)]).astype(np.float32)
    jump = np.arange(4)[:, None] * 128.0 * frequency[None, :]
    turn = np.zeros((16, 128), np.float32)
    turn[:4], turn[8:12] = np.cos(jump), np.sin(jump)
    outs = [((MODEL_WIDTH, 128), narrow), ((MODEL_WIDTH, 128), narrow), ((8, 1024), wide)]
    outs += [
        ((RECUR, 128, width), narrow)
        for width in (1024, O_AT, 1024, 1024, 1024, 2560, 2560, 2560, 1024)
    ]
    scratch = [
        vmem((1024, 2816), narrow),
        vmem((1024, 2560), narrow),
        vmem((1024, 2560), narrow),
        vmem((2560, 1024), narrow),
        vmem((8, 1024), wide),
        vmem((MODEL_WIDTH, 128), wide),
        vmem((1024, 128), wide),
        vmem((MODEL_WIDTH, 128), narrow),
        vmem((MODEL_WIDTH, 128), narrow),
        vmem((RECUR, 128, 1024), wide),
        vmem((RECUR, 128, 1024), wide),
        vmem((RECUR, 128, 1024), wide),
        vmem((RECUR, 128, 2560), wide),
        vmem((RECUR, 128, 2560), wide),
        vmem((RECUR, 128, KV_AT), narrow),
        vmem((RECUR, 4, 2, 128, 256), narrow),
        vmem((RECUR, 4, 128, 128), narrow),
        vmem((RECUR, 3, 2, 128, 256), narrow),
        vmem((RECUR, 3, 128, 128), narrow),
        vmem((3, 2, 128, 256), narrow),
        vmem((3, 128, 128), narrow),
        vmem((4, 8, 128), wide),
        vmem((512, 128), narrow),
        vmem((512, 128), narrow),
        vmem((128, 128), wide),
        vmem((128, 128), wide),
        vmem((RECUR, Q_TILES, 2, 256), wide),
        vmem((512, KV_WIDTH), wide),
        vmem((128, 1024), wide),
        vmem((128, 1024), wide),
        vmem((128, 2560), narrow),
        vmem((128, 2560), narrow),
        vmem((512, 256), narrow),
        vmem((2, 512, 256), wide),
        vmem((2, 512, 256), wide),
        vmem((512, 768), narrow),
        vmem((512, 768), narrow),
        vmem((768, 128), narrow),
        vmem((128, 768), narrow),
        sems((2,)),
        sems((2,)),
        *[vmem((RECUR, 128, width), narrow) for width in (1024, O_AT, 1024, 1024, 1024, 2560, 1024)],
        sems((7, RECUR)),
        sems((4,)),
        sems((2,)),
        sems((RECUR, 3, 3)),
        sems((RECUR, 3, 3)),
        sems((RECUR, 3, 3)),
        sems((RECUR, 3, 3)),
        sems((3,)),
        sems((3,)),
    ]
    here, anywhere = pl.BlockSpec(memory_space=vmem), pl.BlockSpec(memory_space=pl.ANY)
    return pl.pallas_call(
        block_kernel,
        out_shape=[jax.ShapeDtypeStruct(shape, dtype) for shape, dtype in outs],
        in_specs=[here, anywhere] + [here] * 6 + [anywhere] * 4,
        out_specs=[here] * 3 + [anywhere] * 9,
        scratch_shapes=scratch,
        compiler_params=pltpu.CompilerParams(
            collective_id=3, has_side_effects=True, vmem_limit_bytes=60 * 2**20
        ),
        name="run_block",
    )(tokens, cotangent, meta, rope, turn, *gains, *weights)


HEAD_TILES = tuple(
    (6 * (tile // 3) + tile % 3, 6 * (tile // 3) + 3 + tile % 3) if tile < 6 else (6 + tile, -1)
    for tile in range(9)
)
NATURAL_TILES = tuple((2 * tile, 2 * tile + 1 if tile < 7 else -1) for tile in range(8))


def fill_spread(spread, places):
    @pl.loop(0, MODEL_WIDTH // 64)
    def _(i):
        at = pl.multiple_of(i * 64, 64)
        rows = lax.broadcasted_iota(jnp.int32, (64, 1024), 0) + at
        spread[pl.ds(at, 64), :] = jnp.where(rows == places[0:1, :], 1.0, 0.0).astype(jnp.bfloat16)


def chunk_rows(flat, units, pairs, parity, unit):
    where = units * parity + unit
    return flat[pl.ds(where // 2, pairs, stride=units), :], where % 2


def placed_half(found, low):
    value, half = found
    return value if half == (0 if low else 1) else pltpu.roll(value, 64, 1)


def pack_tiles(flat, out, first, tiles, units, pairs):
    low = lax.broadcasted_iota(jnp.int32, (pairs, 128), 1) < 64
    zero = jnp.zeros((pairs, 128), jnp.float32)
    for parity in (0, 1):
        for tile, (left, right) in enumerate(tiles):
            one = placed_half(chunk_rows(flat, units, pairs, parity, left), True) if left >= 0 else zero
            two = (
                placed_half(chunk_rows(flat, units, pairs, parity, right), False)
                if right >= 0
                else zero
            )
            out[first + tile, pl.ds(parity, pairs, stride=2), :] = jnp.where(low, one, two)


def pack_wide(flat, own, tiles):
    for source, out in zip(flat[4:6], own[1:3]):
        for tile in range(20):
            tiles[tile, 0:OWN_ROWS] = source[pl.ds(tile, OWN_ROWS, stride=20), :]
            tiles[tile, OWN_ROWS:] = jnp.zeros((PADDED_ROWS - OWN_ROWS, 128), jnp.float32)
            out[:, tile * 128 : tile * 128 + 128] = tiles[tile].astype(jnp.bfloat16)


def pack_rest(flat, own, spread, tiles, natural, long_rows):
    w_query, w_key, w_value, w_out = flat[:4]
    attention, down = own[0], own[3]
    narrow = jnp.bfloat16
    tiles[...] = jnp.zeros(tiles.shape, jnp.float32)
    natural[...] = jnp.zeros(natural.shape, jnp.float32)
    pack_tiles(w_query, tiles, 0, HEAD_TILES, 15, 15)
    for tile, heads in ((9, (0, 1)), (11, (2, 3)), (13, (4, -1))):
        pack_tiles(w_key, tiles, tile, (heads,), 5, 15)
    for tile, heads in ((10, (0, 1)), (12, (2, 3)), (14, (-1, 4))):
        pack_tiles(w_value, tiles, tile, (heads,), 5, 15)
    low = lax.broadcasted_iota(jnp.int32, (32, 128), 1) < 64
    tiles[13] = jnp.where(low, tiles[13], tiles[14])
    for tile in range(14):
        attention[:, tile * 128 : tile * 128 + 128] = tiles[tile].astype(narrow)
    pack_tiles(w_out, natural, 0, NATURAL_TILES, 15, 15)
    pack_tiles(flat[6], long_rows, 0, NATURAL_TILES, 15, 40)
    both = jnp.concatenate([side_by_side(natural), side_by_side(long_rows)], axis=0)
    both = dot_nn(both.astype(narrow), spread[...]).astype(narrow)
    attention[:, 1792:], down[...] = both[0:32], both[32:112]


def side_by_side(tiles):
    return jnp.concatenate([tiles[tile] for tile in range(8)], axis=1)[:, 0:MODEL_WIDTH]


def natural_places():
    padded = np.arange(1024)
    natural = padded // PADDED_ROWS * OWN_ROWS + padded % PADDED_ROWS
    natural = np.where(padded % PADDED_ROWS < OWN_ROWS, natural, -1)
    return np.broadcast_to(natural[None], (8, 1024)).astype(np.int32)


def unpack_tiles(packed, first, tiles, units, pairs, out):
    spots = {}
    for tile, heads in enumerate(tiles):
        for half, unit in enumerate(heads):
            if unit >= 0:
                spots[unit] = (tile, half)
    low = lax.broadcasted_iota(jnp.int32, (pairs, 128), 1) < 64

    def unit_at(where, is_low):
        parity, unit = where // units, where % units
        tile, half = spots[unit]
        value = packed[first + tile, pl.ds(parity, pairs, stride=2), :]
        return placed_half((value, half), is_low)

    for chunk in range(units):
        out[pl.ds(chunk, pairs, stride=units), :] = jnp.where(
            low, unit_at(2 * chunk, True), unit_at(2 * chunk + 1, False)
        )


def exact_gathered(value, spread):
    first = value.astype(jnp.bfloat16)
    rest = value - first.astype(jnp.float32)
    second = rest.astype(jnp.bfloat16)
    third = (rest - second.astype(jnp.float32)).astype(jnp.bfloat16)
    summed = dot_nt(jnp.concatenate([first, second, third], axis=0), spread[...])
    rows = value.shape[0]
    return summed[0:rows] + summed[rows : 2 * rows] + summed[2 * rows :]


def split_tiles(value, tiles):
    for tile in range(7):
        tiles[tile] = value[:, tile * 128 : tile * 128 + 128]
    tiles[7, :, 0:64] = value[:, 896:960]


def unpack_kernel(*refs):
    inside, places = refs[:7], refs[7]
    d_query, d_key, d_value, d_out, d_gate, d_up, d_down = refs[8:15]
    d_attn, d_ffn, d_router, output, input_grad = refs[15:20]
    held, (spread, tiles, natural, long_rows, sems) = refs[20:27], refs[27:]
    copies = [
        pltpu.make_async_copy(src, dst, sems.at[i])
        for i, (src, dst) in enumerate(zip(inside, held))
    ]
    for copy in copies:
        copy.start()
    fill_spread(spread, places)
    for copy in copies:
        copy.wait()
    attention, gate, up, down, small, moved_grad, moved_output = held
    output[...] = moved_output[...]
    input_grad[...] = moved_grad[...].astype(jnp.float32)
    for tile in range(14):
        tiles[tile] = attention[:, tile * 128 : tile * 128 + 128]
    unpack_tiles(tiles, 0, HEAD_TILES, 15, 15, d_query)
    none = (-1, -1)
    unpack_tiles(tiles, 9, ((0, 1), none, (2, 3), none, (4, -1)), 5, 15, d_key)
    unpack_tiles(tiles, 9, (none, (0, 1), none, (2, 3), (-1, 4)), 5, 15, d_value)
    for packed, out in ((gate, d_gate), (up, d_up)):
        for tile in range(20):
            out[pl.ds(tile, OWN_ROWS, stride=20), :] = packed[
                0:OWN_ROWS, tile * 128 : tile * 128 + 128
            ]
    gathered = exact_gathered(
        jnp.concatenate([attention[:, 1792:], down[...], small[...]], axis=0), spread
    )
    split_tiles(gathered[0:32], natural)
    unpack_tiles(natural, 0, NATURAL_TILES, 15, 15, d_out)
    split_tiles(gathered[32:112], long_rows)
    unpack_tiles(long_rows, 0, NATURAL_TILES, 15, 40, d_down)
    d_attn[...], d_ffn[...], d_router[...] = gathered[112:113], gathered[113:114], gathered[114:117]


def unpack_gradients(sums, small, input_grad, output):
    narrow, wide, vmem = jnp.bfloat16, jnp.float32, pltpu.VMEM
    here, anywhere = pl.BlockSpec(memory_space=vmem), pl.BlockSpec(memory_space=pl.ANY)
    flat = (225, 75, 75, 225, 600, 600, 600)
    inside = (*sums, small, input_grad, output)
    return pl.pallas_call(
        unpack_kernel,
        out_shape=[jax.ShapeDtypeStruct((rows, 128), wide) for rows in flat]
        + [
            jax.ShapeDtypeStruct((1, MODEL_WIDTH), wide),
            jax.ShapeDtypeStruct((1, MODEL_WIDTH), wide),
            jax.ShapeDtypeStruct((RECUR, MODEL_WIDTH), wide),
            jax.ShapeDtypeStruct((MODEL_WIDTH, 128), narrow),
            jax.ShapeDtypeStruct((MODEL_WIDTH, 128), wide),
        ],
        in_specs=[anywhere] * 7 + [here],
        out_specs=[here] * 12,
        scratch_shapes=[vmem(x.shape, x.dtype) for x in inside]
        + [
            vmem((MODEL_WIDTH, 1024), narrow),
            vmem((14, 32, 128), wide),
            vmem((8, 32, 128), wide),
            vmem((8, 80, 128), wide),
            pltpu.SemaphoreType.DMA((7,)),
        ],
        compiler_params=pltpu.CompilerParams(vmem_limit_bytes=59 * 2**20),
        name="unpack_gradients",
    )(*inside, natural_places())


def per_device_fast(
    tokens,
    depths,
    seq_spans,
    cotangent,
    w_query,
    key_weight,
    value_weight,
    w_out,
    w_gate,
    w_up,
    w_down,
    attn_gain,
    ffn_gain,
    router,
):
    *weights, own_tokens, own_meta = gather_weights(
        (w_query, key_weight, value_weight, w_out, w_gate, w_up, w_down),
        tokens[0].T,
        depths,
        seq_spans,
    )
    output, input_grad, small, *factors = run_block(
        own_tokens, cotangent[0].T, own_meta, (attn_gain[None], ffn_gain[None], router), weights
    )
    *sums, small_sum, input_grad = reduce_gradients(
        [x.reshape(RECUR * 128, -1) for x in factors], small, (input_grad,)
    )
    *gradients, d_attn, d_ffn, d_router, output, input_grad = unpack_gradients(
        sums, small_sum, input_grad, output
    )
    return (
        output.T[None],
        input_grad.T[None],
        *[x.reshape(-1) for x in gradients],
        d_attn[0],
        d_ffn[0],
        d_router,
    )


def solution(mesh):
    fits = mesh.shape["seq"] == 8 and mesh.shape["rep"] == 4
    placed = (
        P("rep", "seq", None),
        P("rep", "seq"),
        P("rep", None),
        P("rep", "seq", None),
        P(("seq", "rep")),
        P(("seq", "rep")),
        P(("seq", "rep")),
        P(("seq", "rep")),
        P(("seq", "rep")),
        P(("seq", "rep")),
        P(("seq", "rep")),
        P(),
        P(),
        P(),
    )
    return jax.shard_map(
        per_device_fast if fits else per_device,
        mesh=mesh,
        in_specs=placed,
        out_specs=(
            P("rep", "seq", None),
            P("rep", "seq", None),
            P(("seq", "rep")),
            P(("seq", "rep")),
            P(("seq", "rep")),
            P(("seq", "rep")),
            P(("seq", "rep")),
            P(("seq", "rep")),
            P(("seq", "rep")),
            P(),
            P(),
            P(),
        ),
        check_vma=False,
    )
```
